32 devices in a mesh: section: 4 (over y, x), rows: 2 (over core), dp: 4 (over z).
Axes of the slice: x: 2, y: 2, z: 4, core: 2. Of those that a mesh axis runs over, the one named last changes fastest.
Arguments:
- images: bfloat16 [8, 48, 16, 384], P('dp', 'rows'), may hold values from -6 to 6
- cotangent: bfloat16 [8, 48, 16, 384], P('dp', 'rows'), may hold values from -6 to 6
- order: int32 [4, 2], P('dp'), may hold values from 0 to 1, each once within a row
- heights: int32 [8], P('dp'), may hold values from 12 to 48, as said below
- kernel: float32 [4, 49, 384], P('section'), may hold values from -0.875 to 0.875
- biases: float32 [4, 3, 384], P('section'), may hold values from -3 to 3
- gain: float32 [4, 384], P('section'), may hold values from 0.25 to 1.75
- scale: float32 [4, 384], P('section'), may hold values from 0.4 to 1.2
- up_weight: bfloat16 [4, 384, 1536], P('section'), may hold values from -0.3125 to 0.3125
- up_bias: float32 [4, 1536], P('section'), may hold values from -3 to 3
- down_weight: bfloat16 [4, 1536, 384], P('section'), may hold values from -0.15625 to 0.15625
Outputs:
- kernel_grad: bfloat16 [4, 49, 384], P('section')
- bias_grad: bfloat16 [4, 3, 384], P('section')
- gain_grad: bfloat16 [4, 384], P('section')
- scale_grad: bfloat16 [4, 384], P('section')
- up_weight_grad: bfloat16 [4, 384, 1536], P('section')
- up_bias_grad: bfloat16 [4, 1536], P('section')
- down_weight_grad: bfloat16 [4, 1536, 384], P('section')
The draws below stay inside these ranges and needn't reach their ends.
Inputs may be any that keep to these rules, and one draw needn't show every extreme that they name: `order`: each row holds every number of 0 to 1 once. `heights`: some image has all 48 rows and some image has 12 rows.
All inputs are finite; a program needn't handle non-finite values.
Results may differ from the reference program's by a relative error of at most 0.015.
Values may be sent and summed in bfloat16 or wider, within the bound.
No kernel may reach another device: no remote copies, remote signals or barrier semaphores. Data moves between devices by JAX's collectives and lax.ppermute only.
A program may use at most 128 MiB of HBM per device.

```python
import math
import jax
import jax.numpy as jnp
from jax import lax

C = 384
HID = 1536
COLS = 16
MB = 2
SECTIONS = 4
GROUPS = 4
H = 48
IMAGES = 8


def draw_heights(key, part):
    base = jax.random.randint(key, (IMAGES,), H // 4, H + 1)
    first = jax.random.randint(jax.random.fold_in(key, 11), (), 0, IMAGES)
    step_on = jax.random.randint(jax.random.fold_in(key, 12), (), 1, IMAGES)
    second = (first + step_on) % IMAGES
    places = jnp.arange(IMAGES)
    base = jnp.where(places == first, H, base)
    return jnp.where(places == second, H // 4, base).astype(jnp.int32)


def level_of(key, dims, cuts, smallest, top_value):
    factor_of = 1.0
    for axis_at, parts in cuts:
        steps = jax.random.uniform(jax.random.fold_in(jax.random.fold_in(key, 6), axis_at), (parts,), jnp.float32, smallest / len(cuts), top_value / len(cuts))
        factor_of = factor_of * jnp.repeat(jnp.exp(steps), dims[axis_at] // parts).reshape((-1,) + (1,) * (len(dims) - 1 - axis_at))
    return factor_of


def gaussian(stream_key, shape, width, most, split=(), held_as=jnp.bfloat16):
    values = jax.random.normal(stream_key, shape, jnp.float32) * width
    if len(split) > 0:
        values = level_of(stream_key, shape, split, -0.22, 0.18) * values
    return jnp.clip(values, min=-most, max=most).astype(held_as)


def setup_inputs(seed: int = 0) -> dict:
    key_list = jax.random.split(jax.random.key(seed), 12)
    return {
        "images": gaussian(key_list[0], (IMAGES, H, COLS, C), 1.0, 6.0, ((0, 4), (1, 2))),
        "cotangent": gaussian(key_list[1], (IMAGES, H, COLS, C), 1.0, 6.0, ((0, 4), (1, 2))),
        "order": jax.vmap(lambda own: jax.random.permutation(own, MB))(jax.random.split(key_list[2], GROUPS)).reshape((GROUPS, MB)).astype(jnp.int32),
        "heights": draw_heights(jax.random.fold_in(key_list[11], 71), 0),
        "kernel": gaussian(key_list[4], (SECTIONS, 49, C), 49 ** -0.5, 0.875, ((0, 4),), jnp.float32),
        "biases": gaussian(key_list[5], (SECTIONS, 3, C), 0.5, 3.0, ((0, 4),), jnp.float32),
        "gain": jnp.clip(1.0 + 0.15 * jax.random.normal(key_list[6], (SECTIONS, C), jnp.float32), 0.25, 1.75),
        "scale": jnp.clip(jnp.exp(math.log(1.2) - 1.0986123 * jax.random.uniform(key_list[7], (SECTIONS, C), jnp.float32) ** level_of(key_list[7], (SECTIONS, C), ((0, 4),), -0.2, 0.2)), 0.4, 1.2),
        "up_weight": gaussian(key_list[8], (SECTIONS, C, HID), C ** -0.5, 0.3125, ((0, 4),)),
        "up_bias": gaussian(key_list[9], (SECTIONS, HID), 0.5, 3.0, ((0, 4),), jnp.float32),
        "down_weight": gaussian(key_list[10], (SECTIONS, HID, C), HID ** -0.5, 0.15625, ((0, 4),)),
    }


EPS = 1e-06
ROOT_HALF = 0.7071067811865476
INV_ROOT_TAU = 0.3989422804014327

def gelu_exact(values):
    return 0.5 * values * (1.0 + lax.erf(values * ROOT_HALF))

def gelu_slope(values):
    return 0.5 * (1.0 + lax.erf(values * ROOT_HALF)) + values * jnp.exp(-0.5 * values * values) * INV_ROOT_TAU

def widen_cols(padded):
    return jnp.pad(padded.astype(jnp.float32), ((0, 0), (3, 3), (0, 0)))

def block_forward(padded, row_mask, params):
    kern, biases, gain, scale, up_weight, up_bias, down_weight = params
    row_count = padded.shape[0] - 6
    col_count = padded.shape[1]
    channels = padded.shape[2]
    field = widen_cols(padded)
    inner = field[3:-3, 3:-3]
    conv = jnp.zeros((row_count, col_count, channels), jnp.float32)
    for i in range(7):
        for j in range(7):
            conv = conv + kern[i * 7 + j] * field[i:i + row_count, j:j + col_count]
    conv = conv + biases[0]
    centred = conv - lax.optimization_barrier(jnp.mean(conv, axis=-1, keepdims=True))
    inv_std = lax.rsqrt(lax.optimization_barrier(jnp.mean(centred * centred, axis=-1, keepdims=True)) + EPS)
    normed = centred * inv_std
    features = (normed * gain + biases[1]).astype(jnp.bfloat16).reshape(-1, channels)
    hidden_pre = jnp.dot(features, up_weight, preferred_element_type=jnp.float32) + up_bias
    hidden = gelu_exact(hidden_pre).astype(jnp.bfloat16)
    branch = (jnp.dot(hidden, down_weight, preferred_element_type=jnp.float32) + biases[2]).reshape(row_count, col_count, channels)
    output = (row_mask * (inner + scale * branch)).astype(jnp.bfloat16)
    return (output, (padded, normed, inv_std, features, hidden_pre, branch))

def block_backward_first(grad_out, saved, row_mask, params):
    padded, normed, inv_std, features, hidden_pre, branch = saved
    kern, biases, gain, scale, up_weight, up_bias, down_weight = params
    channels = normed.shape[2]
    grad_res = row_mask * grad_out.astype(jnp.float32)
    scaled = scale * grad_res
    grad_scale = lax.optimization_barrier(jnp.sum(branch * grad_res, axis=(0, 1)))
    grad_bias_out = lax.optimization_barrier(jnp.sum(scaled, axis=(0, 1)))
    grad_branch = scaled.astype(jnp.bfloat16).reshape(-1, channels)
    hidden = gelu_exact(hidden_pre).astype(jnp.bfloat16)
    grad_down = lax.dot_general(hidden, grad_branch, (((0,), (0,)), ((), ())), preferred_element_type=jnp.float32)
    grad_hidden = lax.dot_general(grad_branch, down_weight, (((1,), (1,)), ((), ())), preferred_element_type=jnp.float32)
    grad_pre = grad_hidden * gelu_slope(hidden_pre)
    grad_up_bias = lax.optimization_barrier(jnp.sum(grad_pre, axis=0))
    grad_pre_low = grad_pre.astype(jnp.bfloat16)
    grad_up = lax.dot_general(features, grad_pre_low, (((0,), (0,)), ((), ())), preferred_element_type=jnp.float32)
    grad_feat = lax.dot_general(grad_pre_low, up_weight, (((1,), (1,)), ((), ())), preferred_element_type=jnp.float32).reshape(normed.shape)
    grad_gain = lax.optimization_barrier(jnp.sum(grad_feat * normed, axis=(0, 1)))
    grad_norm_bias = lax.optimization_barrier(jnp.sum(grad_feat, axis=(0, 1)))
    grad_normed = grad_feat * gain
    grad_conv = inv_std * (grad_normed - lax.optimization_barrier(jnp.mean(grad_normed, axis=-1, keepdims=True)) - normed * lax.optimization_barrier(jnp.mean(grad_normed * normed, axis=-1, keepdims=True)))
    grad_conv_bias = lax.optimization_barrier(jnp.sum(grad_conv, axis=(0, 1)))
    small = (jnp.stack([grad_conv_bias, grad_norm_bias, grad_bias_out]), grad_gain[None], grad_scale[None], grad_up, grad_up_bias[None], grad_down)
    return (grad_res, grad_conv, small)

def block_backward_second(grad_res, grad_conv, conv_padded, padded, row_mask, kern):
    row_count = grad_conv.shape[0]
    col_count = grad_conv.shape[1]
    field = widen_cols(padded)
    spread = widen_cols(conv_padded)
    taps = []
    total = jnp.zeros(grad_conv.shape, jnp.float32)
    for i in range(7):
        for j in range(7):
            taps.append(lax.optimization_barrier(jnp.sum(field[i:i + row_count, j:j + col_count] * grad_conv, axis=(0, 1))))
            total = total + kern[i * 7 + j] * spread[6 - i:6 - i + row_count, 6 - j:6 - j + col_count]
    grad_in = (row_mask * (grad_res + total)).astype(jnp.bfloat16)
    return (grad_in, jnp.stack(taps))

def reference(images, cotangent, order, heights, kernel, biases, gain, scale, up_weight, up_bias, down_weight):
    image_ids = (jnp.arange(GROUPS, dtype=jnp.int32)[:, None] * MB + order).reshape(-1).astype(jnp.int32)
    lines = jnp.arange(H, dtype=jnp.int32)
    halo_pad = ((3, 3), (0, 0), (0, 0))

    def section_params(section):
        return (kernel[section], biases[section], gain[section], scale[section], up_weight[section], up_bias[section], down_weight[section])

    def one_slot(totals, slot):
        image_at = image_ids[slot]
        row_mask = (lines < heights[image_at]).astype(jnp.float32)[:, None, None]
        current = jnp.where(row_mask > 0, images[image_at], jnp.zeros((), jnp.bfloat16))
        saved_all = []
        for section in range(SECTIONS):
            current, saved = block_forward(jnp.pad(current, halo_pad), row_mask, section_params(section))
            saved_all.append(saved)
        grad_out = cotangent[slot]
        terms = [None] * SECTIONS
        for section in reversed(range(SECTIONS)):
            params = section_params(section)
            grad_res, grad_conv, small = block_backward_first(grad_out, saved_all[section], row_mask, params)
            grad_out, taps = block_backward_second(grad_res, grad_conv, jnp.pad(grad_conv, halo_pad), saved_all[section][0], row_mask, params[0])
            terms[section] = (taps,) + small
        stacked = tuple((jnp.stack([terms[s][p] for s in range(SECTIONS)]) for p in range(7)))
        return (tuple((a + b for a, b in zip(totals, stacked))), None)
    start = (jnp.zeros((SECTIONS, 49, C), jnp.float32), jnp.zeros((SECTIONS, 3, C), jnp.float32), jnp.zeros((SECTIONS, 1, C), jnp.float32), jnp.zeros((SECTIONS, 1, C), jnp.float32), jnp.zeros((SECTIONS, C, HID), jnp.float32), jnp.zeros((SECTIONS, 1, HID), jnp.float32), jnp.zeros((SECTIONS, HID, C), jnp.float32))
    totals = lax.scan(one_slot, start, jnp.arange(IMAGES, dtype=jnp.int32))[0]
    factor = 1.0 / math.sqrt(IMAGES * H * COLS)
    finished = tuple(((t * factor).astype(jnp.bfloat16) for t in totals))
    return (finished[0], finished[1], finished[2][:, 0], finished[3][:, 0], finished[4], finished[5][:, 0], finished[6])
```

```python
import functools
import math

import jax
import jax.numpy as jnp
from jax import lax
from jax.experimental import pallas as pl
from jax.experimental.pallas import tpu as pltpu
from jax.sharding import PartitionSpec as P

EPS = 1e-06
ROOT_HALF = 0.7071067811865476
INV_ROOT_TAU = 0.3989422804014327
BF = jnp.bfloat16
F32 = jnp.float32
LEFT = 8
WIDE = 16
LANES = 128
VMEM_LIMIT = 56 * 1024 * 1024

IMAGE, HEIGHT, WRITE, READ, ACTIVE, FIRST, LAST, ODD = range(8)


def params(grid_rank=1):
    return pltpu.CompilerParams(
        dimension_semantics=("arbitrary",) * grid_rank, vmem_limit_bytes=VMEM_LIMIT
    )


def whole(shape):
    return pl.BlockSpec(shape, lambda *_: (0,) * len(shape))


def picked(shape, tick, column):
    return pl.BlockSpec(
        (1,) + shape, lambda i, tab: (tab[tick, column],) + (0,) * len(shape)
    )


def group_of(rows):
    return next(g for g in (6, 4, 3, 2, 1) if rows % g == 0)


def masked_rows(value, first, limit):
    row = lax.broadcasted_iota(jnp.int32, value.shape, 0) + first
    return jnp.where(row < limit, value, 0.0)


def fill_sides(field):
    rows, wide, channels = field.shape
    cols = wide - WIDE
    field[:, 0:LEFT, :] = jnp.zeros((rows, LEFT, channels), F32)
    field[:, LEFT + cols :, :] = jnp.zeros((rows, WIDE - LEFT, channels), F32)


def fill_field(field, middle, pair, cross, odd, limit):
    rows = middle.shape[0]
    cols = middle.shape[1]
    span = slice(LEFT, LEFT + cols)
    field[3 : 3 + rows, span, :] = masked_rows(middle.astype(F32), 0, limit)
    none = jnp.zeros(pair.shape, F32)
    near = pair.astype(F32)
    far = none if cross is None else cross.astype(F32)

    @pl.when(odd == 1)
    def _():
        field[0:3, span, :] = masked_rows(near, -3, limit)
        field[rows + 3 :, span, :] = masked_rows(far, rows, limit)

    @pl.when(odd == 0)
    def _():
        field[0:3, span, :] = masked_rows(far, -3, limit)
        field[rows + 3 :, span, :] = masked_rows(near, rows, limit)


def depthwise(field, kern, out, bias, flip):
    rows, cols, channels = out.shape
    group = group_of(rows)
    for at in range(0, channels, LANES):
        lanes = slice(at, at + LANES)

        def step(g, _, lanes=lanes):
            acc = jnp.zeros((group, cols, LANES), F32)
            for j in range(7):
                part = field[pl.ds(g * group, group + 6), LEFT - 3 + j : LEFT - 3 + j + cols, lanes]
                for i in range(7):
                    tap = 48 - (i * 7 + j) if flip else i * 7 + j
                    acc = acc + kern[tap : tap + 1, lanes][None] * part[i : i + group]
            if bias is not None:
                acc = acc + bias[:, lanes][None]
            out[pl.ds(g * group, group), :, lanes] = acc
            return 0

        lax.fori_loop(0, rows // group, step, 0)


def pick_edge(odd, value, near, far):
    rows = value.shape[0]

    @pl.when(odd == 1)
    def _():
        near[...] = value[0:3]
        if far is not None:
            far[...] = value[rows - 3 :]

    @pl.when(odd == 0)
    def _():
        near[...] = value[rows - 3 :]
        if far is not None:
            far[...] = value[0:3]


def forward_kernel(tick, sources, multi, sends, chunk, n_keep, *refs):
    refs = list(refs)
    tab = refs.pop(0)
    feeds = []
    for _ in range(sources[0] + sources[1]):
        feeds.append([refs.pop(0), refs.pop(0), refs.pop(0) if multi else None])
    kern, vec, up, up_bias, down = (refs.pop(0) for _ in range(5))
    if n_keep:
        del refs[:n_keep]
    outgoing = refs.pop(0) if sends else None
    near = refs.pop(0) if sends else None
    far = refs.pop(0) if sends and multi else None
    o_pad, o_z, o_rs, o_n, o_h, o_slope, o_branch, field = refs
    _, rows, cols, channels = o_z.shape
    count = rows * cols
    hidden = up.shape[1]
    limit = tab[tick, HEIGHT]
    odd = tab[tick, ODD]
    fill_sides(field)
    if sources[0]:
        img, img_near, img_far = feeds.pop(0)

        def from_images():
            fill_field(
                field, img[0], img_near[0], None if img_far is None else img_far[0], odd, limit
            )

        if sources[1]:
            pl.when(tab[tick, FIRST] == 1)(from_images)
        else:
            from_images()
    if sources[1]:
        mid, mid_near, mid_far = feeds.pop(0)

        def from_block():
            fill_field(
                field, mid[...], mid_near[...], None if mid_far is None else mid_far[...], odd, limit
            )

        if sources[0]:
            pl.when(tab[tick, FIRST] == 0)(from_block)
        else:
            from_block()
    o_pad[0] = field[:, LEFT : LEFT + cols, :].astype(BF)
    depthwise(field, kern, o_z.at[0], vec[0:1], False)
    conv = o_z[0].reshape(count, channels)
    centred = conv - jnp.mean(conv, axis=-1, keepdims=True)
    inv_std = lax.rsqrt(jnp.mean(centred * centred, axis=-1, keepdims=True) + EPS)
    normed = centred * inv_std
    o_z[0] = normed.reshape(rows, cols, channels)
    o_rs[0] = jnp.broadcast_to(inv_std, (count, LANES))
    features = (normed * vec[3:4] + vec[1:2]).astype(BF)
    o_n[0] = features
    acc = jnp.zeros((count, channels), F32)
    for at in range(0, hidden, chunk):
        span = slice(at, at + chunk)
        pre = jnp.dot(features, up[:, span], preferred_element_type=F32) + up_bias[:, span]
        bell = 1.0 + lax.erf(pre * ROOT_HALF)
        act = (0.5 * pre * bell).astype(BF)
        o_h[0, :, span] = act
        o_slope[0, :, span] = (
            0.5 * bell + pre * jnp.exp(-0.5 * pre * pre) * INV_ROOT_TAU
        ).astype(BF)
        acc = acc + jnp.dot(act, down[span, :], preferred_element_type=F32)
    branch = acc + vec[2:3]
    o_branch[0] = branch
    if sends:
        inner = field[3 : 3 + rows, LEFT : LEFT + cols, :]
        value = inner + (vec[4:5] * branch).reshape(rows, cols, channels)
        outgoing[...] = masked_rows(value, 0, limit).astype(BF)
        pick_edge(odd, outgoing, near, far)


def chain_kernel(tick, sources, multi, edges, chunk, n_keep, *refs):
    refs = list(refs)
    tab = refs.pop(0)
    cot = refs.pop(0) if sources[0] else None
    incoming = refs.pop(0) if sources[1] else None
    z, rs, slope, branch, vec, up, down = (refs.pop(0) for _ in range(7))
    keeps = [refs.pop(0) for _ in range(n_keep)]
    o_go, o_gl, o_sums, o_up_bias, o_conv = (refs.pop(0) for _ in range(5))
    o_res = refs.pop(0) if edges else None
    o_low = refs.pop(0) if edges else None
    near = refs.pop(0) if edges else None
    far = refs.pop(0) if edges and multi else None
    rows, cols, channels = o_conv.shape
    count = rows * cols
    hidden = up.shape[1]
    limit = tab[tick, HEIGHT]
    active = tab[tick, ACTIVE].astype(F32)
    if sources[0] and sources[1]:
        grad = jnp.where(tab[tick, LAST] == 1, cot[0].astype(F32), incoming[...].astype(F32))
    elif sources[0]:
        grad = cot[0].astype(F32)
    else:
        grad = incoming[...].astype(F32)
    grad_res = masked_rows(grad, 0, limit)
    if edges:
        o_res[...] = grad_res.astype(BF)
    flat = grad_res.reshape(count, channels)
    scaled = vec[4:5] * flat
    sum_scale = jnp.sum(branch[0] * flat, axis=0, keepdims=True)
    sum_out = jnp.sum(scaled, axis=0, keepdims=True)
    go = scaled.astype(BF)
    o_go[0] = go
    feat = jnp.zeros((count, channels), F32)
    last_dims = (((1,), (1,)), ((), ()))
    for at in range(0, hidden, chunk):
        span = slice(at, at + chunk)
        grad_hidden = lax.dot_general(go, down[span, :], last_dims, preferred_element_type=F32)
        grad_pre = grad_hidden * slope[0, :, span].astype(F32)
        total = active * jnp.sum(grad_pre, axis=0, keepdims=True)
        o_up_bias[:, span] = total + keeps[3][:, span] if n_keep else total
        low = grad_pre.astype(BF)
        o_gl[0, :, span] = low
        feat = feat + lax.dot_general(low, up[:, span], last_dims, preferred_element_type=F32)
    normed = z[0].reshape(count, channels)
    sum_gain = jnp.sum(feat * normed, axis=0, keepdims=True)
    sum_norm = jnp.sum(feat, axis=0, keepdims=True)
    grad_normed = feat * vec[3:4]
    inner = (
        grad_normed
        - jnp.mean(grad_normed, axis=-1, keepdims=True)
        - normed * jnp.mean(grad_normed * normed, axis=-1, keepdims=True)
    )
    for at in range(0, channels, LANES):
        lanes = slice(at, at + LANES)
        o_conv[:, :, lanes] = (rs[0] * inner[:, lanes]).reshape(rows, cols, LANES)
    grad_conv = o_conv[...]
    sum_conv = jnp.sum(grad_conv.reshape(count, channels), axis=0, keepdims=True)
    if edges:
        o_low[...] = grad_conv.astype(BF)
        pick_edge(tab[tick, ODD], o_low, near, far)
    blank = jnp.zeros((3, channels), F32)
    sums = active * jnp.concatenate(
        [sum_conv, sum_norm, sum_out, sum_gain, sum_scale, blank], axis=0
    )
    o_sums[...] = sums + keeps[2][...] if n_keep else sums


def spread_kernel(tick, multi, *refs):
    refs = list(refs)
    tab, low, near = (refs.pop(0) for _ in range(3))
    far = refs.pop(0) if multi else None
    res, kern, out, field, total = refs
    rows = low.shape[0]
    fill_sides(field)
    fill_field(
        field,
        low[...],
        near[...],
        None if far is None else far[...],
        tab[tick, ODD],
        rows + 3,
    )
    depthwise(field, kern, total, None, True)
    value = total[...] + res[...].astype(F32)
    out[...] = masked_rows(value, 0, tab[tick, HEIGHT]).astype(BF)


def taps_kernel(tick, n_keep, *refs):
    refs = list(refs)
    tab, pad, conv = (refs.pop(0) for _ in range(3))
    keep = refs.pop(0) if n_keep else None
    out, field = refs
    rows, cols, channels = conv.shape
    group = group_of(rows)
    active = tab[tick, ACTIVE].astype(F32)
    fill_sides(field)
    field[:, LEFT : LEFT + cols, :] = pad[0].astype(F32)
    out[49:, :] = jnp.zeros((out.shape[0] - 49, channels), F32)
    for at in range(0, channels, LANES):
        lanes = slice(at, at + LANES)
        for j in range(7):

            def step(g, accs, lanes=lanes, j=j):
                part = field[pl.ds(g * group, group + 6), LEFT - 3 + j : LEFT - 3 + j + cols, lanes]
                grad = conv[pl.ds(g * group, group), :, lanes]
                return tuple(
                    acc
                    + jnp.sum(
                        (part[i : i + group] * grad).reshape(group * cols // 8, 8, LANES), axis=0
                    )
                    for i, acc in enumerate(accs)
                )

            zero = jnp.zeros((8, LANES), F32)
            accs = lax.fori_loop(0, rows // group, step, (zero,) * 7)
            for i in range(7):
                tap = i * 7 + j
                total = active * jnp.sum(accs[i], axis=0, keepdims=True)
                if n_keep:
                    total = total + keep[tap : tap + 1, lanes]
                out[tap : tap + 1, lanes] = total


def product_kernel(slots, tab, left, right, out):
    first_dims = (((0,), (0,)), ((), ()))
    total = lax.dot_general(left[0], right[0], first_dims, preferred_element_type=F32)
    for slot in range(1, slots):
        total = total + lax.dot_general(
            left[slot], right[slot], first_dims, preferred_element_type=F32
        )
    out[0] = total.astype(BF)


def place_kernel(shards, tab, *refs):
    pieces, (down, up) = refs[: 2 * shards], refs[2 * shards :]
    channels = up.shape[0]
    half = down.shape[0] // 2
    share = half // shards
    per = channels // share
    for odd in range(2):
        for at in range(shards):

            @pl.when((tab[0, ODD] == odd) & (tab[0, 8] == at))
            def _(odd=odd, at=at):
                for side in range(2):
                    base = half * (odd ^ side)
                    for k in range(shards):
                        piece = pieces[side * shards + k]
                        i = at ^ k
                        down[base + i * share : base + (i + 1) * share, :] = piece[0]
                        top = (i % per) * share
                        lane = base + (i // per) * channels
                        up[top : top + share, lane : lane + channels] = piece[1]


def body(
    images, cotangent, order, heights, kernel, biases, gain, scale, up_weight, up_bias, down_weight
):
    sections = lax.axis_size("section")
    shards = lax.axis_size("dp")
    strips = lax.axis_size("rows")
    section_at = lax.axis_index("section")
    row_at = lax.axis_index("rows")
    shard_at = lax.axis_index("dp")
    multi = strips > 2
    slots, rows, cols, channels = images.shape
    hidden = up_weight.shape[2]
    count = rows * cols
    chunk = 256
    odd = row_at % 2
    kern, up, down = kernel[0], up_weight[0], down_weight[0]
    vec = jnp.concatenate([biases[0], gain, scale, jnp.zeros((3, channels), F32)], axis=0)
    ticks = slots + sections - 1

    def tick_table(lag):
        offset = jnp.arange(ticks, dtype=jnp.int32) - lag
        active = (offset >= 0) & (offset < slots)
        slot = jnp.clip(offset, 0, slots - 1)
        image = order[0][slot]
        limit = heights[image] - row_at * rows
        same = [
            (section_at == 0).astype(jnp.int32),
            (section_at == sections - 1).astype(jnp.int32),
            odd.astype(jnp.int32),
            shard_at.astype(jnp.int32),
        ]
        columns = [image, limit, jnp.where(active, slot, slots), slot, active.astype(jnp.int32)]
        columns += [jnp.full((ticks,), v, jnp.int32) for v in same]
        return jnp.stack(columns, axis=1)

    table_forward = tick_table(section_at)
    table_backward = tick_table(sections - 1 - section_at)

    row_pairs = [(i, i ^ 1) for i in range(strips)]
    beyond = [(i, i + 1) for i in range(1, strips - 1, 2)]
    beyond += [(b, a) for a, b in beyond]
    both = ("section", "rows")

    def onward(pairs, step):
        stops = range(max(0, -step), min(sections, sections - step))
        return [(s * strips + a, (s + step) * strips + b) for s in stops for a, b in pairs]

    def exchange(near, far):
        return [lax.ppermute(near, "rows", row_pairs)] + (
            [lax.ppermute(far, "rows", beyond)] if multi else []
        )

    straight = [(i, i) for i in range(strips)]
    last_rows, first_rows = images[:, rows - 3 :], images[:, :3]
    image_edges = exchange(
        jnp.where(odd == 1, first_rows, last_rows), jnp.where(odd == 1, last_rows, first_rows)
    )

    strip_shape = (rows, cols, channels)
    edge_shape = (3, cols, channels)
    field_shape = (rows + 6, cols + WIDE, channels)

    keep_shapes = [
        ((rows + 6, cols, channels), BF),
        (strip_shape, F32),
        ((count, LANES), F32),
        ((count, channels), BF),
        ((count, hidden), BF),
        ((count, hidden), BF),
        ((count, channels), F32),
    ]
    kept = ()
    moved = []
    weights = (kern, vec, up, up_bias, down)
    for tick in range(ticks):
        sources = (tick < slots, tick > 0)
        sends = tick < ticks - 1
        operands, specs = [], []
        if sources[0]:
            operands += [images] + image_edges
            specs += [picked(strip_shape, tick, IMAGE)]
            specs += [picked(edge_shape, tick, IMAGE)] * len(image_edges)
        if sources[1]:
            operands += moved
            specs += [whole(v.shape) for v in moved]
        operands += weights
        specs += [whole(v.shape) for v in weights]
        base = 1 + len(operands)
        operands += kept
        specs += [pl.BlockSpec(memory_space=pl.ANY)] * len(kept)
        out_shapes, out_specs = [], []
        if sends:
            for shape in [strip_shape, edge_shape] + ([edge_shape] if multi else []):
                out_shapes.append(jax.ShapeDtypeStruct(shape, BF))
                out_specs.append(whole(shape))
        lead = len(out_shapes)
        for shape, dtype in keep_shapes:
            out_shapes.append(jax.ShapeDtypeStruct((slots + 1,) + shape, dtype))
            out_specs.append(picked(shape, tick, WRITE))
        results = pl.pallas_call(
            functools.partial(
                forward_kernel, tick, sources, multi, sends, chunk, len(kept)
            ),
            out_shape=out_shapes,
            grid_spec=pltpu.PrefetchScalarGridSpec(
                num_scalar_prefetch=1,
                grid=(1,),
                in_specs=specs,
                out_specs=out_specs,
                scratch_shapes=[pltpu.VMEM(field_shape, F32)],
            ),
            input_output_aliases={base + i: lead + i for i in range(len(kept))},
            compiler_params=params(),
            name="forward",
        )(table_forward, *operands)
        kept = tuple(results[lead:])
        if sends:
            moved = [
                lax.ppermute(results[0], both, onward(straight, 1)),
                lax.ppermute(results[1], both, onward(row_pairs, 1)),
            ]
            if multi:
                moved.append(lax.ppermute(results[2], both, onward(beyond, 1)))
    k_pad, k_z, k_rs, k_n, k_h, k_slope, k_branch = kept

    stacked = ()
    tap_sums = None
    incoming = None
    for tick in range(ticks):
        sources = (tick < slots, tick > 0)
        edges = tick < ticks - 1
        operands, specs = [], []
        if sources[0]:
            operands.append(cotangent)
            specs.append(picked(strip_shape, tick, READ))
        if sources[1]:
            operands.append(incoming)
            specs.append(whole(strip_shape))
        operands += [k_z, k_rs, k_slope, k_branch, vec, up, down]
        specs += [
            picked(strip_shape, tick, READ),
            picked((count, LANES), tick, READ),
            picked((count, hidden), tick, READ),
            picked((count, channels), tick, READ),
            whole(vec.shape),
            whole(up.shape),
            whole(down.shape),
        ]
        base = 1 + len(operands)
        operands += stacked
        if stacked:
            specs += [pl.BlockSpec(memory_space=pl.ANY)] * 2
            specs += [whole((8, channels)), whole((1, hidden))]
        out_shapes = [
            jax.ShapeDtypeStruct((slots + 1, count, channels), BF),
            jax.ShapeDtypeStruct((slots + 1, count, hidden), BF),
            jax.ShapeDtypeStruct((8, channels), F32),
            jax.ShapeDtypeStruct((1, hidden), F32),
            jax.ShapeDtypeStruct(strip_shape, F32),
        ]
        out_specs = [
            picked((count, channels), tick, WRITE),
            picked((count, hidden), tick, WRITE),
            whole((8, channels)),
            whole((1, hidden)),
            whole(strip_shape),
        ]
        if edges:
            for shape in [strip_shape, strip_shape, edge_shape] + ([edge_shape] if multi else []):
                out_shapes.append(jax.ShapeDtypeStruct(shape, BF))
                out_specs.append(whole(shape))
        results = pl.pallas_call(
            functools.partial(chain_kernel, tick, sources, multi, edges, chunk, len(stacked)),
            out_shape=out_shapes,
            grid_spec=pltpu.PrefetchScalarGridSpec(
                num_scalar_prefetch=1, grid=(1,), in_specs=specs, out_specs=out_specs
            ),
            input_output_aliases={base + i: i for i in range(len(stacked))},
            compiler_params=params(),
            name="chain",
        )(table_backward, *operands)
        stacked = tuple(results[:4])
        grad_conv = results[4]
        if edges:
            halos = exchange(results[7], results[8] if multi else None)
            operands = [results[6]] + halos + [results[5], kern]
            spread = pl.pallas_call(
                functools.partial(spread_kernel, tick, multi),
                out_shape=jax.ShapeDtypeStruct(strip_shape, BF),
                grid_spec=pltpu.PrefetchScalarGridSpec(
                    num_scalar_prefetch=1,
                    grid=(1,),
                    in_specs=[whole(v.shape) for v in operands],
                    out_specs=whole(strip_shape),
                    scratch_shapes=[
                        pltpu.VMEM(field_shape, F32),
                        pltpu.VMEM(strip_shape, F32),
                    ],
                ),
                compiler_params=params(),
                name="spread",
            )(table_backward, *operands)
            incoming = lax.ppermute(spread, both, onward(straight, -1))
        operands = [k_pad, grad_conv] + ([tap_sums] if tick else [])
        tap_sums = pl.pallas_call(
            functools.partial(taps_kernel, tick, int(tick > 0)),
            out_shape=jax.ShapeDtypeStruct((56, channels), F32),
            grid_spec=pltpu.PrefetchScalarGridSpec(
                num_scalar_prefetch=1,
                grid=(1,),
                in_specs=[picked((rows + 6, cols, channels), tick, READ), whole(strip_shape)]
                + [whole((56, channels))] * int(tick > 0),
                out_specs=whole((56, channels)),
                scratch_shapes=[pltpu.VMEM(field_shape, F32)],
            ),
            input_output_aliases={3: 0} if tick else {},
            compiler_params=params(),
            name="taps",
        )(table_backward, *operands)
    k_go, k_gl, sums, up_bias_sum = stacked

    factor = 1.0 / math.sqrt(shards * slots * strips * rows * cols)
    width = hidden // 4

    def product(mine):
        def call(left, right, wide_left):
            narrow = pl.BlockSpec((slots, count, channels), lambda j, tab: (0, 0, 0))

            def at(j, tab):
                half = tab[0, ODD] if mine else 1 - tab[0, ODD]
                return (0, 0, half * 2 + j)

            wide = pl.BlockSpec((slots, count, width), at)
            shape = (2,) + ((width, channels) if wide_left else (channels, width))
            return pl.pallas_call(
                functools.partial(product_kernel, slots),
                out_shape=jax.ShapeDtypeStruct(shape, BF),
                grid_spec=pltpu.PrefetchScalarGridSpec(
                    num_scalar_prefetch=1,
                    grid=(2,),
                    in_specs=[wide, narrow] if wide_left else [narrow, wide],
                    out_specs=pl.BlockSpec((1,) + shape[1:], lambda j, tab: (j, 0, 0)),
                ),
                compiler_params=params(),
                name="product",
            )(table_backward, left, right)

        return call(k_h, k_go, True), call(k_n, k_gl, False)

    small = jnp.concatenate([tap_sums, sums, up_bias_sum.reshape(-1, channels)], axis=0)
    if multi:
        small = lax.psum(small, ("rows", "dp"))
        parts = [product(False), product(True)]
        down_low, up_low = (
            jnp.where(odd == 1, *(jnp.stack([p[k] for p in o]) for o in (parts, parts[::-1])))
            for k in range(2)
        )
        down_grad = lax.psum(down_low.astype(F32).reshape(hidden, channels), ("rows", "dp"))
        up_grad = up_low.astype(F32).reshape(4, channels, width).transpose(1, 0, 2)
        up_grad = lax.psum(up_grad.reshape(channels, hidden), ("rows", "dp"))
        down_grad = (down_grad * factor).astype(BF)
        up_grad = (up_grad * factor).astype(BF)
    else:
        share = hidden // 2 // shards

        def swap(value):
            return lax.ppermute(value, "rows", row_pairs)

        def peers(values):
            return [
                lax.ppermute(v, "dp", [(i, i ^ k) for i in range(shards)])
                for k, v in enumerate(values)
                if k
            ]

        def tree(values):
            while len(values) > 1:
                values = [a + b for a, b in zip(values[::2], values[1::2])]
            return values[0]

        theirs = [swap(v) for v in product(False)]
        halves = [
            (a.astype(F32) + b.astype(F32)).astype(BF).reshape(shards, share, channels)
            for a, b in zip(product(True), theirs)
        ]
        halves = jnp.stack(halves, axis=1)
        pieces = [
            lax.dynamic_index_in_dim(halves, shard_at ^ k, 0, keepdims=False)
            for k in range(shards)
        ]
        reduced = tree([v.astype(F32) for v in [pieces[0]] + peers(pieces)])
        reduced = (reduced * factor).astype(BF)
        mine = [reduced] + peers([reduced] * shards)
        others = [swap(v) for v in mine]
        small = small + swap(small)
        small = tree([small] + peers([small] * shards))
        operands = mine + others
        down_grad, up_grad = pl.pallas_call(
            functools.partial(place_kernel, shards),
            out_shape=[
                jax.ShapeDtypeStruct((hidden, channels), BF),
                jax.ShapeDtypeStruct((channels, hidden), BF),
            ],
            grid_spec=pltpu.PrefetchScalarGridSpec(
                num_scalar_prefetch=1,
                grid=(1,),
                in_specs=[whole(v.shape) for v in operands],
                out_specs=[whole((hidden, channels)), whole((channels, hidden))],
            ),
            compiler_params=params(),
            name="place",
        )(table_backward, *operands)

    small = (small * factor).astype(BF)
    return (
        small[None, :49],
        small[None, 56:59],
        small[59:60],
        small[60:61],
        up_grad[None],
        small[64:].reshape(1, hidden),
        down_grad[None],
    )


def solution(mesh):
    in_specs = (
        P("dp", "rows", None, None),
        P("dp", "rows", None, None),
        P("dp", None),
        P("dp"),
        P("section", None, None),
        P("section", None, None),
        P("section", None),
        P("section", None),
        P("section", None, None),
        P("section", None),
        P("section", None, None),
    )
    out_specs = (
        P("section", None, None),
        P("section", None, None),
        P("section", None),
        P("section", None),
        P("section", None, None),
        P("section", None),
        P("section", None, None),
    )
    return jax.shard_map(body, mesh=mesh, in_specs=in_specs, out_specs=out_specs, check_vma=False)
```

```python
import functools
import math

import jax
import jax.numpy as jnp
from jax import lax
from jax.experimental import pallas as pl
from jax.experimental.pallas import tpu as pltpu
from jax.sharding import PartitionSpec as P

EPS = 1e-06
ROOT_HALF = 0.7071067811865476
INV_ROOT_TAU = 0.3989422804014327
BF = jnp.bfloat16
F32 = jnp.float32
LANES = 128
CHUNK = 512
VMEM_LIMIT = 28 * 1024 * 1024

IN_VMEM = pl.BlockSpec(memory_space=pltpu.VMEM)
IN_SMEM = pl.BlockSpec(memory_space=pltpu.SMEM)
ANYWHERE = pl.BlockSpec(memory_space=pl.ANY)


def call(kernel, name, info, operands, outputs, unread=(), keeps=(), scratch=()):
    base = 1 + len(operands) + len(unread)
    lead = len(outputs) - len(keeps)
    return pl.pallas_call(
        kernel,
        out_shape=[jax.ShapeDtypeStruct(*o) for o in outputs],
        in_specs=[IN_SMEM]
        + [IN_VMEM] * len(operands)
        + [ANYWHERE] * len(unread)
        + [IN_VMEM] * len(keeps),
        out_specs=[IN_VMEM] * len(outputs),
        scratch_shapes=[pltpu.VMEM(*s) for s in scratch],
        input_output_aliases={base + i: lead + i for i in range(len(keeps))},
        compiler_params=pltpu.CompilerParams(vmem_limit_bytes=VMEM_LIMIT),
        name=name,
    )(info, *operands, *unread, *keeps)


class Plan:
    def __init__(self, slots, sections, rows, multi):
        self.slots, self.sections, self.rows, self.multi = slots, sections, rows, multi

    def at(self, info, tick, backward):
        section = info[2 * self.slots]
        lag = self.sections - 1 - section if backward else section
        offset = tick - lag
        slot = jnp.clip(offset, 0, self.slots - 1)
        image = info[slot]
        limit = info[self.slots + image] - info[2 * self.slots + 1] * self.rows
        return (offset >= 0) & (offset < self.slots), slot, image, limit

    def section(self, info):
        return info[2 * self.slots]

    def odd(self, info):
        return info[2 * self.slots + 1] % 2

    def shard(self, info):
        return info[2 * self.slots + 2]


def group_of(rows):
    return next(g for g in (8, 6, 4, 3, 2, 1) if rows % g == 0)


def masked_rows(value, first, limit):
    row = lax.broadcasted_iota(jnp.int32, value.shape, 0) + first
    return jnp.where(row < limit, value, 0.0)


def moved_cols(value, steps):
    if steps == 0:
        return value
    cols = value.shape[1]
    col = lax.broadcasted_iota(jnp.int32, value.shape, 1)
    inside = col < cols - steps if steps > 0 else col >= -steps
    return jnp.where(inside, pltpu.roll(value, (-steps) % cols, 1), 0.0)


def fill_field(field, middle, near, far, odd, limit):
    rows = middle.shape[0]
    field[3 : 3 + rows] = masked_rows(middle.astype(F32), 0, limit)
    near = near.astype(F32)
    far = jnp.zeros(near.shape, F32) if far is None else far.astype(F32)

    @pl.when(odd == 1)
    def _():
        field[0:3] = masked_rows(near, -3, limit)
        field[rows + 3 :] = masked_rows(far, rows, limit)

    @pl.when(odd == 0)
    def _():
        field[0:3] = masked_rows(far, -3, limit)
        field[rows + 3 :] = masked_rows(near, rows, limit)


def depthwise(field, kern, out, bias, flip):
    rows, cols, channels = out.shape
    group = group_of(rows)
    for at in range(0, channels, LANES):
        lanes = slice(at, at + LANES)

        def step(g, _, lanes=lanes):
            part = field[pl.ds(g * group, group + 6), :, lanes]
            total = jnp.zeros((group, cols, LANES), F32)
            for j in range(7):
                acc = jnp.zeros((group, cols, LANES), F32)
                for i in range(7):
                    tap = 48 - (i * 7 + j) if flip else i * 7 + j
                    acc = acc + kern[tap : tap + 1, lanes][None] * part[i : i + group]
                total = total + moved_cols(acc, j - 3)
            if bias is not None:
                total = total + bias[:, lanes][None]
            out[pl.ds(g * group, group), :, lanes] = total
            return 0

        lax.fori_loop(0, rows // group, step, 0)


def pick_edge(odd, value, near, far):
    rows = value.shape[0]

    @pl.when(odd == 1)
    def _():
        near[...] = value[0:3]
        if far is not None:
            far[...] = value[rows - 3 :]

    @pl.when(odd == 0)
    def _():
        near[...] = value[rows - 3 :]
        if far is not None:
            far[...] = value[0:3]


def forward_kernel(plan, tick, sources, sends, n_keep, *refs):
    refs = list(refs)
    info = refs.pop(0)
    feeds = []
    for _ in range(sources[0] + sources[1]):
        feeds.append([refs.pop(0), refs.pop(0), refs.pop(0) if plan.multi else None])
    kern, bias, gain, scale, up, up_bias, down = (refs.pop(0) for _ in range(7))
    del refs[:n_keep]
    outgoing = refs.pop(0) if sends else None
    near = refs.pop(0) if sends else None
    far = refs.pop(0) if sends and plan.multi else None
    o_pad, o_z, o_rs, o_n, o_h, o_slope, o_branch, field = refs
    _, rows, cols, channels = o_z.shape
    count = rows * cols
    hidden = up.shape[2]
    active, slot, image, limit = plan.at(info, tick, False)
    odd = plan.odd(info)

    @pl.when(active)
    def _():
        left = list(feeds)
        first = plan.section(info) == 0
        if sources[0]:
            img = left.pop(0)

            @pl.when(first)
            def _():
                fill_field(field, *(None if v is None else v[image] for v in img), odd, limit)

        if sources[1]:
            mid = left.pop(0)

            @pl.when(jnp.logical_not(first))
            def _():
                fill_field(field, *(None if v is None else v[...] for v in mid), odd, limit)

        o_pad[slot] = field[...].astype(BF)
        depthwise(field, kern.at[0], o_z.at[slot], bias[0, 0:1], False)
        conv = o_z[slot].reshape(count, channels)
        centred = conv - jnp.mean(conv, axis=-1, keepdims=True)
        inv_std = lax.rsqrt(jnp.mean(centred * centred, axis=-1, keepdims=True) + EPS)
        normed = centred * inv_std
        o_z[slot] = normed.reshape(rows, cols, channels)
        o_rs[slot] = jnp.broadcast_to(inv_std, (count, LANES))
        features = (normed * gain[...] + bias[0, 1:2]).astype(BF)
        o_n[slot] = features
        acc = jnp.zeros((count, channels), F32)
        for at in range(0, hidden, CHUNK):
            span = slice(at, at + CHUNK)
            pre = jnp.dot(features, up[0, :, span], preferred_element_type=F32) + up_bias[:, span]
            bell = 1.0 + lax.erf(pre * ROOT_HALF)
            act = (0.5 * pre * bell).astype(BF)
            o_h[slot, :, span] = act
            o_slope[slot, :, span] = (
                0.5 * bell + pre * jnp.exp(-0.5 * pre * pre) * INV_ROOT_TAU
            ).astype(BF)
            acc = acc + jnp.dot(act, down[0, span, :], preferred_element_type=F32)
        branch = acc + bias[0, 2:3]
        o_branch[slot] = branch
        if sends:
            value = field[3 : 3 + rows] + (scale[...] * branch).reshape(rows, cols, channels)
            outgoing[...] = masked_rows(value, 0, limit).astype(BF)
            pick_edge(odd, outgoing, near, far)


def residual(plan, info, tick, cot, incoming, slot, limit):
    if cot is None:
        grad = incoming[...].astype(F32)
    elif incoming is None:
        grad = cot[slot].astype(F32)
    else:
        last = plan.section(info) == plan.sections - 1
        grad = jnp.where(last, cot[slot].astype(F32), incoming[...].astype(F32))
    return masked_rows(grad, 0, limit)


def chain_kernel(plan, tick, sources, edges, n_keep, *refs):
    refs = list(refs)
    info = refs.pop(0)
    cot = refs.pop(0) if sources[0] else None
    incoming = refs.pop(0) if sources[1] else None
    z, rs, slope, branch, gain, scale, up, down = (refs.pop(0) for _ in range(8))
    old_sums, old_up_bias = (refs.pop(0), refs.pop(0)) if n_keep else (None, None)
    o_go, o_gl, o_conv = (refs.pop(0) for _ in range(3))
    o_res = refs.pop(0) if edges else None
    o_low = refs.pop(0) if edges else None
    near = refs.pop(0) if edges else None
    far = refs.pop(0) if edges and plan.multi else None
    o_sums, o_up_bias = refs
    rows, cols, channels = o_conv.shape
    count = rows * cols
    hidden = up.shape[2]
    active, slot, _, limit = plan.at(info, tick, True)
    if not n_keep:

        @pl.when(jnp.logical_not(active))
        def _():
            o_sums[...] = jnp.zeros(o_sums.shape, F32)
            o_up_bias[...] = jnp.zeros(o_up_bias.shape, F32)

    @pl.when(active)
    def _():
        grad_res = residual(plan, info, tick, cot, incoming, slot, limit)
        if edges:
            o_res[...] = grad_res.astype(BF)
        flat = grad_res.reshape(count, channels)
        scaled = scale[...] * flat
        sum_scale = jnp.sum(branch[slot] * flat, axis=0, keepdims=True)
        sum_out = jnp.sum(scaled, axis=0, keepdims=True)
        go = scaled.astype(BF)
        o_go[...] = go
        feat = jnp.zeros((count, channels), F32)
        last_dims = (((1,), (1,)), ((), ()))
        for at in range(0, hidden, CHUNK):
            span = slice(at, at + CHUNK)
            grad_hidden = lax.dot_general(
                go, down[0, span, :], last_dims, preferred_element_type=F32
            )
            grad_pre = grad_hidden * slope[slot, :, span].astype(F32)
            total = jnp.sum(grad_pre, axis=0, keepdims=True)
            o_up_bias[:, span] = total + old_up_bias[:, span] if n_keep else total
            low = grad_pre.astype(BF)
            o_gl[:, span] = low
            feat = feat + lax.dot_general(
                low, up[0, :, span], last_dims, preferred_element_type=F32
            )
        normed = z[slot].reshape(count, channels)
        sum_gain = jnp.sum(feat * normed, axis=0, keepdims=True)
        sum_norm = jnp.sum(feat, axis=0, keepdims=True)
        grad_normed = feat * gain[...]
        inner = (
            grad_normed
            - jnp.mean(grad_normed, axis=-1, keepdims=True)
            - normed * jnp.mean(grad_normed * normed, axis=-1, keepdims=True)
        )
        for at in range(0, channels, LANES):
            lanes = slice(at, at + LANES)
            o_conv[:, :, lanes] = (rs[slot] * inner[:, lanes]).reshape(rows, cols, LANES)
        grad_conv = o_conv[...]
        sum_conv = jnp.sum(grad_conv.reshape(count, channels), axis=0, keepdims=True)
        if edges:
            o_low[...] = grad_conv.astype(BF)
            pick_edge(plan.odd(info), o_low, near, far)
        blank = jnp.zeros((3, channels), F32)
        sums = jnp.concatenate([sum_conv, sum_norm, sum_out, sum_gain, sum_scale, blank], axis=0)
        o_sums[...] = sums + old_sums[...] if n_keep else sums


def spread_kernel(plan, tick, *refs):
    refs = list(refs)
    info, low, near = (refs.pop(0) for _ in range(3))
    far = refs.pop(0) if plan.multi else None
    res, kern, out, field, total = refs
    rows = low.shape[0]
    active, _, _, limit = plan.at(info, tick, True)

    @pl.when(active)
    def _():
        fill_field(
            field,
            low[...],
            near[...],
            None if far is None else far[...],
            plan.odd(info),
            rows + 3,
        )
        depthwise(field, kern.at[0], total, None, True)
        value = total[...] + res[...].astype(F32)
        out[...] = masked_rows(value, 0, limit).astype(BF)


def taps_kernel(plan, tick, n_unread, n_keep, info, pad, conv, *refs):
    refs = refs[n_unread:]
    old = refs[0] if n_keep else None
    out = refs[n_keep]
    rows, cols, channels = conv.shape
    group = group_of(rows)
    active, slot, _, _ = plan.at(info, tick, True)
    if not n_keep:

        @pl.when(jnp.logical_not(active))
        def _():
            out[...] = jnp.zeros(out.shape, F32)

    @pl.when(active)
    def _():
        out[49:, :] = jnp.zeros((out.shape[0] - 49, channels), F32)
        for at in range(0, channels, LANES):
            lanes = slice(at, at + LANES)
            for j in range(7):

                def step(g, accs, lanes=lanes, j=j):
                    part = pad[slot, pl.ds(g * group, group + 6), :, lanes].astype(F32)
                    grad = moved_cols(conv[pl.ds(g * group, group), :, lanes], 3 - j)
                    return tuple(
                        acc
                        + jnp.sum(
                            (part[i : i + group] * grad).reshape(group * cols // 8, 8, LANES),
                            axis=0,
                        )
                        for i, acc in enumerate(accs)
                    )

                zero = jnp.zeros((8, LANES), F32)
                accs = lax.fori_loop(0, rows // group, step, (zero,) * 7)
                for i in range(7):
                    tap = i * 7 + j
                    total = jnp.sum(accs[i], axis=0, keepdims=True)
                    if n_keep:
                        total = total + old[tap : tap + 1, lanes]
                    out[tap : tap + 1, lanes] = total


def first_product(left, right):
    return lax.dot_general(
        left, right, (((0,), (0,)), ((), ())), preferred_element_type=F32
    )


def product_kernel(plan, tick, last, wide_left, n_unread, n_keep, info, left, right, *refs):
    refs = refs[n_unread:]
    old = refs[0] if n_keep else None
    outs = refs[n_keep:]
    active, slot, _, _ = plan.at(info, tick, True)
    odd = plan.odd(info)
    stacked = left if wide_left else right
    width = stacked.shape[-1] // 4

    def term(block, odd):
        at = (block + 2 * (1 - odd)) % 4 * width
        span = slice(at, at + width)
        if wide_left:
            return first_product(left[slot, :, span], right[...])
        return first_product(left[slot], right[:, span])

    def put(block, value):
        if last:
            outs[block // 2][block % 2] = value.astype(BF)
        else:
            outs[0][block] = value

    for side in range(2):

        @pl.when(active & (odd == side) & (slot == 0))
        def _(side=side):
            for block in range(4):
                put(block, term(block, side))

        if n_keep:

            @pl.when(active & (odd == side) & (slot > 0))
            def _(side=side):
                for block in range(4):
                    put(block, old[block] + term(block, side))

    if last and n_keep:

        @pl.when(jnp.logical_not(active))
        def _():
            for block in range(4):
                put(block, old[block])


def merge_kernel(plan, shards, info, mine, theirs, *outs):
    blocks, height, channels = mine.shape
    total = mine[...].astype(F32) + theirs[...].astype(F32)
    total = total.reshape(shards, blocks * height // shards, channels)
    at = plan.shard(info)
    for own in range(shards):

        @pl.when(at == own)
        def _(own=own):
            for k, out in enumerate(outs):
                out[...] = total[own ^ k].astype(BF)


def tree(values):
    while len(values) > 1:
        values = [a + b for a, b in zip(values[::2], values[1::2])]
    return values[0]


def finish_kernel(factor, info, *refs):
    refs[-1][...] = (tree([r[...].astype(F32) for r in refs[:-1]]) * factor).astype(BF)


def place_kernel(plan, shards, flat, info, *refs):
    pieces, out = refs[:-1], refs[-1]
    share, channels = pieces[0].shape
    half = share * shards
    per = channels // share
    for odd in range(2):
        for at in range(shards):

            @pl.when((plan.odd(info) == odd) & (plan.shard(info) == at))
            def _(odd=odd, at=at):
                for side in range(2):
                    base = half * (odd ^ side)
                    for k in range(shards):
                        piece = pieces[side * shards + k]
                        i = at ^ k
                        if flat:
                            out[base + i * share : base + (i + 1) * share, :] = piece[...]
                        else:
                            top = (i % per) * share
                            lane = base + (i // per) * channels
                            out[top : top + share, lane : lane + channels] = piece[...]


def body(
    images, cotangent, order, heights, kernel, biases, gain, scale, up_weight, up_bias, down_weight
):
    sections = lax.axis_size("section")
    shards = lax.axis_size("dp")
    strips = lax.axis_size("rows")
    section_at = lax.axis_index("section")
    row_at = lax.axis_index("rows")
    shard_at = lax.axis_index("dp")
    multi = strips > 2
    slots, rows, cols, channels = images.shape
    hidden = up_weight.shape[2]
    count = rows * cols
    odd = row_at % 2
    ticks = slots + sections - 1
    plan = Plan(slots, sections, rows, multi)
    here = jnp.stack([section_at, row_at, shard_at]).astype(jnp.int32)
    info = jnp.concatenate([order[0], heights, here])

    row_pairs = [(i, i ^ 1) for i in range(strips)]
    straight = [(i, i) for i in range(strips)]
    beyond = [(i, i + 1) for i in range(1, strips - 1, 2)]
    beyond += [(b, a) for a, b in beyond]
    both = ("section", "rows")

    def onward(pairs, stages, step):
        return [(s * strips + a, (s + step) * strips + b) for s in stages for a, b in pairs]

    def exchange(near, far):
        return [lax.ppermute(near, "rows", row_pairs)] + (
            [lax.ppermute(far, "rows", beyond)] if multi else []
        )

    last_rows, first_rows = images[:, rows - 3 :], images[:, :3]
    image_edges = exchange(
        jnp.where(odd == 1, first_rows, last_rows), jnp.where(odd == 1, last_rows, first_rows)
    )

    strip_shape = (rows, cols, channels)
    field_shape = (rows + 6, cols, channels)
    strip_out = (strip_shape, BF)
    edge_outs = [((3, cols, channels), BF)] * (2 if multi else 1)

    kept_outs = [
        ((slots,) + field_shape, BF),
        ((slots,) + strip_shape, F32),
        ((slots, count, LANES), F32),
        ((slots, count, channels), BF),
        ((slots, count, hidden), BF),
        ((slots, count, hidden), BF),
        ((slots, count, channels), F32),
    ]
    kept = []
    moved = []
    for tick in range(ticks):
        sources = (tick < slots, tick > 0)
        sends = tick < ticks - 1
        operands = ([images] + image_edges) * sources[0] + moved
        operands += [kernel, biases, gain, scale, up_weight, up_bias, down_weight]
        outputs = ([strip_out] + edge_outs) * sends + kept_outs
        results = call(
            functools.partial(forward_kernel, plan, tick, sources, sends, len(kept)),
            "forward",
            info,
            operands,
            outputs,
            keeps=kept,
            scratch=[(field_shape, F32)],
        )
        kept = list(results[len(results) - len(kept_outs) :])
        if sends:
            stages = [s for s in range(sections - 1) if 0 <= tick - s < slots]
            moved = [
                lax.ppermute(results[0], both, onward(straight, stages, 1)),
                lax.ppermute(results[1], both, onward(row_pairs, stages, 1)),
            ]
            if multi:
                moved.append(lax.ppermute(results[2], both, onward(beyond, stages, 1)))
    k_pad, k_z, k_rs, k_n, k_h, k_slope, k_branch = kept

    sums = []
    taps = []
    product_keeps = [[], []]
    incoming = None
    width = hidden // 4
    for tick in range(ticks):
        sources = (tick < slots, tick > 0)
        last = tick == ticks - 1
        operands = [cotangent] * sources[0] + [incoming] * sources[1]
        operands += [k_z, k_rs, k_slope, k_branch, gain, scale, up_weight, down_weight]
        outputs = [((count, channels), BF), ((count, hidden), BF), (strip_shape, F32)]
        outputs += ([strip_out] * 2 + edge_outs) * (not last)
        sum_outs = [((8, channels), F32), ((1, hidden), F32)]
        results = call(
            functools.partial(chain_kernel, plan, tick, sources, not last, len(sums)),
            "chain",
            info,
            operands,
            outputs + sum_outs,
            keeps=sums,
        )
        sums = list(results[-2:])
        go, gl, grad_conv = results[:3]
        unread = []
        if not last:
            halos = exchange(results[5], results[6] if multi else None)
            (spread,) = call(
                functools.partial(spread_kernel, plan, tick),
                "spread",
                info,
                [results[4]] + halos + [results[3], kernel],
                [strip_out],
                scratch=[(field_shape, F32), (strip_shape, F32)],
            )
            stages = [s for s in range(1, sections) if 0 <= tick - (sections - 1 - s) < slots]
            incoming = lax.ppermute(spread, both, onward(straight, stages, -1))
            unread = [spread]
        for at, (left, right, shape) in enumerate(
            [(k_h, go, (width, channels)), (k_n, gl, (channels, width))]
        ):
            product_keep = product_keeps[at]
            outputs = [((2,) + shape, BF)] * 2 if last else [((4,) + shape, F32)]
            product_keeps[at] = call(
                functools.partial(
                    product_kernel, plan, tick, last, at == 0, len(unread), len(product_keep)
                ),
                "product",
                info,
                [left, right] + list(product_keep) * last,
                outputs,
                unread=unread,
                keeps=() if last else product_keep,
            )
        taps = call(
            functools.partial(taps_kernel, plan, tick, len(unread), len(taps)),
            "taps",
            info,
            [k_pad, grad_conv],
            [((56, channels), F32)],
            unread=unread,
            keeps=taps,
        )
        if not last:
            incoming, taps, product_keeps = lax.optimization_barrier(
                (incoming, list(taps), [list(v) for v in product_keeps])
            )

    factor = 1.0 / math.sqrt(shards * slots * strips * rows * cols)
    small = jnp.concatenate([taps[0], sums[0], sums[1].reshape(-1, channels)], axis=0)
    if multi:
        small = lax.psum(small, ("rows", "dp"))
        grads = []
        for at, (theirs, mine) in enumerate(product_keeps):
            low = jnp.where(
                odd == 1, jnp.concatenate([theirs, mine]), jnp.concatenate([mine, theirs])
            ).astype(F32)
            if at == 0:
                low = low.reshape(hidden, channels)
            else:
                low = low.transpose(1, 0, 2).reshape(channels, hidden)
            grads.append((lax.psum(low, ("rows", "dp")) * factor).astype(BF))
    else:
        share = hidden // 2 // shards
        piece_out = ((share, channels), BF)

        def swap(value):
            return lax.ppermute(value, "rows", row_pairs)

        def peers(values):
            return [
                lax.ppermute(v, "dp", [(i, i ^ k) for i in range(shards)])
                for k, v in enumerate(values)
                if k
            ]

        grads = []
        for at, (theirs, mine) in enumerate(product_keeps):
            pieces = call(
                functools.partial(merge_kernel, plan, shards),
                "merge",
                info,
                [mine, swap(theirs)],
                [piece_out] * shards,
            )
            (own,) = call(
                functools.partial(finish_kernel, factor),
                "finish",
                info,
                [pieces[0]] + peers(pieces),
                [piece_out],
            )
            own_half = [own] + peers([own] * shards)
            shape = (hidden, channels) if at == 0 else (channels, hidden)
            grads += call(
                functools.partial(place_kernel, plan, shards, at == 0),
                "place",
                info,
                own_half + [swap(v) for v in own_half],
                [(shape, BF)],
            )
        small = small + swap(small)
        small = tree([small] + peers([small] * shards))

    small = (small * factor).astype(BF)
    return (
        small[None, :49],
        small[None, 56:59],
        small[59:60],
        small[60:61],
        grads[1][None],
        small[64:].reshape(1, hidden),
        grads[0][None],
    )


def solution(mesh):
    in_specs = (
        P("dp", "rows", None, None),
        P("dp", "rows", None, None),
        P("dp", None),
        P("dp"),
        P("section", None, None),
        P("section", None, None),
        P("section", None),
        P("section", None),
        P("section", None, None),
        P("section", None),
        P("section", None, None),
    )
    out_specs = (
        P("section", None, None),
        P("section", None, None),
        P("section", None),
        P("section", None),
        P("section", None, None),
        P("section", None),
        P("section", None, None),
    )
    return jax.shard_map(body, mesh=mesh, in_specs=in_specs, out_specs=out_specs, check_vma=False)
```

```python
import functools
import math

import jax
import jax.numpy as jnp
from jax import lax
from jax.experimental import pallas as pl
from jax.experimental.pallas import tpu as pltpu
from jax.sharding import PartitionSpec as P

EPS = 1e-06
ROOT_HALF = 0.7071067811865476
INV_ROOT_TAU = 0.3989422804014327
BF = jnp.bfloat16
F32 = jnp.float32
LANES = 128
CHUNK = 512
VMEM_LIMIT = 20 * 1024 * 1024

IN_VMEM = pl.BlockSpec(memory_space=pltpu.VMEM)
IN_SMEM = pl.BlockSpec(memory_space=pltpu.SMEM)
ANYWHERE = pl.BlockSpec(memory_space=pl.ANY)


TOKEN = ((8, LANES), F32)


def call(kernel, name, info, operands, outputs, after, keeps=(), scratch=()):
    base = 2 + len(operands)
    outputs = [TOKEN] + list(outputs)
    lead = len(outputs) - len(keeps)

    def run(info, *refs):
        kernel(info, *refs[: len(operands)], *refs[len(operands) + 1 + len(keeps) + 1 :])

    results = pl.pallas_call(
        run,
        out_shape=[jax.ShapeDtypeStruct(*o) for o in outputs],
        in_specs=[IN_SMEM] + [IN_VMEM] * len(operands) + [ANYWHERE] + [IN_VMEM] * len(keeps),
        out_specs=[IN_VMEM] * len(outputs),
        scratch_shapes=[pltpu.VMEM(*s) for s in scratch],
        input_output_aliases={base + i: lead + i for i in range(len(keeps))},
        cost_estimate=pl.CostEstimate(
            flops=0, transcendentals=0, bytes_accessed=int(COST[name] * 3.69e6)
        ),
        compiler_params=pltpu.CompilerParams(vmem_limit_bytes=VMEM_LIMIT),
        name=name,
    )(info, *operands, after, *keeps)
    return results[0], list(results[1:])


COST = {
    "forward": 5.0, "pack": 1, "chain": 3.0, "spread": 3, "product": 2, "merge": 1, "taps": 4,
    "total": 1, "finish": 1, "place": 2,
}


class Plan:
    def __init__(self, slots, rows, multi):
        self.slots, self.rows, self.multi = slots, rows, multi

    def section(self, info):
        return info[2 * self.slots]

    def image(self, info, slot):
        return info[slot]

    def limit(self, info, slot):
        height = info[self.slots + info[slot]]
        return height - info[2 * self.slots + 1] * self.rows

    def odd(self, info):
        return info[2 * self.slots + 1] % 2

    def shard(self, info):
        return info[2 * self.slots + 2]


class Packed:
    def __init__(self, ref):
        self.ref = ref

    def bias(self, at):
        return self.ref[49 + at : 50 + at]

    def gain(self):
        return self.ref[52:53]

    def scale(self):
        return self.ref[53:54]


def group_of(rows):
    return next(g for g in (8, 6, 4, 3, 2, 1) if rows % g == 0)


def masked_rows(value, first, limit):
    row = lax.broadcasted_iota(jnp.int32, value.shape, 0) + first
    return jnp.where(row < limit, value, 0.0)


def moved_cols(value, steps):
    if steps == 0:
        return value
    cols = value.shape[1]
    col = lax.broadcasted_iota(jnp.int32, value.shape, 1)
    inside = col < cols - steps if steps > 0 else col >= -steps
    return jnp.where(inside, pltpu.roll(value, (-steps) % cols, 1), 0.0)


def fill_field(field, middle, near, far, odd, limit):
    rows = middle.shape[0]
    field[3 : 3 + rows] = masked_rows(middle.astype(F32), 0, limit)
    near = near.astype(F32)
    far = jnp.zeros(near.shape, F32) if far is None else far.astype(F32)

    @pl.when(odd == 1)
    def _():
        field[0:3] = masked_rows(near, -3, limit)
        field[rows + 3 :] = masked_rows(far, rows, limit)

    @pl.when(odd == 0)
    def _():
        field[0:3] = masked_rows(far, -3, limit)
        field[rows + 3 :] = masked_rows(near, rows, limit)


def depthwise(field, kern, out, bias, flip):
    rows, cols, channels = out.shape
    group = group_of(rows)
    groups = rows // group

    def step(n, _):
        g = n % groups
        lanes = pl.ds(pl.multiple_of(n // groups * LANES, LANES), LANES)
        part = field[pl.ds(g * group, group + 6), :, lanes]
        total = jnp.zeros((group, cols, LANES), F32)
        for j in range(7):
            acc = jnp.zeros((group, cols, LANES), F32)
            for i in range(7):
                tap = 48 - (i * 7 + j) if flip else i * 7 + j
                acc = acc + kern[tap : tap + 1, lanes][None] * part[i : i + group]
            total = total + moved_cols(acc, j - 3)
        if bias is not None:
            total = total + kern[bias : bias + 1, lanes][None]
        out[pl.ds(g * group, group), :, lanes] = total
        return 0

    lax.fori_loop(0, groups * (channels // LANES), step, 0)


def pick_edge(odd, value, near, far):
    rows = value.shape[0]

    @pl.when(odd == 1)
    def _():
        near[...] = value[0:3]
        if far is not None:
            far[...] = value[rows - 3 :]

    @pl.when(odd == 0)
    def _():
        near[...] = value[rows - 3 :]
        if far is not None:
            far[...] = value[0:3]


def forward_kernel(plan, section, slot, sends, info, *refs):
    refs = list(refs)
    if section == 0:
        source = [refs.pop(0), refs.pop(0), refs.pop(0) if plan.multi else None]
    else:
        package = refs.pop(0)
    packed = Packed(refs.pop(0))
    up_bias, up, down = refs.pop(0), refs.pop(0), refs.pop(0)
    outgoing = refs.pop(0) if sends else None
    near = refs.pop(0) if sends else None
    far = refs.pop(0) if sends and plan.multi else None
    o_pad, o_z, o_rs, o_n, o_h, o_slope, o_branch, field = refs
    rows, cols, channels = o_z.shape
    count = rows * cols
    hidden = up.shape[2]
    limit = plan.limit(info, slot)
    odd = plan.odd(info)

    @pl.when(plan.section(info) == section)
    def _():
        if section == 0:
            at = plan.image(info, slot)
            parts = [None if v is None else v[at] for v in source]
        else:
            far_rows = package[rows + 3 :] if plan.multi else None
            parts = [package[0:rows], package[rows : rows + 3], far_rows]
        fill_field(field, *parts, odd, limit)
        o_pad[...] = field[...].astype(BF)
        depthwise(field, packed.ref, o_z, 49, False)
        conv = o_z[...].reshape(count, channels)
        centred = conv - jnp.mean(conv, axis=-1, keepdims=True)
        inv_std = lax.rsqrt(jnp.mean(centred * centred, axis=-1, keepdims=True) + EPS)
        normed = centred * inv_std
        o_z[...] = normed.reshape(rows, cols, channels)
        o_rs[...] = jnp.broadcast_to(inv_std, (count, LANES))
        features = (normed * packed.gain() + packed.bias(1)).astype(BF)
        o_n[...] = features
        o_branch[...] = jnp.broadcast_to(packed.bias(2), (count, channels))

        def units(n, _):
            span = pl.ds(pl.multiple_of(n * CHUNK, CHUNK), CHUNK)
            pre = jnp.dot(o_n[...], up[0, :, span], preferred_element_type=F32) + up_bias[:, span]
            bell = 1.0 + lax.erf(pre * ROOT_HALF)
            act = (0.5 * pre * bell).astype(BF)
            o_h[:, span] = act
            o_slope[:, span] = (
                0.5 * bell + pre * jnp.exp(-0.5 * pre * pre) * INV_ROOT_TAU
            ).astype(BF)
            o_branch[...] += jnp.dot(act, down[0, span, :], preferred_element_type=F32)
            return 0

        lax.fori_loop(0, hidden // CHUNK, units, 0, unroll=True)
        branch = o_branch[...]
        if sends:
            value = field[3 : 3 + rows] + (packed.scale() * branch).reshape(rows, cols, channels)
            outgoing[0:rows] = masked_rows(value, 0, limit).astype(BF)
            pick_edge(odd, outgoing.at[0:rows], near, far)


def chain_kernel(plan, section, slot, top, edges, info, *refs):
    refs = list(refs)
    grad_out, z, rs, slope, branch = (refs.pop(0) for _ in range(5))
    packed = Packed(refs.pop(0))
    up, down = refs.pop(0), refs.pop(0)
    o_res = refs.pop(0) if edges else None
    o_low = refs.pop(0) if edges else None
    near = refs.pop(0) if edges else None
    far = refs.pop(0) if edges and plan.multi else None
    o_conv, o_go, o_gl, o_sums, o_up_bias, feat_ref = refs
    rows, cols, channels = o_conv.shape
    count = rows * cols
    hidden = up.shape[2]

    @pl.when(plan.section(info) == section)
    def _():
        grad = grad_out[slot] if top else grad_out[...]
        grad_res = masked_rows(grad.astype(F32), 0, plan.limit(info, slot))
        if edges:
            o_res[...] = grad_res.astype(BF)
        flat = grad_res.reshape(count, channels)
        scaled = packed.scale() * flat
        sum_scale = jnp.sum(branch[...] * flat, axis=0, keepdims=True)
        sum_out = jnp.sum(scaled, axis=0, keepdims=True)
        go = scaled.astype(BF)
        o_go[...] = go
        feat_ref[...] = jnp.zeros((count, channels), F32)
        last_dims = (((1,), (1,)), ((), ()))

        def units(n, _):
            span = pl.ds(pl.multiple_of(n * CHUNK, CHUNK), CHUNK)
            grad_hidden = lax.dot_general(
                o_go[...], down[0, span, :], last_dims, preferred_element_type=F32
            )
            grad_pre = grad_hidden * slope[:, span].astype(F32)
            o_up_bias[:, span] = jnp.sum(grad_pre, axis=0, keepdims=True)
            low = grad_pre.astype(BF)
            o_gl[:, span] = low
            feat_ref[...] += lax.dot_general(
                low, up[0, :, span], last_dims, preferred_element_type=F32
            )
            return 0

        lax.fori_loop(0, hidden // CHUNK, units, 0, unroll=True)
        feat = feat_ref[...]
        normed = z[...].reshape(count, channels)
        sum_gain = jnp.sum(feat * normed, axis=0, keepdims=True)
        sum_norm = jnp.sum(feat, axis=0, keepdims=True)
        grad_normed = feat * packed.gain()
        inner = (
            grad_normed
            - jnp.mean(grad_normed, axis=-1, keepdims=True)
            - normed * jnp.mean(grad_normed * normed, axis=-1, keepdims=True)
        )
        for at in range(0, channels, LANES):
            lanes = slice(at, at + LANES)
            o_conv[:, :, lanes] = (rs[...] * inner[:, lanes]).reshape(rows, cols, LANES)
        grad_conv = o_conv[...]
        sum_conv = jnp.sum(grad_conv.reshape(count, channels), axis=0, keepdims=True)
        if edges:
            o_low[...] = grad_conv.astype(BF)
            pick_edge(plan.odd(info), o_low, near, far)
        blank = jnp.zeros((3, channels), F32)
        o_sums[...] = jnp.concatenate(
            [sum_conv, sum_norm, sum_out, sum_gain, sum_scale, blank], axis=0
        )


def spread_kernel(plan, section, slot, info, *refs):
    refs = list(refs)
    low, near = refs.pop(0), refs.pop(0)
    far = refs.pop(0) if plan.multi else None
    res, packed, out, field, total = refs
    rows = low.shape[0]

    @pl.when(plan.section(info) == section)
    def _():
        fill_field(
            field,
            low[...],
            near[...],
            None if far is None else far[...],
            plan.odd(info),
            rows + 3,
        )
        depthwise(field, packed, total, None, True)
        value = total[...] + res[...].astype(F32)
        out[...] = masked_rows(value, 0, plan.limit(info, slot)).astype(BF)


def taps_kernel(info, pad, conv, out):
    rows, cols, channels = conv.shape
    group = group_of(rows)
    out[49:, :] = jnp.zeros((out.shape[0] - 49, channels), F32)

    def across(n, _):
        lanes = pl.ds(pl.multiple_of(n * LANES, LANES), LANES)
        for j in range(7):

            def step(g, accs, j=j):
                part = pad[pl.ds(g * group, group + 6), :, lanes].astype(F32)
                grad = moved_cols(conv[pl.ds(g * group, group), :, lanes], 3 - j)
                return tuple(
                    acc
                    + jnp.sum(
                        (part[i : i + group] * grad).reshape(group * cols // 8, 8, LANES),
                        axis=0,
                    )
                    for i, acc in enumerate(accs)
                )

            zero = jnp.zeros((8, LANES), F32)
            accs = lax.fori_loop(0, rows // group, step, (zero,) * 7)
            for i in range(7):
                tap = i * 7 + j
                out[tap : tap + 1, lanes] = jnp.sum(accs[i], axis=0, keepdims=True)
        return 0

    lax.fori_loop(0, channels // LANES, across, 0)


def product_kernel(plan, wide_left, more, info, left, right, *refs):
    width = (left if wide_left else right).shape[-1] // 4
    first_dims = (((0,), (0,)), ((), ()))
    other = 2 * (1 - plan.odd(info))

    def term(block):
        span = pl.ds(pl.multiple_of((block + other) % 4 * width, LANES), width)
        total = lax.dot_general(
            left[:, span] if wide_left else left[...],
            right[...] if wide_left else right[:, span],
            first_dims,
            preferred_element_type=F32,
        )
        return total + refs[0][block] if more else total

    if len(refs) == 1 + more:
        for block in range(4):
            refs[-1][block] = term(block)
        return
    smalls, (theirs, mine) = refs[more:-2], refs[-2:]
    height = mine.shape[0]
    size = left.shape[-1] if not wide_left else width
    for block in range(4):
        out = mine if block // 2 else theirs
        out[block % 2 * size : (block % 2 + 1) * size] = term(block).astype(mine.dtype)
    if smalls:
        rest = height - 2 * size
        out_rows = slice(2 * size, height)
        rows = smalls[0].shape[0] // 2
        odd = plan.odd(info)
        blank = jnp.zeros((rest - rows, mine.shape[1]), F32)

        def half(at):
            start = pl.multiple_of(at * rows, 8)
            return jnp.concatenate([tree([v[pl.ds(start, rows)] for v in smalls]), blank], axis=0)

        mine[out_rows] = half(odd).astype(mine.dtype)
        theirs[out_rows] = half(1 - odd).astype(mine.dtype)


def gather_kernel(info, taps, sums, units, out):
    channels = out.shape[1]
    out[0:56] = taps[...]
    out[49:54] = sums[0:5]
    wide = units.shape[1] // channels
    for k in range(wide):
        out[54 + k : 55 + k] = units[:, k * channels : (k + 1) * channels]
    out[54 + wide :] = jnp.zeros((out.shape[0] - 54 - wide, channels), F32)


def merge_kernel(plan, info, mine, theirs, *refs):
    outs, total = refs[:-1], refs[-1]
    share = outs[0].shape[0]
    total[...] = mine[...].astype(F32) + theirs[...].astype(F32)
    for k, out in enumerate(outs):
        at = pl.multiple_of((plan.shard(info) ^ k) * share, 16)
        out[...] = total[pl.ds(at, share)].astype(BF)


def tree(values):
    while len(values) > 1:
        pairs = [a + b for a, b in zip(values[::2], values[1::2])]
        values = pairs + values[len(pairs) * 2 :]
    return values[0]


def pack_kernel(plan, section, info, *refs):
    edges, out = refs[:-1], refs[-1]
    rows = out.shape[0] - 3 * len(edges)

    @pl.when(plan.section(info) == section)
    def _():
        for k, edge in enumerate(edges):
            out[rows + 3 * k : rows + 3 * (k + 1)] = edge[...]


def finish_kernel(factor, info, *refs):
    refs[-1][...] = (tree([r[...].astype(F32) for r in refs[:-1]]) * factor).astype(BF)


def place_down_kernel(plan, shards, info, *refs):
    pieces, out = refs[:-1], refs[-1]
    share = pieces[0].shape[0]
    for side in range(2):
        base = (plan.odd(info) ^ side) * shards
        for k in range(shards):
            at = pl.multiple_of((base + (plan.shard(info) ^ k)) * share, 16)
            out[pl.ds(at, share)] = pieces[side * shards + k][...]


def place_up_kernel(plan, shards, info, *refs):
    pieces = refs[: 2 * shards]
    up, kern, bias, gain, scale, units, full = refs[2 * shards :]
    share = pieces[0].shape[0]
    channels = up.shape[0]
    for side in range(2):
        half = plan.odd(info) ^ side
        for k in range(shards):
            at = pl.multiple_of((plan.shard(info) ^ k) * share, 16)
            full[half, pl.ds(at, share)] = pieces[side * shards + k][...]
    for half in range(2):
        for block in range(2):
            lane = (2 * half + block) * channels
            up[:, lane : lane + channels] = full[half, block * channels : (block + 1) * channels]
    small = jnp.concatenate(
        [full[half, 2 * channels : 2 * channels + 32] for half in range(2)], axis=0
    ).astype(F32)
    kern[...] = small[0:49].astype(BF)
    bias[...] = small[49:52].astype(BF)
    gain[...] = small[52:53].astype(BF)
    scale[...] = small[53:54].astype(BF)
    for k in range(units.shape[1] // channels):
        units[:, k * channels : (k + 1) * channels] = small[54 + k : 55 + k].astype(BF)


def body(
    images, cotangent, order, heights, kernel, biases, gain, scale, up_weight, up_bias, down_weight
):
    sections = lax.axis_size("section")
    shards = lax.axis_size("dp")
    strips = lax.axis_size("rows")
    section_at = lax.axis_index("section")
    row_at = lax.axis_index("rows")
    shard_at = lax.axis_index("dp")
    multi = strips > 2
    slots, rows, cols, channels = images.shape
    hidden = up_weight.shape[2]
    count = rows * cols
    odd = row_at % 2
    plan = Plan(slots, rows, multi)
    here = jnp.stack([section_at, row_at, shard_at]).astype(jnp.int32)
    info = jnp.concatenate([order[0], heights, here])
    packed = jnp.concatenate([kernel[0], biases[0], gain, scale])

    row_pairs = [(i, i ^ 1) for i in range(strips)]
    straight = [(i, i) for i in range(strips)]
    beyond = [(i, i + 1) for i in range(1, strips - 1, 2)]
    beyond += [(b, a) for a, b in beyond]

    def carry(value, pairs, source, target):
        return lax.ppermute(
            value,
            ("section", "rows"),
            [(source * strips + a, target * strips + b) for a, b in pairs],
        )

    def halos_of(near, far, source, target):
        return [carry(near, row_pairs, source, target)] + (
            [carry(far, beyond, source, target)] if multi else []
        )

    last_rows, first_rows = images[:, rows - 3 :], images[:, :3]
    image_near = jnp.where(odd == 1, first_rows, last_rows)
    image_far = jnp.where(odd == 1, last_rows, first_rows) if multi else None
    image_halos = halos_of(image_near, image_far, 0, 0)

    strip_shape = (rows, cols, channels)
    field_shape = (rows + 6, cols, channels)
    strip_out = (strip_shape, BF)
    package_out = ((rows + (6 if multi else 3), cols, channels), BF)
    edge_outs = [((3, cols, channels), BF)] * (2 if multi else 1)

    kept_outs = [
        (field_shape, BF),
        (strip_shape, F32),
        ((count, LANES), F32),
        ((count, channels), BF),
        ((count, hidden), BF),
        ((count, hidden), BF),
        ((count, channels), F32),
    ]
    chain_outs = [
        (strip_shape, F32),
        ((count, channels), BF),
        ((count, hidden), BF),
        ((8, channels), F32),
        ((1, hidden), F32),
    ]
    kept = [[] for _ in range(slots)]
    chained = [[] for _ in range(slots)]
    moved = [[images] + image_halos] * slots
    incoming = [cotangent] * slots
    partial = [[], []]
    token = jnp.zeros(*TOKEN)

    def forward(section, slot):
        nonlocal token
        sends = section < sections - 1
        token, results = call(
            functools.partial(forward_kernel, plan, section, slot, sends),
            "forward",
            info,
            moved[slot] + [packed, up_bias, up_weight, down_weight],
            ([package_out] + edge_outs) * sends + kept_outs,
            token,
            keeps=kept[slot],
            scratch=[(field_shape, F32)],
        )
        kept[slot] = results[len(results) - len(kept_outs) :]
        if sends:
            halos = halos_of(results[1], results[2] if multi else None, section, section)
            token, package = call(
                functools.partial(pack_kernel, plan, section),
                "pack",
                info,
                halos,
                [package_out],
                token,
                keeps=[results[0]],
            )
            moved[slot] = [carry(package[0], straight, section, section + 1)]

    def backward(section, slot):
        nonlocal token
        edges = section > 0
        _, z, rs, _, _, slope, branch = kept[slot]
        token, results = call(
            functools.partial(chain_kernel, plan, section, slot, section == sections - 1, edges),
            "chain",
            info,
            [incoming[slot], z, rs, slope, branch, packed, up_weight, down_weight],
            ([strip_out] * 2 + edge_outs) * edges + chain_outs,
            token,
            keeps=chained[slot],
            scratch=[((count, channels), F32)],
        )
        chained[slot] = results[len(results) - len(chain_outs) :]
        if edges:
            halos = halos_of(results[2], results[3] if multi else None, section, section)
            token, (spread,) = call(
                functools.partial(spread_kernel, plan, section, slot),
                "spread",
                info,
                [results[1]] + halos + [results[0], packed],
                [strip_out],
                token,
                scratch=[(field_shape, F32), (strip_shape, F32)],
            )
            incoming[slot] = carry(spread, straight, section, section - 1)

    for section in range(sections - 1):
        for slot in range(slots):
            forward(section, slot)
    for slot in range(slots):
        forward(sections - 1, slot)
        backward(sections - 1, slot)
    for section in range(sections - 2, 0, -1):
        for slot in range(slots):
            backward(section, slot)
    factor = 1.0 / math.sqrt(shards * slots * strips * rows * cols)
    heights_of = [hidden // 2 + pad for pad in (0, 64)]
    partial = [[], []]
    smalls = []

    def product(at, slot):
        nonlocal token
        last = slot == slots - 1
        left, right = [
            (kept[slot][4], chained[slot][1]),
            (kept[slot][3], chained[slot][2]),
        ][at]
        extra = smalls if last and at == 1 else []
        outputs = [((4, channels, channels), F32)]
        if last:
            outputs = [((heights_of[at], channels), BF)] * 2
        token, partial[at] = call(
            functools.partial(product_kernel, plan, at == 0, len(partial[at])),
            "product",
            info,
            [left, right] + partial[at] + extra,
            outputs,
            token,
        )

    def small_terms(slot):
        nonlocal token
        conv, _, _, sums, units = chained[slot]
        token, (taps,) = call(
            taps_kernel, "taps", info, [kept[slot][0], conv], [((56, channels), F32)], token
        )
        token, (small,) = call(
            gather_kernel, "total", info, [taps, sums, units], [((64, channels), F32)], token
        )
        smalls.append(small)

    for slot in range(slots):
        backward(0, slot)
        product(0, slot)
        if slot < slots - 1:
            product(1, slot)
        small_terms(slot)

    def swap(value):
        return lax.ppermute(value, "rows", row_pairs)

    def peers(values):
        return [
            lax.ppermute(v, "dp", [(i, i ^ k) for i in range(shards)])
            for k, v in enumerate(values)
            if k
        ]

    def merged(at):
        nonlocal token
        theirs, mine = partial[at]
        share = heights_of[at] // shards
        token, pieces = call(
            functools.partial(merge_kernel, plan),
            "merge",
            info,
            [mine, swap(theirs)],
            [((share, channels), BF)] * shards,
            token,
            scratch=[((heights_of[at], channels), F32)],
        )
        return [pieces[0]] + peers(pieces)

    def finished(pieces):
        nonlocal token
        token, (own,) = call(
            functools.partial(finish_kernel, factor),
            "finish",
            info,
            pieces,
            [(pieces[0].shape, BF)],
            token,
        )
        half = [own] + peers([own] * shards)
        return half + [swap(v) for v in half]

    small_outs = [((49, channels), BF), ((3, channels), BF), ((1, channels), BF)]
    small_outs += [((1, channels), BF), ((1, hidden), BF)]
    if multi:
        product(1, slots - 1)
        sides = []
        for theirs, mine in partial:
            pair = jnp.where(odd == 1, jnp.stack([theirs, mine]), jnp.stack([mine, theirs]))
            sides.append(lax.psum(pair.astype(F32), ("rows", "dp")) * factor)
        down_grad = sides[0].reshape(hidden, channels).astype(BF)
        up_grad = sides[1][:, : 2 * channels].reshape(4, channels, channels)
        up_grad = up_grad.transpose(1, 0, 2).reshape(channels, hidden).astype(BF)
        small = sides[1][:, 2 * channels : 2 * channels + 32].reshape(64, channels).astype(BF)
        kern_grad, bias_grad, gain_grad, scale_grad = (
            small[:49], small[49:52], small[52:53], small[53:54]
        )
        unit_grad = small[54 : 54 + hidden // channels].reshape(1, hidden)
    else:
        first = merged(0)
        product(1, slots - 1)
        second = merged(1)
        down_half = finished(first)
        up_half = finished(second)
        token, (down_grad,) = call(
            functools.partial(place_down_kernel, plan, shards),
            "place",
            info,
            down_half,
            [((hidden, channels), BF)],
            token,
        )
        token, results = call(
            functools.partial(place_up_kernel, plan, shards),
            "place",
            info,
            up_half,
            [((channels, hidden), BF)] + small_outs,
            token,
            scratch=[((2, heights_of[1], channels), BF)],
        )
        up_grad, kern_grad, bias_grad, gain_grad, scale_grad, unit_grad = results
    return (
        kern_grad[None],
        bias_grad[None],
        gain_grad,
        scale_grad,
        up_grad[None],
        unit_grad,
        down_grad[None],
    )


def solution(mesh):
    in_specs = (
        P("dp", "rows", None, None),
        P("dp", "rows", None, None),
        P("dp", None),
        P("dp"),
        P("section", None, None),
        P("section", None, None),
        P("section", None),
        P("section", None),
        P("section", None, None),
        P("section", None),
        P("section", None, None),
    )
    out_specs = (
        P("section", None, None),
        P("section", None, None),
        P("section", None),
        P("section", None),
        P("section", None, None),
        P("section", None),
        P("section", None, None),
    )
    return jax.shard_map(body, mesh=mesh, in_specs=in_specs, out_specs=out_specs, check_vma=False)
```

```python
import functools
import math

import jax
import jax.numpy as jnp
from jax import lax
from jax.experimental import pallas as pl
from jax.experimental.pallas import tpu as pltpu
from jax.sharding import PartitionSpec as P

EPS = 1e-06
ROOT_HALF = 0.7071067811865476
INV_ROOT_TAU = 0.3989422804014327
BF = jnp.bfloat16
F32 = jnp.float32
LANES = 128
CHUNK = 512
VMEM_LIMIT = 20 * 1024 * 1024

IN_VMEM = pl.BlockSpec(memory_space=pltpu.VMEM)
IN_SMEM = pl.BlockSpec(memory_space=pltpu.SMEM)
ANYWHERE = pl.BlockSpec(memory_space=pl.ANY)
IN_HBM = pl.BlockSpec(memory_space=pltpu.HBM)


TOKEN = ((8, LANES), F32)


def call(kernel, name, info, operands, outputs, after, keeps=(), scratch=(), apart=(), flags=()):
    base = 2 + len(operands)
    outputs = [TOKEN] + list(outputs)
    lead = len(outputs) - len(keeps)

    def run(info, *refs):
        kernel(info, *refs[: len(operands)], *refs[len(operands) + 1 + len(keeps) + 1 :])

    results = pl.pallas_call(
        run,
        out_shape=[jax.ShapeDtypeStruct(*o) for o in outputs],
        in_specs=[IN_SMEM]
        + [IN_HBM if k in apart else IN_VMEM for k in range(len(operands))]
        + [ANYWHERE]
        + [IN_VMEM] * len(keeps),
        out_specs=[IN_VMEM] * len(outputs),
        scratch_shapes=[pltpu.VMEM(*s) for s in scratch] + list(flags),
        input_output_aliases={base + i: lead + i for i in range(len(keeps))},
        cost_estimate=pl.CostEstimate(
            flops=0, transcendentals=0, bytes_accessed=int(COST[name] * 3.69e6)
        ),
        compiler_params=pltpu.CompilerParams(vmem_limit_bytes=VMEM_LIMIT),
        name=name,
    )(info, *operands, after, *keeps)
    return results[0], list(results[1:])


COST = {
    "forward": 5.0, "pack": 1, "chain": 3.0, "spread": 3, "product": 2, "merge": 1, "taps": 4,
    "total": 1, "finish": 1, "place": 2,
}


class Plan:
    def __init__(self, slots, rows, multi):
        self.slots, self.rows, self.multi = slots, rows, multi

    def section(self, info):
        return info[2 * self.slots]

    def image(self, info, slot):
        return info[slot]

    def limit(self, info, slot):
        height = info[self.slots + info[slot]]
        return height - info[2 * self.slots + 1] * self.rows

    def odd(self, info):
        return info[2 * self.slots + 1] % 2

    def shard(self, info):
        return info[2 * self.slots + 2]


class Packed:
    def __init__(self, ref):
        self.ref = ref

    def bias(self, at):
        return self.ref[49 + at : 50 + at]

    def gain(self):
        return self.ref[52:53]

    def scale(self):
        return self.ref[53:54]


def group_of(rows):
    return next(g for g in (8, 6, 4, 3, 2, 1) if rows % g == 0)


def masked_rows(value, first, limit):
    row = lax.broadcasted_iota(jnp.int32, value.shape, 0) + first
    return jnp.where(row < limit, value, 0.0)


def moved_cols(value, steps):
    if steps == 0:
        return value
    cols = value.shape[1]
    col = lax.broadcasted_iota(jnp.int32, value.shape, 1)
    inside = col < cols - steps if steps > 0 else col >= -steps
    return jnp.where(inside, pltpu.roll(value, (-steps) % cols, 1), 0.0)


def fill_field(field, middle, near, far, odd, limit):
    rows = middle.shape[0]
    field[3 : 3 + rows] = masked_rows(middle.astype(F32), 0, limit)
    near = near.astype(F32)
    far = jnp.zeros(near.shape, F32) if far is None else far.astype(F32)

    @pl.when(odd == 1)
    def _():
        field[0:3] = masked_rows(near, -3, limit)
        field[rows + 3 :] = masked_rows(far, rows, limit)

    @pl.when(odd == 0)
    def _():
        field[0:3] = masked_rows(far, -3, limit)
        field[rows + 3 :] = masked_rows(near, rows, limit)


def depthwise(field, kern, out, bias, flip):
    rows, cols, channels = out.shape
    group = group_of(rows)
    groups = rows // group

    def step(n, _):
        g = n % groups
        lanes = pl.ds(pl.multiple_of(n // groups * LANES, LANES), LANES)
        part = field[pl.ds(g * group, group + 6), :, lanes]
        total = jnp.zeros((group, cols, LANES), F32)
        for j in range(7):
            acc = jnp.zeros((group, cols, LANES), F32)
            for i in range(7):
                tap = 48 - (i * 7 + j) if flip else i * 7 + j
                acc = acc + kern[tap : tap + 1, lanes][None] * part[i : i + group]
            total = total + moved_cols(acc, j - 3)
        if bias is not None:
            total = total + kern[bias : bias + 1, lanes][None]
        out[pl.ds(g * group, group), :, lanes] = total
        return 0

    lax.fori_loop(0, groups * (channels // LANES), step, 0)


def pick_edge(odd, value, near, far):
    rows = value.shape[0]

    @pl.when(odd == 1)
    def _():
        near[...] = value[0:3]
        if far is not None:
            far[...] = value[rows - 3 :]

    @pl.when(odd == 0)
    def _():
        near[...] = value[rows - 3 :]
        if far is not None:
            far[...] = value[0:3]


def forward_kernel(plan, section, slot, sends, cold, info, *refs):
    refs = list(refs)
    if section == 0:
        source = [refs.pop(0), refs.pop(0), refs.pop(0) if plan.multi else None]
    else:
        package = refs.pop(0)
    packed = Packed(refs.pop(0))
    up_bias, up, down = refs.pop(0), refs.pop(0), refs.pop(0)
    far_up, far_down, far_bias = up, down, up_bias
    outgoing = refs.pop(0) if sends else None
    near = refs.pop(0) if sends else None
    far = refs.pop(0) if sends and plan.multi else None
    o_pad, o_z, o_rs, o_n, o_h, o_slope, o_branch, field = refs[:8]
    fetches = []
    if section == 0:
        image, flag = refs[8], refs[-1]
        one = pltpu.make_async_copy(source[0].at[plan.image(info, slot)], image, flag.at[0])
    if cold:
        up, down, up_bias = refs[9:12]
        fetches = [
            pltpu.make_async_copy(far_up, up, flag.at[1]),
            pltpu.make_async_copy(far_down, down, flag.at[2]),
            pltpu.make_async_copy(far_bias, up_bias, flag.at[3]),
        ]
    rows, cols, channels = o_z.shape
    count = rows * cols
    hidden = up.shape[2]
    limit = plan.limit(info, slot)
    odd = plan.odd(info)

    @pl.when(plan.section(info) == section)
    def _():
        if section == 0:
            one.start()
        for fetch in fetches:
            fetch.start()
        if section == 0:
            at = plan.image(info, slot)
            one.wait()
            parts = [image[...]] + [None if v is None else v[at] for v in source[1:]]
        else:
            far_rows = package[rows + 3 :] if plan.multi else None
            parts = [package[0:rows], package[rows : rows + 3], far_rows]
        fill_field(field, *parts, odd, limit)
        o_pad[...] = field[...].astype(BF)
        depthwise(field, packed.ref, o_z, 49, False)
        conv = o_z[...].reshape(count, channels)
        centred = conv - jnp.mean(conv, axis=-1, keepdims=True)
        inv_std = lax.rsqrt(jnp.mean(centred * centred, axis=-1, keepdims=True) + EPS)
        normed = centred * inv_std
        o_z[...] = normed.reshape(rows, cols, channels)
        o_rs[...] = jnp.broadcast_to(inv_std, (count, LANES))
        features = (normed * packed.gain() + packed.bias(1)).astype(BF)
        o_n[...] = features
        o_branch[...] = jnp.broadcast_to(packed.bias(2), (count, channels))
        for fetch in fetches:
            fetch.wait()

        def units(n, _):
            span = pl.ds(pl.multiple_of(n * CHUNK, CHUNK), CHUNK)
            pre = jnp.dot(o_n[...], up[0, :, span], preferred_element_type=F32) + up_bias[:, span]
            bell = 1.0 + lax.erf(pre * ROOT_HALF)
            act = (0.5 * pre * bell).astype(BF)
            o_h[:, span] = act
            o_slope[:, span] = (
                0.5 * bell + pre * jnp.exp(-0.5 * pre * pre) * INV_ROOT_TAU
            ).astype(BF)
            o_branch[...] += jnp.dot(act, down[0, span, :], preferred_element_type=F32)
            return 0

        lax.fori_loop(0, hidden // CHUNK, units, 0, unroll=True)
        branch = o_branch[...]
        if sends:
            value = field[3 : 3 + rows] + (packed.scale() * branch).reshape(rows, cols, channels)
            outgoing[0:rows] = masked_rows(value, 0, limit).astype(BF)
            pick_edge(odd, outgoing.at[0:rows], near, far)


def chain_kernel(plan, section, slot, top, edges, info, *refs):
    refs = list(refs)
    grad_out, z, rs, slope, branch = (refs.pop(0) for _ in range(5))
    packed = Packed(refs.pop(0))
    up, down = refs.pop(0), refs.pop(0)
    o_res = refs.pop(0) if edges else None
    o_low = refs.pop(0) if edges else None
    near = refs.pop(0) if edges else None
    far = refs.pop(0) if edges and plan.multi else None
    o_conv, o_go, o_gl, o_sums, o_up_bias, feat_ref = refs
    rows, cols, channels = o_conv.shape
    count = rows * cols
    hidden = up.shape[2]

    @pl.when(plan.section(info) == section)
    def _():
        grad = grad_out[slot] if top else grad_out[...]
        grad_res = masked_rows(grad.astype(F32), 0, plan.limit(info, slot))
        if edges:
            o_res[...] = grad_res.astype(BF)
        flat = grad_res.reshape(count, channels)
        scaled = packed.scale() * flat
        sum_scale = jnp.sum(branch[...] * flat, axis=0, keepdims=True)
        sum_out = jnp.sum(scaled, axis=0, keepdims=True)
        go = scaled.astype(BF)
        o_go[...] = go
        feat_ref[...] = jnp.zeros((count, channels), F32)
        last_dims = (((1,), (1,)), ((), ()))

        def units(n, _):
            span = pl.ds(pl.multiple_of(n * CHUNK, CHUNK), CHUNK)
            grad_hidden = lax.dot_general(
                o_go[...], down[0, span, :], last_dims, preferred_element_type=F32
            )
            grad_pre = grad_hidden * slope[:, span].astype(F32)
            o_up_bias[:, span] = jnp.sum(grad_pre, axis=0, keepdims=True)
            low = grad_pre.astype(BF)
            o_gl[:, span] = low
            feat_ref[...] += lax.dot_general(
                low, up[0, :, span], last_dims, preferred_element_type=F32
            )
            return 0

        lax.fori_loop(0, hidden // CHUNK, units, 0, unroll=True)
        feat = feat_ref[...]
        normed = z[...].reshape(count, channels)
        sum_gain = jnp.sum(feat * normed, axis=0, keepdims=True)
        sum_norm = jnp.sum(feat, axis=0, keepdims=True)
        grad_normed = feat * packed.gain()
        inner = (
            grad_normed
            - jnp.mean(grad_normed, axis=-1, keepdims=True)
            - normed * jnp.mean(grad_normed * normed, axis=-1, keepdims=True)
        )
        for at in range(0, channels, LANES):
            lanes = slice(at, at + LANES)
            o_conv[:, :, lanes] = (rs[...] * inner[:, lanes]).reshape(rows, cols, LANES)
        grad_conv = o_conv[...]
        sum_conv = jnp.sum(grad_conv.reshape(count, channels), axis=0, keepdims=True)
        if edges:
            o_low[...] = grad_conv.astype(BF)
            pick_edge(plan.odd(info), o_low, near, far)
        blank = jnp.zeros((3, channels), F32)
        o_sums[...] = jnp.concatenate(
            [sum_conv, sum_norm, sum_out, sum_gain, sum_scale, blank], axis=0
        )


def spread_kernel(plan, section, slot, info, *refs):
    refs = list(refs)
    low, near = refs.pop(0), refs.pop(0)
    far = refs.pop(0) if plan.multi else None
    res, packed, out, field, total = refs
    rows = low.shape[0]

    @pl.when(plan.section(info) == section)
    def _():
        fill_field(
            field,
            low[...],
            near[...],
            None if far is None else far[...],
            plan.odd(info),
            rows + 3,
        )
        depthwise(field, packed, total, None, True)
        value = total[...] + res[...].astype(F32)
        out[...] = masked_rows(value, 0, plan.limit(info, slot)).astype(BF)


def taps_kernel(info, pad, conv, out, field):
    rows, cols, channels = conv.shape
    group = group_of(rows)
    out[49:, :] = jnp.zeros((out.shape[0] - 49, channels), F32)
    field[...] = pad[...].astype(F32)

    def across(n, _):
        lanes = pl.ds(pl.multiple_of(n * LANES, LANES), LANES)
        for j in range(7):

            def step(g, accs, j=j):
                part = field[pl.ds(g * group, group + 6), :, lanes]
                grad = moved_cols(conv[pl.ds(g * group, group), :, lanes], 3 - j)
                return tuple(
                    acc
                    + jnp.sum(
                        (part[i : i + group] * grad).reshape(group * cols // 8, 8, LANES),
                        axis=0,
                    )
                    for i, acc in enumerate(accs)
                )

            zero = jnp.zeros((8, LANES), F32)
            accs = lax.fori_loop(0, rows // group, step, (zero,) * 7)
            for i in range(7):
                tap = i * 7 + j
                out[tap : tap + 1, lanes] = jnp.sum(accs[i], axis=0, keepdims=True)
        return 0

    lax.fori_loop(0, channels // LANES, across, 0)


def product_kernel(plan, wide_left, more, last, info, left, right, *refs):
    width = (left if wide_left else right).shape[-1] // 4
    size = width if wide_left else left.shape[-1]
    first_dims = (((0,), (0,)), ((), ()))
    odd = plan.odd(info)
    smalls, (theirs, mine) = refs[more:-2], refs[-2:]
    for block in range(4):
        at = pl.multiple_of((block + 2 * (1 - odd)) % 4 * width, LANES)
        span = pl.ds(at, width)
        total = lax.dot_general(
            left[:, span] if wide_left else left[...],
            right[...] if wide_left else right[:, span],
            first_dims,
            preferred_element_type=F32,
        )
        rows = slice(block % 2 * size, (block % 2 + 1) * size)
        out, at = (theirs, 0) if block < 2 else (mine, more - 1)
        if more and (more == 2 or block >= 2):
            total = total + refs[at][rows]
        out[rows] = total.astype(out.dtype)
    if last and smalls:
        rows = smalls[0].shape[0] // 2
        blank = jnp.zeros((mine.shape[0] - 2 * size - rows, mine.shape[1]), F32)

        def half(at):
            start = pl.multiple_of(at * rows, 8)
            return jnp.concatenate([tree([v[pl.ds(start, rows)] for v in smalls]), blank], axis=0)

        mine[2 * size :] = half(odd).astype(mine.dtype)
        theirs[2 * size :] = half(1 - odd).astype(mine.dtype)


def add_kernel(info, mine, theirs, out):
    out[...] = mine[...] + theirs[...].astype(F32)


def gather_kernel(info, taps, sums, units, out):
    channels = out.shape[1]
    out[0:56] = taps[...]
    out[49:54] = sums[0:5]
    wide = units.shape[1] // channels
    for k in range(wide):
        out[54 + k : 55 + k] = units[:, k * channels : (k + 1) * channels]
    out[54 + wide :] = jnp.zeros((out.shape[0] - 54 - wide, channels), F32)


def merge_kernel(plan, info, mine, theirs, *refs):
    outs, total = refs[:-1], refs[-1]
    share = outs[0].shape[0]
    total[...] = mine[...].astype(F32) + theirs[...].astype(F32)
    for k, out in enumerate(outs):
        at = pl.multiple_of((plan.shard(info) ^ k) * share, 16)
        out[...] = total[pl.ds(at, share)].astype(BF)


def tree(values):
    while len(values) > 1:
        pairs = [a + b for a, b in zip(values[::2], values[1::2])]
        values = pairs + values[len(pairs) * 2 :]
    return values[0]


def pack_kernel(plan, section, info, *refs):
    edges, out = refs[:-1], refs[-1]
    rows = out.shape[0] - 3 * len(edges)

    @pl.when(plan.section(info) == section)
    def _():
        for k, edge in enumerate(edges):
            out[rows + 3 * k : rows + 3 * (k + 1)] = edge[...]


def finish_kernel(factor, info, *refs):
    refs[-1][...] = (tree([r[...].astype(F32) for r in refs[:-1]]) * factor).astype(BF)


def place_down_kernel(plan, shards, info, *refs):
    pieces, out = refs[:-1], refs[-1]
    share = pieces[0].shape[0]
    for side in range(2):
        base = (plan.odd(info) ^ side) * shards
        for k in range(shards):
            at = pl.multiple_of((base + (plan.shard(info) ^ k)) * share, 16)
            out[pl.ds(at, share)] = pieces[side * shards + k][...]


def place_up_kernel(plan, shards, info, *refs):
    pieces = refs[: 2 * shards]
    up, kern, bias, gain, scale, units, full = refs[2 * shards :]
    share = pieces[0].shape[0]
    channels = up.shape[0]
    for side in range(2):
        half = plan.odd(info) ^ side
        for k in range(shards):
            at = pl.multiple_of((plan.shard(info) ^ k) * share, 16)
            full[half, pl.ds(at, share)] = pieces[side * shards + k][...]
    for half in range(2):
        for block in range(2):
            lane = (2 * half + block) * channels
            up[:, lane : lane + channels] = full[half, block * channels : (block + 1) * channels]
    small = jnp.concatenate(
        [full[half, 2 * channels : 2 * channels + 32] for half in range(2)], axis=0
    ).astype(F32)
    kern[...] = small[0:49].astype(BF)
    bias[...] = small[49:52].astype(BF)
    gain[...] = small[52:53].astype(BF)
    scale[...] = small[53:54].astype(BF)
    for k in range(units.shape[1] // channels):
        units[:, k * channels : (k + 1) * channels] = small[54 + k : 55 + k].astype(BF)


def body(
    images, cotangent, order, heights, kernel, biases, gain, scale, up_weight, up_bias, down_weight
):
    sections = lax.axis_size("section")
    shards = lax.axis_size("dp")
    strips = lax.axis_size("rows")
    section_at = lax.axis_index("section")
    row_at = lax.axis_index("rows")
    shard_at = lax.axis_index("dp")
    multi = strips > 2
    slots, rows, cols, channels = images.shape
    hidden = up_weight.shape[2]
    count = rows * cols
    odd = row_at % 2
    plan = Plan(slots, rows, multi)
    here = jnp.stack([section_at, row_at, shard_at]).astype(jnp.int32)
    info = jnp.concatenate([order[0], heights, here])
    packed = jnp.concatenate([kernel[0], biases[0], gain, scale])

    row_pairs = [(i, i ^ 1) for i in range(strips)]
    straight = [(i, i) for i in range(strips)]
    beyond = [(i, i + 1) for i in range(1, strips - 1, 2)]
    beyond += [(b, a) for a, b in beyond]

    def carry(value, pairs, source, target):
        return lax.ppermute(
            value,
            ("section", "rows"),
            [(source * strips + a, target * strips + b) for a, b in pairs],
        )

    def halos_of(near, far, source, target):
        return [carry(near, row_pairs, source, target)] + (
            [carry(far, beyond, source, target)] if multi else []
        )

    last_rows, first_rows = images[:, rows - 3 :], images[:, :3]
    image_near = jnp.where(odd == 1, first_rows, last_rows)
    image_far = jnp.where(odd == 1, last_rows, first_rows) if multi else None
    image_halos = halos_of(image_near, image_far, 0, 0)

    strip_shape = (rows, cols, channels)
    field_shape = (rows + 6, cols, channels)
    strip_out = (strip_shape, BF)
    package_out = ((rows + (6 if multi else 3), cols, channels), BF)
    edge_outs = [((3, cols, channels), BF)] * (2 if multi else 1)

    kept_outs = [
        (field_shape, BF),
        (strip_shape, F32),
        ((count, LANES), F32),
        ((count, channels), BF),
        ((count, hidden), BF),
        ((count, hidden), BF),
        ((count, channels), F32),
    ]
    chain_outs = [
        (strip_shape, F32),
        ((count, channels), BF),
        ((count, hidden), BF),
        ((8, channels), F32),
        ((1, hidden), F32),
    ]
    kept = [[] for _ in range(slots)]
    chained = [[] for _ in range(slots)]
    moved = [[images] + image_halos] * slots
    incoming = [cotangent] * slots
    partial = [[], []]
    token = jnp.zeros(*TOKEN)

    def forward(section, slot):
        nonlocal token
        sends = section < sections - 1
        cold = section == 0 and slot == 0
        operands = moved[slot] + [packed, up_bias, up_weight, down_weight]
        places = [0] * (section == 0) + [len(operands) - k for k in (1, 2, 3)] * cold
        for k in places:
            operands[k] = pltpu.with_memory_space_constraint(operands[k], pltpu.HBM)
        fetched = [(strip_shape, BF)] * (section == 0)
        fetched += [(v.shape, v.dtype) for v in (up_weight, down_weight, up_bias)] * cold
        token, results = call(
            functools.partial(forward_kernel, plan, section, slot, sends, cold),
            "forward",
            info,
            operands,
            ([package_out] + edge_outs) * sends + kept_outs,
            token,
            keeps=kept[slot],
            scratch=[(field_shape, F32)] + fetched,
            apart=places,
            flags=[pltpu.SemaphoreType.DMA((4,))] * (section == 0),
        )
        kept[slot] = results[len(results) - len(kept_outs) :]
        if sends:
            halos = halos_of(results[1], results[2] if multi else None, section, section)
            token, package = call(
                functools.partial(pack_kernel, plan, section),
                "pack",
                info,
                halos,
                [package_out],
                token,
                keeps=[results[0]],
            )
            moved[slot] = [carry(package[0], straight, section, section + 1)]

    def backward(section, slot):
        nonlocal token
        edges = section > 0
        _, z, rs, _, _, slope, branch = kept[slot]
        token, results = call(
            functools.partial(chain_kernel, plan, section, slot, section == sections - 1, edges),
            "chain",
            info,
            [incoming[slot], z, rs, slope, branch, packed, up_weight, down_weight],
            ([strip_out] * 2 + edge_outs) * edges + chain_outs,
            token,
            keeps=chained[slot],
            scratch=[((count, channels), F32)],
        )
        chained[slot] = results[len(results) - len(chain_outs) :]
        if edges:
            halos = halos_of(results[2], results[3] if multi else None, section, section)
            token, (spread,) = call(
                functools.partial(spread_kernel, plan, section, slot),
                "spread",
                info,
                [results[1]] + halos + [results[0], packed],
                [strip_out],
                token,
                scratch=[(field_shape, F32), (strip_shape, F32)],
            )
            incoming[slot] = carry(spread, straight, section, section - 1)

    for section in range(sections - 1):
        for slot in range(slots):
            forward(section, slot)
    for slot in range(slots):
        forward(sections - 1, slot)
        backward(sections - 1, slot)
    for section in range(sections - 2, 0, -1):
        for slot in range(slots):
            backward(section, slot)
    factor = 1.0 / math.sqrt(shards * slots * strips * rows * cols)
    heights_of = [hidden // 2 + pad for pad in (0, 64)]
    partial = [[], []]
    earlier = [[], []]
    smalls = []

    def swap(value):
        return lax.ppermute(value, "rows", row_pairs)

    def product(at, slot):
        nonlocal token
        last = slot == slots - 1
        left, right = [
            (kept[slot][4], chained[slot][1]),
            (kept[slot][3], chained[slot][2]),
        ][at]
        extra = smalls if last and at == 1 else []
        older = partial[at] if at == 1 else partial[at][1:]
        outputs = [((hidden // 2, channels), F32 if at == 1 else BF), ((hidden // 2, channels), F32)]
        if last:
            outputs = [((heights_of[at], channels), BF)] * 2
        token, (theirs, mine) = call(
            functools.partial(product_kernel, plan, at == 0, len(older), last),
            "product",
            info,
            [left, right] + older + extra,
            outputs,
            token,
        )
        partial[at] = [theirs, mine]

    def collect(at):
        nonlocal token
        theirs, mine = partial[at]
        earlier[at].append(theirs)
        if not multi:
            token, (mine,) = call(
                add_kernel,
                "total",
                info,
                [mine, swap(theirs)],
                [((hidden // 2, channels), F32)],
                token,
            )
        partial[at] = [theirs, mine]

    def small_terms(slot):
        nonlocal token
        conv, _, _, sums, units = chained[slot]
        token, (taps,) = call(
            taps_kernel,
            "taps",
            info,
            [kept[slot][0], conv],
            [((56, channels), F32)],
            token,
            scratch=[(field_shape, F32)],
        )
        token, (small,) = call(
            gather_kernel, "total", info, [taps, sums, units], [((64, channels), F32)], token
        )
        smalls.append(small)

    for slot in range(slots):
        backward(0, slot)
        product(0, slot)
        if slot < slots - 1:
            product(1, slot)
        small_terms(slot)
        if slot < slots - 1:
            collect(0)

    def peers(values):
        return [
            lax.ppermute(v, "dp", [(i, i ^ k) for i in range(shards)])
            for k, v in enumerate(values)
            if k
        ]

    def merged(at):
        nonlocal token
        theirs, mine = partial[at]
        share = heights_of[at] // shards
        token, pieces = call(
            functools.partial(merge_kernel, plan),
            "merge",
            info,
            [mine, swap(theirs)],
            [((share, channels), BF)] * shards,
            token,
            scratch=[((heights_of[at], channels), F32)],
        )
        return [pieces[0]] + peers(pieces)

    def finished(pieces):
        nonlocal token
        token, (own,) = call(
            functools.partial(finish_kernel, factor),
            "finish",
            info,
            pieces,
            [(pieces[0].shape, BF)],
            token,
        )
        half = [own] + peers([own] * shards)
        return half + [swap(v) for v in half]

    small_outs = [((49, channels), BF), ((3, channels), BF), ((1, channels), BF)]
    small_outs += [((1, channels), BF), ((1, hidden), BF)]
    if multi:
        product(1, slots - 1)
        sides = []
        for at, (theirs, mine) in enumerate(partial):
            for term in earlier[at]:
                theirs = theirs.at[: hidden // 2].add(term)
            pair = jnp.where(odd == 1, jnp.stack([theirs, mine]), jnp.stack([mine, theirs]))
            sides.append(lax.psum(pair.astype(F32), ("rows", "dp")) * factor)
        down_grad = sides[0].reshape(hidden, channels).astype(BF)
        up_grad = sides[1][:, : 2 * channels].reshape(4, channels, channels)
        up_grad = up_grad.transpose(1, 0, 2).reshape(channels, hidden).astype(BF)
        small = sides[1][:, 2 * channels : 2 * channels + 32].reshape(64, channels).astype(BF)
        kern_grad, bias_grad, gain_grad, scale_grad = (
            small[:49], small[49:52], small[52:53], small[53:54]
        )
        unit_grad = small[54 : 54 + hidden // channels].reshape(1, hidden)
    else:
        first = merged(0)
        product(1, slots - 1)
        second = merged(1)
        down_half = finished(first)
        up_half = finished(second)
        token, (down_grad,) = call(
            functools.partial(place_down_kernel, plan, shards),
            "place",
            info,
            down_half,
            [((hidden, channels), BF)],
            token,
        )
        token, results = call(
            functools.partial(place_up_kernel, plan, shards),
            "place",
            info,
            up_half,
            [((channels, hidden), BF)] + small_outs,
            token,
            scratch=[((2, heights_of[1], channels), BF)],
        )
        up_grad, kern_grad, bias_grad, gain_grad, scale_grad, unit_grad = results
    return (
        kern_grad[None],
        bias_grad[None],
        gain_grad,
        scale_grad,
        up_grad[None],
        unit_grad,
        down_grad[None],
    )


def solution(mesh):
    in_specs = (
        P("dp", "rows", None, None),
        P("dp", "rows", None, None),
        P("dp", None),
        P("dp"),
        P("section", None, None),
        P("section", None, None),
        P("section", None),
        P("section", None),
        P("section", None, None),
        P("section", None),
        P("section", None, None),
    )
    out_specs = (
        P("section", None, None),
        P("section", None, None),
        P("section", None),
        P("section", None),
        P("section", None, None),
        P("section", None),
        P("section", None, None),
    )
    return jax.shard_map(body, mesh=mesh, in_specs=in_specs, out_specs=out_specs, check_vma=False)
```

```python
import functools
import math

import jax
import jax.numpy as jnp
from jax import lax
from jax.experimental import pallas as pl
from jax.experimental.pallas import tpu as pltpu
from jax.sharding import PartitionSpec as P

EPS = 1e-06
ROOT_HALF = 0.7071067811865476
INV_ROOT_TAU = 0.3989422804014327
BF = jnp.bfloat16
F32 = jnp.float32
LANES = 128
CHUNK = 768
VMEM_LIMIT = 20 * 1024 * 1024

IN_VMEM = pl.BlockSpec(memory_space=pltpu.VMEM)
IN_SMEM = pl.BlockSpec(memory_space=pltpu.SMEM)
ANYWHERE = pl.BlockSpec(memory_space=pl.ANY)
IN_HBM = pl.BlockSpec(memory_space=pltpu.HBM)


TOKEN = ((8, LANES), F32)


def call(kernel, name, info, operands, outputs, after, keeps=(), scratch=(), apart=(), flags=()):
    base = 2 + len(operands)
    outputs = [TOKEN] + list(outputs)
    lead = len(outputs) - len(keeps)

    def run(info, *refs):
        kernel(info, *refs[: len(operands)], *refs[len(operands) + 1 + len(keeps) + 1 :])

    results = pl.pallas_call(
        run,
        out_shape=[jax.ShapeDtypeStruct(*o) for o in outputs],
        in_specs=[IN_SMEM]
        + [IN_HBM if k in apart else IN_VMEM for k in range(len(operands))]
        + [ANYWHERE]
        + [IN_VMEM] * len(keeps),
        out_specs=[IN_VMEM] * len(outputs),
        scratch_shapes=[pltpu.VMEM(*s) for s in scratch] + list(flags),
        input_output_aliases={base + i: lead + i for i in range(len(keeps))},
        cost_estimate=pl.CostEstimate(
            flops=0, transcendentals=0, bytes_accessed=int(COST[name] * 3.69e6)
        ),
        compiler_params=pltpu.CompilerParams(vmem_limit_bytes=VMEM_LIMIT),
        name=name,
    )(info, *operands, after, *keeps)
    return results[0], list(results[1:])


COST = {
    "forward": 5.0, "pack": 1, "chain": 3.0, "spread": 3, "product": 2, "merge": 1, "taps": 4,
    "total": 1, "finish": 1, "place": 2,
}


class Plan:
    def __init__(self, slots, rows, multi):
        self.slots, self.rows, self.multi = slots, rows, multi

    def section(self, info):
        return info[2 * self.slots]

    def image(self, info, slot):
        return info[slot]

    def limit(self, info, slot):
        height = info[self.slots + info[slot]]
        return height - info[2 * self.slots + 1] * self.rows

    def odd(self, info):
        return info[2 * self.slots + 1] % 2

    def shard(self, info):
        return info[2 * self.slots + 2]


class Packed:
    def __init__(self, ref):
        self.ref = ref

    def bias(self, at):
        return self.ref[49 + at : 50 + at]

    def gain(self):
        return self.ref[52:53]

    def scale(self):
        return self.ref[53:54]


def group_of(rows):
    return next(g for g in (8, 6, 4, 3, 2, 1) if rows % g == 0)


def masked_rows(value, first, limit):
    row = lax.broadcasted_iota(jnp.int32, value.shape, 0) + first
    return jnp.where(row < limit, value, 0.0)


def moved_cols(value, steps):
    if steps == 0:
        return value
    cols = value.shape[1]
    col = lax.broadcasted_iota(jnp.int32, value.shape, 1)
    inside = col < cols - steps if steps > 0 else col >= -steps
    return jnp.where(inside, pltpu.roll(value, (-steps) % cols, 1), 0.0)


def fill_field(field, middle, near, far, odd, limit):
    rows = middle.shape[0]
    field[3 : 3 + rows] = masked_rows(middle.astype(F32), 0, limit)
    near = near.astype(F32)
    far = jnp.zeros(near.shape, F32) if far is None else far.astype(F32)

    @pl.when(odd == 1)
    def _():
        field[0:3] = masked_rows(near, -3, limit)
        field[rows + 3 :] = masked_rows(far, rows, limit)

    @pl.when(odd == 0)
    def _():
        field[0:3] = masked_rows(far, -3, limit)
        field[rows + 3 :] = masked_rows(near, rows, limit)


def depthwise(field, kern, out, bias, flip):
    rows, cols, channels = out.shape
    group = group_of(rows)
    groups = rows // group

    def step(n, _):
        g = n % groups
        lanes = pl.ds(pl.multiple_of(n // groups * LANES, LANES), LANES)
        part = field[pl.ds(g * group, group + 6), :, lanes]
        total = jnp.zeros((group, cols, LANES), F32)
        for j in range(7):
            acc = jnp.zeros((group, cols, LANES), F32)
            for i in range(7):
                tap = 48 - (i * 7 + j) if flip else i * 7 + j
                acc = acc + kern[tap : tap + 1, lanes][None] * part[i : i + group]
            total = total + moved_cols(acc, j - 3)
        if bias is not None:
            total = total + kern[bias : bias + 1, lanes][None]
        out[pl.ds(g * group, group), :, lanes] = total
        return 0

    lax.fori_loop(0, groups * (channels // LANES), step, 0)


def pick_edge(odd, value, near, far):
    rows = value.shape[0]

    @pl.when(odd == 1)
    def _():
        near[...] = value[0:3]
        if far is not None:
            far[...] = value[rows - 3 :]

    @pl.when(odd == 0)
    def _():
        near[...] = value[rows - 3 :]
        if far is not None:
            far[...] = value[0:3]


def forward_kernel(plan, section, slot, sends, cold, info, *refs):
    refs = list(refs)
    if section == 0:
        source = [refs.pop(0), refs.pop(0), refs.pop(0) if plan.multi else None]
    else:
        package = refs.pop(0)
    packed = Packed(refs.pop(0))
    up_bias, up, down = refs.pop(0), refs.pop(0), refs.pop(0)
    far_up, far_down, far_bias = up, down, up_bias
    outgoing = refs.pop(0) if sends else None
    near = refs.pop(0) if sends else None
    far = refs.pop(0) if sends and plan.multi else None
    o_pad, o_z, o_rs, o_n, o_h, o_slope, o_branch, field = refs[:8]
    fetches = []
    if section == 0:
        image, flag = refs[8], refs[-1]
        one = pltpu.make_async_copy(source[0].at[plan.image(info, slot)], image, flag.at[0])
    if cold:
        up, down, up_bias = refs[9:12]
        fetches = [
            pltpu.make_async_copy(far_up, up, flag.at[1]),
            pltpu.make_async_copy(far_down, down, flag.at[2]),
            pltpu.make_async_copy(far_bias, up_bias, flag.at[3]),
        ]
    rows, cols, channels = o_z.shape
    count = rows * cols
    hidden = up.shape[2]
    limit = plan.limit(info, slot)
    odd = plan.odd(info)

    @pl.when(plan.section(info) == section)
    def _():
        if section == 0:
            one.start()
        for fetch in fetches:
            fetch.start()
        if section == 0:
            at = plan.image(info, slot)
            one.wait()
            parts = [image[...]] + [None if v is None else v[at] for v in source[1:]]
        else:
            far_rows = package[rows + 3 :] if plan.multi else None
            parts = [package[0:rows], package[rows : rows + 3], far_rows]
        fill_field(field, *parts, odd, limit)
        o_pad[...] = field[...].astype(BF)
        depthwise(field, packed.ref, o_z, 49, False)
        conv = o_z[...].reshape(count, channels)
        centred = conv - jnp.mean(conv, axis=-1, keepdims=True)
        inv_std = lax.rsqrt(jnp.mean(centred * centred, axis=-1, keepdims=True) + EPS)
        normed = centred * inv_std
        o_z[...] = normed.reshape(rows, cols, channels)
        o_rs[...] = jnp.broadcast_to(inv_std, (count, LANES))
        features = (normed * packed.gain() + packed.bias(1)).astype(BF)
        o_n[...] = features
        o_branch[...] = jnp.broadcast_to(packed.bias(2), (count, channels))
        for fetch in fetches:
            fetch.wait()

        def units(n, _):
            span = pl.ds(pl.multiple_of(n * CHUNK, CHUNK), CHUNK)
            pre = jnp.dot(o_n[...], up[0, :, span], preferred_element_type=F32) + up_bias[:, span]
            bell = 1.0 + lax.erf(pre * ROOT_HALF)
            act = (0.5 * pre * bell).astype(BF)
            o_h[:, span] = act
            o_slope[:, span] = (
                0.5 * bell + pre * jnp.exp(-0.5 * pre * pre) * INV_ROOT_TAU
            ).astype(BF)
            o_branch[...] += jnp.dot(act, down[0, span, :], preferred_element_type=F32)
            return 0

        lax.fori_loop(0, hidden // CHUNK, units, 0, unroll=True)
        branch = o_branch[...]
        if sends:
            value = field[3 : 3 + rows] + (packed.scale() * branch).reshape(rows, cols, channels)
            outgoing[0:rows] = masked_rows(value, 0, limit).astype(BF)
            pick_edge(odd, outgoing.at[0:rows], near, far)


def chain_kernel(plan, section, slot, top, edges, info, *refs):
    refs = list(refs)
    grad_out, z, rs, slope, branch = (refs.pop(0) for _ in range(5))
    packed = Packed(refs.pop(0))
    up, down = refs.pop(0), refs.pop(0)
    o_res = refs.pop(0) if edges else None
    o_low = refs.pop(0) if edges else None
    near = refs.pop(0) if edges else None
    far = refs.pop(0) if edges and plan.multi else None
    o_conv, o_go, o_gl, o_sums, o_up_bias, feat_ref = refs
    rows, cols, channels = o_conv.shape
    count = rows * cols
    hidden = up.shape[2]

    @pl.when(plan.section(info) == section)
    def _():
        grad = grad_out[slot] if top else grad_out[...]
        grad_res = masked_rows(grad.astype(F32), 0, plan.limit(info, slot))
        if edges:
            o_res[...] = grad_res.astype(BF)
        flat = grad_res.reshape(count, channels)
        scaled = packed.scale() * flat
        sum_scale = jnp.sum(branch[...] * flat, axis=0, keepdims=True)
        sum_out = jnp.sum(scaled, axis=0, keepdims=True)
        go = scaled.astype(BF)
        o_go[...] = go
        feat_ref[...] = jnp.zeros((count, channels), F32)
        last_dims = (((1,), (1,)), ((), ()))

        def units(n, _):
            span = pl.ds(pl.multiple_of(n * CHUNK, CHUNK), CHUNK)
            grad_hidden = lax.dot_general(
                o_go[...], down[0, span, :], last_dims, preferred_element_type=F32
            )
            grad_pre = grad_hidden * slope[:, span].astype(F32)
            o_up_bias[:, span] = jnp.sum(grad_pre, axis=0, keepdims=True)
            low = grad_pre.astype(BF)
            o_gl[:, span] = low
            feat_ref[...] += lax.dot_general(
                low, up[0, :, span], last_dims, preferred_element_type=F32
            )
            return 0

        lax.fori_loop(0, hidden // CHUNK, units, 0, unroll=True)
        feat = feat_ref[...]
        normed = z[...].reshape(count, channels)
        sum_gain = jnp.sum(feat * normed, axis=0, keepdims=True)
        sum_norm = jnp.sum(feat, axis=0, keepdims=True)
        grad_normed = feat * packed.gain()
        inner = (
            grad_normed
            - jnp.mean(grad_normed, axis=-1, keepdims=True)
            - normed * jnp.mean(grad_normed * normed, axis=-1, keepdims=True)
        )
        for at in range(0, channels, LANES):
            lanes = slice(at, at + LANES)
            o_conv[:, :, lanes] = (rs[...] * inner[:, lanes]).reshape(rows, cols, LANES)
        grad_conv = o_conv[...]
        sum_conv = jnp.sum(grad_conv.reshape(count, channels), axis=0, keepdims=True)
        if edges:
            o_low[...] = grad_conv.astype(BF)
            pick_edge(plan.odd(info), o_low, near, far)
        blank = jnp.zeros((3, channels), F32)
        o_sums[...] = jnp.concatenate(
            [sum_conv, sum_norm, sum_out, sum_gain, sum_scale, blank], axis=0
        )


def spread_kernel(plan, section, slot, info, *refs):
    refs = list(refs)
    low, near = refs.pop(0), refs.pop(0)
    far = refs.pop(0) if plan.multi else None
    res, packed, out, field, total = refs
    rows = low.shape[0]

    @pl.when(plan.section(info) == section)
    def _():
        fill_field(
            field,
            low[...],
            near[...],
            None if far is None else far[...],
            plan.odd(info),
            rows + 3,
        )
        depthwise(field, packed, total, None, True)
        value = total[...] + res[...].astype(F32)
        out[...] = masked_rows(value, 0, plan.limit(info, slot)).astype(BF)


def taps_kernel(info, pad, conv, out, field):
    rows, cols, channels = conv.shape
    group = group_of(rows)
    out[49:, :] = jnp.zeros((out.shape[0] - 49, channels), F32)
    field[...] = pad[...].astype(F32)

    def across(n, _):
        lanes = pl.ds(pl.multiple_of(n * LANES, LANES), LANES)
        for j in range(7):

            def step(g, accs, j=j):
                part = field[pl.ds(g * group, group + 6), :, lanes]
                grad = moved_cols(conv[pl.ds(g * group, group), :, lanes], 3 - j)
                return tuple(
                    acc
                    + jnp.sum(
                        (part[i : i + group] * grad).reshape(group * cols // 8, 8, LANES),
                        axis=0,
                    )
                    for i, acc in enumerate(accs)
                )

            zero = jnp.zeros((8, LANES), F32)
            accs = lax.fori_loop(0, rows // group, step, (zero,) * 7, unroll=True)
            for i in range(7):
                tap = i * 7 + j
                out[tap : tap + 1, lanes] = jnp.sum(accs[i], axis=0, keepdims=True)
        return 0

    lax.fori_loop(0, channels // LANES, across, 0)


def product_kernel(plan, wide_left, more, last, info, left, right, *refs):
    width = (left if wide_left else right).shape[-1] // 4
    size = width if wide_left else left.shape[-1]
    first_dims = (((0,), (0,)), ((), ()))
    odd = plan.odd(info)
    smalls, (theirs, mine) = refs[more:-2], refs[-2:]
    for block in range(4):
        at = pl.multiple_of((block + 2 * (1 - odd)) % 4 * width, LANES)
        span = pl.ds(at, width)
        total = lax.dot_general(
            left[:, span] if wide_left else left[...],
            right[...] if wide_left else right[:, span],
            first_dims,
            preferred_element_type=F32,
        )
        rows = slice(block % 2 * size, (block % 2 + 1) * size)
        out, at = (theirs, 0) if block < 2 else (mine, more - 1)
        if more and (more == 2 or block >= 2):
            total = total + refs[at][rows]
        out[rows] = total.astype(out.dtype)
    if last and smalls:
        rows = smalls[0].shape[0] // 2
        blank = jnp.zeros((mine.shape[0] - 2 * size - rows, mine.shape[1]), F32)

        def half(at):
            start = pl.multiple_of(at * rows, 8)
            return jnp.concatenate([tree([v[pl.ds(start, rows)] for v in smalls]), blank], axis=0)

        mine[2 * size :] = half(odd).astype(mine.dtype)
        theirs[2 * size :] = half(1 - odd).astype(mine.dtype)


def add_kernel(info, mine, theirs, out):
    out[...] = mine[...] + theirs[...].astype(F32)


def gather_kernel(info, taps, sums, units, out):
    channels = out.shape[1]
    out[0:56] = taps[...]
    out[49:54] = sums[0:5]
    wide = units.shape[1] // channels
    for k in range(wide):
        out[54 + k : 55 + k] = units[:, k * channels : (k + 1) * channels]
    out[54 + wide :] = jnp.zeros((out.shape[0] - 54 - wide, channels), F32)


def merge_kernel(plan, info, mine, theirs, *refs):
    outs, total = refs[:-1], refs[-1]
    share = outs[0].shape[0]
    total[...] = mine[...].astype(F32) + theirs[...].astype(F32)
    for k, out in enumerate(outs):
        at = pl.multiple_of((plan.shard(info) ^ k) * share, 16)
        out[...] = total[pl.ds(at, share)].astype(BF)


def tree(values):
    while len(values) > 1:
        pairs = [a + b for a, b in zip(values[::2], values[1::2])]
        values = pairs + values[len(pairs) * 2 :]
    return values[0]


def pack_kernel(plan, section, info, *refs):
    edges, out = refs[:-1], refs[-1]
    rows = out.shape[0] - 3 * len(edges)

    @pl.when(plan.section(info) == section)
    def _():
        for k, edge in enumerate(edges):
            out[rows + 3 * k : rows + 3 * (k + 1)] = edge[...]


def finish_kernel(factor, info, *refs):
    refs[-1][...] = (tree([r[...].astype(F32) for r in refs[:-1]]) * factor).astype(BF)


def place_down_kernel(plan, shards, info, *refs):
    pieces, out = refs[:-1], refs[-1]
    share = pieces[0].shape[0]
    for side in range(2):
        base = (plan.odd(info) ^ side) * shards
        for k in range(shards):
            at = pl.multiple_of((base + (plan.shard(info) ^ k)) * share, 16)
            out[pl.ds(at, share)] = pieces[side * shards + k][...]


def place_up_kernel(plan, shards, info, *refs):
    pieces = refs[: 2 * shards]
    up, kern, bias, gain, scale, units, full = refs[2 * shards :]
    share = pieces[0].shape[0]
    channels = up.shape[0]
    for side in range(2):
        half = plan.odd(info) ^ side
        for k in range(shards):
            at = pl.multiple_of((plan.shard(info) ^ k) * share, 16)
            full[half, pl.ds(at, share)] = pieces[side * shards + k][...]
    for half in range(2):
        for block in range(2):
            lane = (2 * half + block) * channels
            up[:, lane : lane + channels] = full[half, block * channels : (block + 1) * channels]
    small = jnp.concatenate(
        [full[half, 2 * channels : 2 * channels + 32] for half in range(2)], axis=0
    ).astype(F32)
    kern[...] = small[0:49].astype(BF)
    bias[...] = small[49:52].astype(BF)
    gain[...] = small[52:53].astype(BF)
    scale[...] = small[53:54].astype(BF)
    for k in range(units.shape[1] // channels):
        units[:, k * channels : (k + 1) * channels] = small[54 + k : 55 + k].astype(BF)


def body(
    images, cotangent, order, heights, kernel, biases, gain, scale, up_weight, up_bias, down_weight
):
    sections = lax.axis_size("section")
    shards = lax.axis_size("dp")
    strips = lax.axis_size("rows")
    section_at = lax.axis_index("section")
    row_at = lax.axis_index("rows")
    shard_at = lax.axis_index("dp")
    multi = strips > 2
    slots, rows, cols, channels = images.shape
    hidden = up_weight.shape[2]
    count = rows * cols
    odd = row_at % 2
    plan = Plan(slots, rows, multi)
    here = jnp.stack([section_at, row_at, shard_at]).astype(jnp.int32)
    info = jnp.concatenate([order[0], heights, here])
    packed = jnp.concatenate([kernel[0], biases[0], gain, scale])

    row_pairs = [(i, i ^ 1) for i in range(strips)]
    straight = [(i, i) for i in range(strips)]
    beyond = [(i, i + 1) for i in range(1, strips - 1, 2)]
    beyond += [(b, a) for a, b in beyond]

    def carry(value, pairs, source, target):
        return lax.ppermute(
            value,
            ("section", "rows"),
            [(source * strips + a, target * strips + b) for a, b in pairs],
        )

    def halos_of(near, far, section):
        return [lax.ppermute(near, "rows", row_pairs)] + (
            [carry(far, beyond, section, section)] if multi else []
        )

    last_rows, first_rows = images[:, rows - 3 :], images[:, :3]
    image_near = jnp.where(odd == 1, first_rows, last_rows)
    image_far = jnp.where(odd == 1, last_rows, first_rows) if multi else None
    image_halos = halos_of(image_near, image_far, 0)

    strip_shape = (rows, cols, channels)
    field_shape = (rows + 6, cols, channels)
    strip_out = (strip_shape, BF)
    package_out = ((rows + (6 if multi else 3), cols, channels), BF)
    edge_outs = [((3, cols, channels), BF)] * (2 if multi else 1)

    kept_outs = [
        (field_shape, BF),
        (strip_shape, F32),
        ((count, LANES), F32),
        ((count, channels), BF),
        ((count, hidden), BF),
        ((count, hidden), BF),
        ((count, channels), F32),
    ]
    chain_outs = [
        (strip_shape, F32),
        ((count, channels), BF),
        ((count, hidden), BF),
        ((8, channels), F32),
        ((1, hidden), F32),
    ]
    kept = [[] for _ in range(slots)]
    chained = [[] for _ in range(slots)]
    moved = [[images] + image_halos] * slots
    incoming = [cotangent] * slots
    partial = [[], []]
    token = jnp.zeros(*TOKEN)

    def forward(section, slot):
        nonlocal token
        sends = section < sections - 1
        cold = section == 0 and slot == 0
        operands = moved[slot] + [packed, up_bias, up_weight, down_weight]
        places = [0] * (section == 0) + [len(operands) - k for k in (1, 2, 3)] * cold
        for k in places:
            operands[k] = pltpu.with_memory_space_constraint(operands[k], pltpu.HBM)
        fetched = [(strip_shape, BF)] * (section == 0)
        fetched += [(v.shape, v.dtype) for v in (up_weight, down_weight, up_bias)] * cold
        token, results = call(
            functools.partial(forward_kernel, plan, section, slot, sends, cold),
            "forward",
            info,
            operands,
            ([package_out] + edge_outs) * sends + kept_outs,
            token,
            keeps=kept[slot],
            scratch=[(field_shape, F32)] + fetched,
            apart=places,
            flags=[pltpu.SemaphoreType.DMA((4,))] * (section == 0),
        )
        kept[slot] = results[len(results) - len(kept_outs) :]
        if sends:
            halos = halos_of(results[1], results[2] if multi else None, section)
            token, package = call(
                functools.partial(pack_kernel, plan, section),
                "pack",
                info,
                halos,
                [package_out],
                token,
                keeps=[results[0]],
            )
            moved[slot] = [carry(package[0], straight, section, section + 1)]

    def backward(section, slot):
        nonlocal token
        edges = section > 0
        _, z, rs, _, _, slope, branch = kept[slot]
        token, results = call(
            functools.partial(chain_kernel, plan, section, slot, section == sections - 1, edges),
            "chain",
            info,
            [incoming[slot], z, rs, slope, branch, packed, up_weight, down_weight],
            ([strip_out] * 2 + edge_outs) * edges + chain_outs,
            token,
            keeps=chained[slot],
            scratch=[((count, channels), F32)],
        )
        chained[slot] = results[len(results) - len(chain_outs) :]
        if edges:
            halos = halos_of(results[2], results[3] if multi else None, section)
            token, (spread,) = call(
                functools.partial(spread_kernel, plan, section, slot),
                "spread",
                info,
                [results[1]] + halos + [results[0], packed],
                [strip_out],
                token,
                scratch=[(field_shape, F32), (strip_shape, F32)],
            )
            incoming[slot] = carry(spread, straight, section, section - 1)

    for section in range(sections - 1):
        for slot in range(slots):
            forward(section, slot)
    for slot in range(slots):
        forward(sections - 1, slot)
        backward(sections - 1, slot)
    for section in range(sections - 2, 0, -1):
        for slot in range(slots):
            backward(section, slot)
    factor = 1.0 / math.sqrt(shards * slots * strips * rows * cols)
    heights_of = [hidden // 2 + pad for pad in (0, 64)]
    partial = [[], []]
    earlier = [[], []]
    smalls = []

    def swap(value):
        return lax.ppermute(value, "rows", row_pairs)

    def product(at, slot):
        nonlocal token
        last = slot == slots - 1
        left, right = [
            (kept[slot][4], chained[slot][1]),
            (kept[slot][3], chained[slot][2]),
        ][at]
        extra = smalls if last and at == 1 else []
        older = partial[at] if at == 1 else partial[at][1:]
        outputs = [((hidden // 2, channels), F32 if at == 1 else BF), ((hidden // 2, channels), F32)]
        if last:
            outputs = [((heights_of[at], channels), BF)] * 2
        token, (theirs, mine) = call(
            functools.partial(product_kernel, plan, at == 0, len(older), last),
            "product",
            info,
            [left, right] + older + extra,
            outputs,
            token,
        )
        partial[at] = [theirs, mine]

    def collect(at):
        nonlocal token
        theirs, mine = partial[at]
        earlier[at].append(theirs)
        if not multi:
            token, (mine,) = call(
                add_kernel,
                "total",
                info,
                [mine, swap(theirs)],
                [((hidden // 2, channels), F32)],
                token,
            )
        partial[at] = [theirs, mine]

    def small_terms(slot):
        nonlocal token
        conv, _, _, sums, units = chained[slot]
        token, (taps,) = call(
            taps_kernel,
            "taps",
            info,
            [kept[slot][0], conv],
            [((56, channels), F32)],
            token,
            scratch=[(field_shape, F32)],
        )
        token, (small,) = call(
            gather_kernel, "total", info, [taps, sums, units], [((64, channels), F32)], token
        )
        smalls.append(small)

    for slot in range(slots):
        backward(0, slot)
        product(0, slot)
        if slot < slots - 1:
            product(1, slot)
        small_terms(slot)
        if slot < slots - 1:
            collect(0)

    def peers(values):
        return [
            lax.ppermute(v, "dp", [(i, i ^ k) for i in range(shards)])
            for k, v in enumerate(values)
            if k
        ]

    def merged(at):
        nonlocal token
        theirs, mine = partial[at]
        share = heights_of[at] // shards
        token, pieces = call(
            functools.partial(merge_kernel, plan),
            "merge",
            info,
            [mine, swap(theirs)],
            [((share, channels), BF)] * shards,
            token,
            scratch=[((heights_of[at], channels), F32)],
        )
        return [pieces[0]] + peers(pieces)

    def finished(pieces):
        nonlocal token
        token, (own,) = call(
            functools.partial(finish_kernel, factor),
            "finish",
            info,
            pieces,
            [(pieces[0].shape, BF)],
            token,
        )
        half = [own] + peers([own] * shards)
        return half + [swap(v) for v in half]

    small_outs = [((49, channels), BF), ((3, channels), BF), ((1, channels), BF)]
    small_outs += [((1, channels), BF), ((1, hidden), BF)]
    if multi:
        product(1, slots - 1)
        sides = []
        for at, (theirs, mine) in enumerate(partial):
            for term in earlier[at]:
                theirs = theirs.at[: hidden // 2].add(term)
            pair = jnp.where(odd == 1, jnp.stack([theirs, mine]), jnp.stack([mine, theirs]))
            sides.append(lax.psum(pair.astype(F32), ("rows", "dp")) * factor)
        down_grad = sides[0].reshape(hidden, channels).astype(BF)
        up_grad = sides[1][:, : 2 * channels].reshape(4, channels, channels)
        up_grad = up_grad.transpose(1, 0, 2).reshape(channels, hidden).astype(BF)
        small = sides[1][:, 2 * channels : 2 * channels + 32].reshape(64, channels).astype(BF)
        kern_grad, bias_grad, gain_grad, scale_grad = (
            small[:49], small[49:52], small[52:53], small[53:54]
        )
        unit_grad = small[54 : 54 + hidden // channels].reshape(1, hidden)
    else:
        first = merged(0)
        product(1, slots - 1)
        second = merged(1)
        down_half = finished(first)
        up_half = finished(second)
        token, (down_grad,) = call(
            functools.partial(place_down_kernel, plan, shards),
            "place",
            info,
            down_half,
            [((hidden, channels), BF)],
            token,
        )
        token, results = call(
            functools.partial(place_up_kernel, plan, shards),
            "place",
            info,
            up_half,
            [((channels, hidden), BF)] + small_outs,
            token,
            scratch=[((2, heights_of[1], channels), BF)],
        )
        up_grad, kern_grad, bias_grad, gain_grad, scale_grad, unit_grad = results
    return (
        kern_grad[None],
        bias_grad[None],
        gain_grad,
        scale_grad,
        up_grad[None],
        unit_grad,
        down_grad[None],
    )


def solution(mesh):
    in_specs = (
        P("dp", "rows", None, None),
        P("dp", "rows", None, None),
        P("dp", None),
        P("dp"),
        P("section", None, None),
        P("section", None, None),
        P("section", None),
        P("section", None),
        P("section", None, None),
        P("section", None),
        P("section", None, None),
    )
    out_specs = (
        P("section", None, None),
        P("section", None, None),
        P("section", None),
        P("section", None),
        P("section", None, None),
        P("section", None),
        P("section", None, None),
    )
    return jax.shard_map(body, mesh=mesh, in_specs=in_specs, out_specs=out_specs, check_vma=False)
```

```python
import functools
import math

import jax
import jax.numpy as jnp
from jax import lax
from jax.experimental import pallas as pl
from jax.experimental.pallas import tpu as pltpu
from jax.sharding import PartitionSpec as P

EPS = 1e-06
ROOT_HALF = 0.7071067811865476
INV_ROOT_TAU = 0.3989422804014327
BF = jnp.bfloat16
F32 = jnp.float32
LANES = 128
CHUNK = 768
VMEM_LIMIT = 20 * 1024 * 1024

IN_VMEM = pl.BlockSpec(memory_space=pltpu.VMEM)
IN_SMEM = pl.BlockSpec(memory_space=pltpu.SMEM)
ANYWHERE = pl.BlockSpec(memory_space=pl.ANY)
IN_HBM = pl.BlockSpec(memory_space=pltpu.HBM)


TOKEN = ((8, LANES), F32)


def call(kernel, name, info, operands, outputs, after, keeps=(), scratch=(), apart=(), flags=()):
    base = 2 + len(operands)
    outputs = [TOKEN] + list(outputs)
    lead = len(outputs) - len(keeps)

    def run(info, *refs):
        kernel(info, *refs[: len(operands)], *refs[len(operands) + 1 + len(keeps) + 1 :])

    results = pl.pallas_call(
        run,
        out_shape=[jax.ShapeDtypeStruct(*o) for o in outputs],
        in_specs=[IN_SMEM]
        + [IN_HBM if k in apart else IN_VMEM for k in range(len(operands))]
        + [ANYWHERE]
        + [IN_VMEM] * len(keeps),
        out_specs=[IN_VMEM] * len(outputs),
        scratch_shapes=[pltpu.VMEM(*s) for s in scratch] + list(flags),
        input_output_aliases={base + i: lead + i for i in range(len(keeps))},
        cost_estimate=pl.CostEstimate(
            flops=0, transcendentals=0, bytes_accessed=int(COST[name] * 3.69e6)
        ),
        compiler_params=pltpu.CompilerParams(vmem_limit_bytes=VMEM_LIMIT),
        name=name,
    )(info, *operands, after, *keeps)
    return results[0], list(results[1:])


COST = {
    "forward": 5.0, "pack": 1, "chain": 3.0, "spread": 3, "product": 2, "merge": 1, "taps": 4,
    "total": 1, "finish": 1, "place": 2,
}


class Plan:
    def __init__(self, slots, rows, multi):
        self.slots, self.rows, self.multi = slots, rows, multi

    def section(self, info):
        return info[2 * self.slots]

    def image(self, info, slot):
        return info[slot]

    def limit(self, info, slot):
        height = info[self.slots + info[slot]]
        return height - info[2 * self.slots + 1] * self.rows

    def odd(self, info):
        return info[2 * self.slots + 1] % 2

    def shard(self, info):
        return info[2 * self.slots + 2]


class Packed:
    def __init__(self, ref):
        self.ref = ref

    def bias(self, at):
        return self.ref[49 + at : 50 + at]

    def gain(self):
        return self.ref[52:53]

    def scale(self):
        return self.ref[53:54]


def group_of(rows):
    return next(g for g in (8, 6, 4, 3, 2, 1) if rows % g == 0)


def masked_rows(value, first, limit):
    row = lax.broadcasted_iota(jnp.int32, value.shape, 0) + first
    return jnp.where(row < limit, value, 0.0)


def moved_cols(value, steps):
    if steps == 0:
        return value
    cols = value.shape[1]
    col = lax.broadcasted_iota(jnp.int32, value.shape, 1)
    inside = col < cols - steps if steps > 0 else col >= -steps
    return jnp.where(inside, pltpu.roll(value, (-steps) % cols, 1), 0.0)


def fill_field(field, middle, near, far, odd, limit):
    rows = middle.shape[0]
    field[3 : 3 + rows] = masked_rows(middle.astype(F32), 0, limit)
    near = near.astype(F32)
    far = jnp.zeros(near.shape, F32) if far is None else far.astype(F32)

    @pl.when(odd == 1)
    def _():
        field[0:3] = masked_rows(near, -3, limit)
        field[rows + 3 :] = masked_rows(far, rows, limit)

    @pl.when(odd == 0)
    def _():
        field[0:3] = masked_rows(far, -3, limit)
        field[rows + 3 :] = masked_rows(near, rows, limit)


def depthwise(field, kern, out, bias, flip):
    rows, cols, channels = out.shape
    group = group_of(rows)
    groups = rows // group

    def step(n, _):
        g = n % groups
        lanes = pl.ds(pl.multiple_of(n // groups * LANES, LANES), LANES)
        part = field[pl.ds(g * group, group + 6), :, lanes]
        total = jnp.zeros((group, cols, LANES), F32)
        for j in range(7):
            acc = jnp.zeros((group, cols, LANES), F32)
            for i in range(7):
                tap = 48 - (i * 7 + j) if flip else i * 7 + j
                acc = acc + kern[tap : tap + 1, lanes][None] * part[i : i + group]
            total = total + moved_cols(acc, j - 3)
        if bias is not None:
            total = total + kern[bias : bias + 1, lanes][None]
        out[pl.ds(g * group, group), :, lanes] = total
        return 0

    lax.fori_loop(0, groups * (channels // LANES), step, 0)


def pick_edge(odd, value, near, far):
    rows = value.shape[0]

    @pl.when(odd == 1)
    def _():
        near[...] = value[0:3]
        if far is not None:
            far[...] = value[rows - 3 :]

    @pl.when(odd == 0)
    def _():
        near[...] = value[rows - 3 :]
        if far is not None:
            far[...] = value[0:3]


def forward_kernel(plan, section, slot, sends, cold, info, *refs):
    refs = list(refs)
    if section == 0:
        source = [refs.pop(0), refs.pop(0), refs.pop(0) if plan.multi else None]
    else:
        package = refs.pop(0)
    packed = Packed(refs.pop(0))
    up_bias, up, down = refs.pop(0), refs.pop(0), refs.pop(0)
    far_up, far_down, far_bias = up, down, up_bias
    outgoing = refs.pop(0) if sends else None
    near = refs.pop(0) if sends else None
    far = refs.pop(0) if sends and plan.multi else None
    o_pad, o_z, o_rs, o_n, o_h, o_slope, o_branch, field = refs[:8]
    fetches = []
    if section == 0:
        image, flag = refs[8], refs[-1]
        one = pltpu.make_async_copy(source[0].at[plan.image(info, slot)], image, flag.at[0])
    if cold:
        up, down, up_bias = refs[9:12]
        fetches = [
            pltpu.make_async_copy(far_up, up, flag.at[1]),
            pltpu.make_async_copy(far_down, down, flag.at[2]),
            pltpu.make_async_copy(far_bias, up_bias, flag.at[3]),
        ]
    rows, cols, channels = o_z.shape
    count = rows * cols
    hidden = up.shape[2]
    limit = plan.limit(info, slot)
    odd = plan.odd(info)

    @pl.when(plan.section(info) == section)
    def _():
        if section == 0:
            one.start()
        for fetch in fetches:
            fetch.start()
        if section == 0:
            at = plan.image(info, slot)
            one.wait()
            parts = [image[...]] + [None if v is None else v[at] for v in source[1:]]
        else:
            far_rows = package[rows + 3 :] if plan.multi else None
            parts = [package[0:rows], package[rows : rows + 3], far_rows]
        fill_field(field, *parts, odd, limit)
        o_pad[...] = field[...].astype(BF)
        depthwise(field, packed.ref, o_z, 49, False)
        conv = o_z[...].reshape(count, channels)
        centred = conv - jnp.mean(conv, axis=-1, keepdims=True)
        inv_std = lax.rsqrt(jnp.mean(centred * centred, axis=-1, keepdims=True) + EPS)
        normed = centred * inv_std
        o_z[...] = normed.reshape(rows, cols, channels)
        o_rs[...] = jnp.broadcast_to(inv_std, (count, LANES))
        features = (normed * packed.gain() + packed.bias(1)).astype(BF)
        o_n[...] = features
        o_branch[...] = jnp.broadcast_to(packed.bias(2), (count, channels))
        for fetch in fetches:
            fetch.wait()

        def units(n, _):
            span = pl.ds(pl.multiple_of(n * CHUNK, CHUNK), CHUNK)
            pre = jnp.dot(o_n[...], up[0, :, span], preferred_element_type=F32) + up_bias[:, span]
            bell = 1.0 + lax.erf(pre * ROOT_HALF)
            act = (0.5 * pre * bell).astype(BF)
            o_h[:, span] = act
            o_slope[:, span] = (
                0.5 * bell + pre * jnp.exp(-0.5 * pre * pre) * INV_ROOT_TAU
            ).astype(BF)
            o_branch[...] += jnp.dot(act, down[0, span, :], preferred_element_type=F32)
            return 0

        lax.fori_loop(0, hidden // CHUNK, units, 0, unroll=True)
        branch = o_branch[...]
        if sends:
            value = field[3 : 3 + rows] + (packed.scale() * branch).reshape(rows, cols, channels)
            outgoing[0:rows] = masked_rows(value, 0, limit).astype(BF)
            pick_edge(odd, outgoing.at[0:rows], near, far)


def chain_kernel(plan, section, slot, top, edges, info, *refs):
    refs = list(refs)
    grad_out, z, rs, slope, branch = (refs.pop(0) for _ in range(5))
    packed = Packed(refs.pop(0))
    up, down = refs.pop(0), refs.pop(0)
    o_res = refs.pop(0) if edges else None
    o_low = refs.pop(0) if edges else None
    near = refs.pop(0) if edges else None
    far = refs.pop(0) if edges and plan.multi else None
    o_conv, o_go, o_gl, o_sums, o_up_bias, feat_ref = refs
    rows, cols, channels = o_conv.shape
    count = rows * cols
    hidden = up.shape[2]

    @pl.when(plan.section(info) == section)
    def _():
        grad = grad_out[slot] if top else grad_out[...]
        grad_res = masked_rows(grad.astype(F32), 0, plan.limit(info, slot))
        if edges:
            o_res[...] = grad_res.astype(BF)
        flat = grad_res.reshape(count, channels)
        scaled = packed.scale() * flat
        sum_scale = jnp.sum(branch[...] * flat, axis=0, keepdims=True)
        sum_out = jnp.sum(scaled, axis=0, keepdims=True)
        go = scaled.astype(BF)
        o_go[...] = go
        feat_ref[...] = jnp.zeros((count, channels), F32)
        last_dims = (((1,), (1,)), ((), ()))

        def units(n, _):
            span = pl.ds(pl.multiple_of(n * CHUNK, CHUNK), CHUNK)
            grad_hidden = lax.dot_general(
                o_go[...], down[0, span, :], last_dims, preferred_element_type=F32
            )
            grad_pre = grad_hidden * slope[:, span].astype(F32)
            o_up_bias[:, span] = jnp.sum(grad_pre, axis=0, keepdims=True)
            low = grad_pre.astype(BF)
            o_gl[:, span] = low
            feat_ref[...] += lax.dot_general(
                low, up[0, :, span], last_dims, preferred_element_type=F32
            )
            return 0

        lax.fori_loop(0, hidden // CHUNK, units, 0, unroll=True)
        feat = feat_ref[...]
        normed = z[...].reshape(count, channels)
        sum_gain = jnp.sum(feat * normed, axis=0, keepdims=True)
        sum_norm = jnp.sum(feat, axis=0, keepdims=True)
        grad_normed = feat * packed.gain()
        inner = (
            grad_normed
            - jnp.mean(grad_normed, axis=-1, keepdims=True)
            - normed * jnp.mean(grad_normed * normed, axis=-1, keepdims=True)
        )
        for at in range(0, channels, LANES):
            lanes = slice(at, at + LANES)
            o_conv[:, :, lanes] = (rs[...] * inner[:, lanes]).reshape(rows, cols, LANES)
        grad_conv = o_conv[...]
        sum_conv = jnp.sum(grad_conv.reshape(count, channels), axis=0, keepdims=True)
        if edges:
            o_low[...] = grad_conv.astype(BF)
            pick_edge(plan.odd(info), o_low, near, far)
        blank = jnp.zeros((3, channels), F32)
        o_sums[...] = jnp.concatenate(
            [sum_conv, sum_norm, sum_out, sum_gain, sum_scale, blank], axis=0
        )


def spread_kernel(plan, section, slot, info, *refs):
    refs = list(refs)
    low, near = refs.pop(0), refs.pop(0)
    far = refs.pop(0) if plan.multi else None
    res, packed, out, field, total = refs
    rows = low.shape[0]

    @pl.when(plan.section(info) == section)
    def _():
        fill_field(
            field,
            low[...],
            near[...],
            None if far is None else far[...],
            plan.odd(info),
            rows + 3,
        )
        depthwise(field, packed, total, None, True)
        value = total[...] + res[...].astype(F32)
        out[...] = masked_rows(value, 0, plan.limit(info, slot)).astype(BF)


def taps_kernel(info, pad, conv, out, field):
    rows, cols, channels = conv.shape
    group = group_of(rows)
    out[49:, :] = jnp.zeros((out.shape[0] - 49, channels), F32)
    field[...] = pad[...].astype(F32)

    def across(n, _):
        lanes = pl.ds(pl.multiple_of(n * LANES, LANES), LANES)
        for j in range(7):

            def step(g, accs, j=j):
                part = field[pl.ds(g * group, group + 6), :, lanes]
                grad = moved_cols(conv[pl.ds(g * group, group), :, lanes], 3 - j)
                return tuple(
                    acc
                    + jnp.sum(
                        (part[i : i + group] * grad).reshape(group * cols // 8, 8, LANES),
                        axis=0,
                    )
                    for i, acc in enumerate(accs)
                )

            zero = jnp.zeros((8, LANES), F32)
            accs = lax.fori_loop(0, rows // group, step, (zero,) * 7, unroll=True)
            for i in range(7):
                tap = i * 7 + j
                out[tap : tap + 1, lanes] = jnp.sum(accs[i], axis=0, keepdims=True)
        return 0

    lax.fori_loop(0, channels // LANES, across, 0)


def product_kernel(plan, wide_left, more, last, info, left, right, *refs):
    width = (left if wide_left else right).shape[-1] // 4
    size = width if wide_left else left.shape[-1]
    first_dims = (((0,), (0,)), ((), ()))
    odd = plan.odd(info)
    smalls, (theirs, mine) = refs[more:-2], refs[-2:]
    for block in range(4):
        at = pl.multiple_of((block + 2 * (1 - odd)) % 4 * width, LANES)
        span = pl.ds(at, width)
        total = lax.dot_general(
            left[:, span] if wide_left else left[...],
            right[...] if wide_left else right[:, span],
            first_dims,
            preferred_element_type=F32,
        )
        rows = slice(block % 2 * size, (block % 2 + 1) * size)
        out, at = (theirs, 0) if block < 2 else (mine, more - 1)
        if more and (more == 2 or block >= 2):
            total = total + refs[at][rows]
        out[rows] = total.astype(out.dtype)
    if last and smalls:
        rows = smalls[0].shape[0] // 2
        blank = jnp.zeros((mine.shape[0] - 2 * size - rows, mine.shape[1]), F32)

        def half(at):
            start = pl.multiple_of(at * rows, 8)
            return jnp.concatenate([tree([v[pl.ds(start, rows)] for v in smalls]), blank], axis=0)

        mine[2 * size :] = half(odd).astype(mine.dtype)
        theirs[2 * size :] = half(1 - odd).astype(mine.dtype)


def add_kernel(info, mine, theirs, out):
    out[...] = mine[...] + theirs[...].astype(F32)


def gather_kernel(info, taps, sums, units, out):
    channels = out.shape[1]
    out[0:56] = taps[...]
    out[49:54] = sums[0:5]
    wide = units.shape[1] // channels
    for k in range(wide):
        out[54 + k : 55 + k] = units[:, k * channels : (k + 1) * channels]
    out[54 + wide :] = jnp.zeros((out.shape[0] - 54 - wide, channels), F32)


def merge_kernel(plan, info, mine, theirs, *refs):
    outs, total = refs[:-1], refs[-1]
    share = outs[0].shape[0]
    total[...] = mine[...].astype(F32) + theirs[...].astype(F32)
    for k, out in enumerate(outs):
        at = pl.multiple_of((plan.shard(info) ^ k) * share, 16)
        out[...] = total[pl.ds(at, share)].astype(BF)


def tree(values):
    while len(values) > 1:
        pairs = [a + b for a, b in zip(values[::2], values[1::2])]
        values = pairs + values[len(pairs) * 2 :]
    return values[0]


def place_kernel(plan, shards, info, *refs):
    each = 2 * shards
    outs = refs[2 * each :]
    place_down_kernel(plan, shards, info, *refs[:each], outs[0])
    place_up_kernel(plan, shards, info, *refs[each : 2 * each], *outs[1:])


def pack_kernel(plan, section, info, *refs):
    edges, out = refs[:-1], refs[-1]
    rows = out.shape[0] - 3 * len(edges)

    @pl.when(plan.section(info) == section)
    def _():
        for k, edge in enumerate(edges):
            out[rows + 3 * k : rows + 3 * (k + 1)] = edge[...]


def finish_kernel(factor, info, *refs):
    refs[-1][...] = (tree([r[...].astype(F32) for r in refs[:-1]]) * factor).astype(BF)


def place_down_kernel(plan, shards, info, *refs):
    pieces, out = refs[:-1], refs[-1]
    share = pieces[0].shape[0]
    for side in range(2):
        base = (plan.odd(info) ^ side) * shards
        for k in range(shards):
            at = pl.multiple_of((base + (plan.shard(info) ^ k)) * share, 16)
            out[pl.ds(at, share)] = pieces[side * shards + k][...]


def place_up_kernel(plan, shards, info, *refs):
    pieces = refs[: 2 * shards]
    up, kern, bias, gain, scale, units, full = refs[2 * shards :]
    share = pieces[0].shape[0]
    channels = up.shape[0]
    for side in range(2):
        half = plan.odd(info) ^ side
        for k in range(shards):
            at = pl.multiple_of((plan.shard(info) ^ k) * share, 16)
            full[half, pl.ds(at, share)] = pieces[side * shards + k][...]
    for half in range(2):
        for block in range(2):
            lane = (2 * half + block) * channels
            up[:, lane : lane + channels] = full[half, block * channels : (block + 1) * channels]
    small = jnp.concatenate(
        [full[half, 2 * channels : 2 * channels + 32] for half in range(2)], axis=0
    ).astype(F32)
    kern[...] = small[0:49].astype(BF)
    bias[...] = small[49:52].astype(BF)
    gain[...] = small[52:53].astype(BF)
    scale[...] = small[53:54].astype(BF)
    for k in range(units.shape[1] // channels):
        units[:, k * channels : (k + 1) * channels] = small[54 + k : 55 + k].astype(BF)


def body(
    images, cotangent, order, heights, kernel, biases, gain, scale, up_weight, up_bias, down_weight
):
    sections = lax.axis_size("section")
    shards = lax.axis_size("dp")
    strips = lax.axis_size("rows")
    section_at = lax.axis_index("section")
    row_at = lax.axis_index("rows")
    shard_at = lax.axis_index("dp")
    multi = strips > 2
    slots, rows, cols, channels = images.shape
    hidden = up_weight.shape[2]
    count = rows * cols
    odd = row_at % 2
    plan = Plan(slots, rows, multi)
    here = jnp.stack([section_at, row_at, shard_at]).astype(jnp.int32)
    info = jnp.concatenate([order[0], heights, here])
    packed = jnp.concatenate([kernel[0], biases[0], gain, scale])

    row_pairs = [(i, i ^ 1) for i in range(strips)]
    straight = [(i, i) for i in range(strips)]
    beyond = [(i, i + 1) for i in range(1, strips - 1, 2)]
    beyond += [(b, a) for a, b in beyond]

    def carry(value, pairs, source, target):
        return lax.ppermute(
            value,
            ("section", "rows"),
            [(source * strips + a, target * strips + b) for a, b in pairs],
        )

    def halos_of(near, far, section):
        return [lax.ppermute(near, "rows", row_pairs)] + (
            [carry(far, beyond, section, section)] if multi else []
        )

    last_rows, first_rows = images[:, rows - 3 :], images[:, :3]
    image_near = jnp.where(odd == 1, first_rows, last_rows)
    image_far = jnp.where(odd == 1, last_rows, first_rows) if multi else None
    image_halos = halos_of(image_near, image_far, 0)

    strip_shape = (rows, cols, channels)
    field_shape = (rows + 6, cols, channels)
    strip_out = (strip_shape, BF)
    package_out = ((rows + (6 if multi else 3), cols, channels), BF)
    edge_outs = [((3, cols, channels), BF)] * (2 if multi else 1)

    kept_outs = [
        (field_shape, BF),
        (strip_shape, F32),
        ((count, LANES), F32),
        ((count, channels), BF),
        ((count, hidden), BF),
        ((count, hidden), BF),
        ((count, channels), F32),
    ]
    chain_outs = [
        (strip_shape, F32),
        ((count, channels), BF),
        ((count, hidden), BF),
        ((8, channels), F32),
        ((1, hidden), F32),
    ]
    kept = [[] for _ in range(slots)]
    chained = [[] for _ in range(slots)]
    moved = [[images] + image_halos] * slots
    incoming = [cotangent] * slots
    partial = [[], []]
    token = jnp.zeros(*TOKEN)

    def forward(section, slot):
        nonlocal token
        sends = section < sections - 1
        cold = section == 0 and slot == 0
        operands = moved[slot] + [packed, up_bias, up_weight, down_weight]
        places = [0] * (section == 0) + [len(operands) - k for k in (1, 2, 3)] * cold
        for k in places:
            operands[k] = pltpu.with_memory_space_constraint(operands[k], pltpu.HBM)
        fetched = [(strip_shape, BF)] * (section == 0)
        fetched += [(v.shape, v.dtype) for v in (up_weight, down_weight, up_bias)] * cold
        token, results = call(
            functools.partial(forward_kernel, plan, section, slot, sends, cold),
            "forward",
            info,
            operands,
            ([package_out] + edge_outs) * sends + kept_outs,
            token,
            keeps=kept[slot],
            scratch=[(field_shape, F32)] + fetched,
            apart=places,
            flags=[pltpu.SemaphoreType.DMA((4,))] * (section == 0),
        )
        kept[slot] = results[len(results) - len(kept_outs) :]
        if sends:
            halos = halos_of(results[1], results[2] if multi else None, section)
            token, package = call(
                functools.partial(pack_kernel, plan, section),
                "pack",
                info,
                halos,
                [package_out],
                token,
                keeps=[results[0]],
            )
            moved[slot] = [carry(package[0], straight, section, section + 1)]

    def backward(section, slot):
        nonlocal token
        edges = section > 0
        _, z, rs, _, _, slope, branch = kept[slot]
        token, results = call(
            functools.partial(chain_kernel, plan, section, slot, section == sections - 1, edges),
            "chain",
            info,
            [incoming[slot], z, rs, slope, branch, packed, up_weight, down_weight],
            ([strip_out] * 2 + edge_outs) * edges + chain_outs,
            token,
            keeps=chained[slot],
            scratch=[((count, channels), F32)],
        )
        chained[slot] = results[len(results) - len(chain_outs) :]
        if edges:
            halos = halos_of(results[2], results[3] if multi else None, section)
            token, (spread,) = call(
                functools.partial(spread_kernel, plan, section, slot),
                "spread",
                info,
                [results[1]] + halos + [results[0], packed],
                [strip_out],
                token,
                scratch=[(field_shape, F32), (strip_shape, F32)],
            )
            incoming[slot] = carry(spread, straight, section, section - 1)

    for section in range(sections - 1):
        for slot in range(slots):
            forward(section, slot)
    for slot in range(slots):
        forward(sections - 1, slot)
        backward(sections - 1, slot)
    for section in range(sections - 2, 0, -1):
        for slot in range(slots):
            backward(section, slot)
    factor = 1.0 / math.sqrt(shards * slots * strips * rows * cols)
    heights_of = [hidden // 2 + pad for pad in (0, 64)]
    partial = [[], []]
    earlier = [[], []]
    smalls = []

    def swap(value):
        return lax.ppermute(value, "rows", row_pairs)

    def product(at, slot):
        nonlocal token
        last = slot == slots - 1
        left, right = [
            (kept[slot][4], chained[slot][1]),
            (kept[slot][3], chained[slot][2]),
        ][at]
        extra = smalls if last and at == 1 else []
        older = partial[at] if at == 1 else partial[at][1:]
        outputs = [((hidden // 2, channels), F32 if at == 1 else BF), ((hidden // 2, channels), F32)]
        if last:
            outputs = [((heights_of[at], channels), BF)] * 2
        token, (theirs, mine) = call(
            functools.partial(product_kernel, plan, at == 0, len(older), last),
            "product",
            info,
            [left, right] + older + extra,
            outputs,
            token,
        )
        partial[at] = [theirs, mine]

    def collect(at):
        nonlocal token
        theirs, mine = partial[at]
        earlier[at].append(theirs)
        if not multi:
            token, (mine,) = call(
                add_kernel,
                "total",
                info,
                [mine, swap(theirs)],
                [((hidden // 2, channels), F32)],
                token,
            )
        partial[at] = [theirs, mine]

    def small_terms(slot):
        nonlocal token
        conv, _, _, sums, units = chained[slot]
        token, (taps,) = call(
            taps_kernel,
            "taps",
            info,
            [kept[slot][0], conv],
            [((56, channels), F32)],
            token,
            scratch=[(field_shape, F32)],
        )
        token, (small,) = call(
            gather_kernel, "total", info, [taps, sums, units], [((64, channels), F32)], token
        )
        smalls.append(small)

    for slot in range(slots):
        backward(0, slot)
        product(0, slot)
        if slot < slots - 1:
            product(1, slot)
        small_terms(slot)
        if slot < slots - 1:
            collect(0)

    def peers(values):
        return [
            lax.ppermute(v, "dp", [(i, i ^ k) for i in range(shards)])
            for k, v in enumerate(values)
            if k
        ]

    def merged(at):
        nonlocal token
        theirs, mine = partial[at]
        share = heights_of[at] // shards
        token, pieces = call(
            functools.partial(merge_kernel, plan),
            "merge",
            info,
            [mine, swap(theirs)],
            [((share, channels), BF)] * shards,
            token,
            scratch=[((heights_of[at], channels), F32)],
        )
        return [pieces[0]] + peers(pieces)

    def finished(pieces):
        nonlocal token
        token, (own,) = call(
            functools.partial(finish_kernel, factor),
            "finish",
            info,
            pieces,
            [(pieces[0].shape, BF)],
            token,
        )
        half = [own] + peers([own] * shards)
        return half + [swap(v) for v in half]

    small_outs = [((49, channels), BF), ((3, channels), BF), ((1, channels), BF)]
    small_outs += [((1, channels), BF), ((1, hidden), BF)]
    if multi:
        product(1, slots - 1)
        sides = []
        for at, (theirs, mine) in enumerate(partial):
            for term in earlier[at]:
                theirs = theirs.at[: hidden // 2].add(term)
            pair = jnp.where(odd == 1, jnp.stack([theirs, mine]), jnp.stack([mine, theirs]))
            sides.append(lax.psum(pair.astype(F32), ("rows", "dp")) * factor)
        down_grad = sides[0].reshape(hidden, channels).astype(BF)
        up_grad = sides[1][:, : 2 * channels].reshape(4, channels, channels)
        up_grad = up_grad.transpose(1, 0, 2).reshape(channels, hidden).astype(BF)
        small = sides[1][:, 2 * channels : 2 * channels + 32].reshape(64, channels).astype(BF)
        kern_grad, bias_grad, gain_grad, scale_grad = (
            small[:49], small[49:52], small[52:53], small[53:54]
        )
        unit_grad = small[54 : 54 + hidden // channels].reshape(1, hidden)
    else:
        first = merged(0)
        product(1, slots - 1)
        second = merged(1)
        down_half = finished(first)
        up_half = finished(second)
        token, results = call(
            functools.partial(place_kernel, plan, shards),
            "place",
            info,
            down_half + up_half,
            [((hidden, channels), BF), ((channels, hidden), BF)] + small_outs,
            token,
            scratch=[((2, heights_of[1], channels), BF)],
        )
        down_grad, up_grad, kern_grad, bias_grad, gain_grad, scale_grad, unit_grad = results
    return (
        kern_grad[None],
        bias_grad[None],
        gain_grad,
        scale_grad,
        up_grad[None],
        unit_grad,
        down_grad[None],
    )


def solution(mesh):
    in_specs = (
        P("dp", "rows", None, None),
        P("dp", "rows", None, None),
        P("dp", None),
        P("dp"),
        P("section", None, None),
        P("section", None, None),
        P("section", None),
        P("section", None),
        P("section", None, None),
        P("section", None),
        P("section", None, None),
    )
    out_specs = (
        P("section", None, None),
        P("section", None, None),
        P("section", None),
        P("section", None),
        P("section", None, None),
        P("section", None),
        P("section", None, None),
    )
    return jax.shard_map(body, mesh=mesh, in_specs=in_specs, out_specs=out_specs, check_vma=False)
```

```python
import functools
import math

import jax
import jax.numpy as jnp
from jax import lax
from jax.experimental import pallas as pl
from jax.experimental.pallas import tpu as pltpu
from jax.sharding import PartitionSpec as P

EPS = 1e-06
ROOT_HALF = 0.7071067811865476
INV_ROOT_TAU = 0.3989422804014327
BF = jnp.bfloat16
F32 = jnp.float32
LANES = 128
CHUNK = 768
VMEM_LIMIT = 20 * 1024 * 1024

IN_VMEM = pl.BlockSpec(memory_space=pltpu.VMEM)
IN_SMEM = pl.BlockSpec(memory_space=pltpu.SMEM)
ANYWHERE = pl.BlockSpec(memory_space=pl.ANY)
IN_HBM = pl.BlockSpec(memory_space=pltpu.HBM)


TOKEN = ((8, LANES), F32)


def call(kernel, name, info, operands, outputs, after, keeps=(), scratch=(), apart=(), flags=()):
    base = 2 + len(operands)
    outputs = [TOKEN] + list(outputs)
    lead = len(outputs) - len(keeps)

    def run(info, *refs):
        kernel(info, *refs[: len(operands)], *refs[len(operands) + 1 + len(keeps) + 1 :])

    results = pl.pallas_call(
        run,
        out_shape=[jax.ShapeDtypeStruct(*o) for o in outputs],
        in_specs=[IN_SMEM]
        + [IN_HBM if k in apart else IN_VMEM for k in range(len(operands))]
        + [ANYWHERE]
        + [IN_VMEM] * len(keeps),
        out_specs=[IN_VMEM] * len(outputs),
        scratch_shapes=[pltpu.VMEM(*s) for s in scratch] + list(flags),
        input_output_aliases={base + i: lead + i for i in range(len(keeps))},
        cost_estimate=pl.CostEstimate(
            flops=0, transcendentals=0, bytes_accessed=int(COST[name] * 3.69e6)
        ),
        compiler_params=pltpu.CompilerParams(vmem_limit_bytes=VMEM_LIMIT),
        name=name,
    )(info, *operands, after, *keeps)
    return results[0], list(results[1:])


COST = {
    "forward": 5.0, "pack": 1, "chain": 3.0, "spread": 3, "product": 2, "merge": 1, "taps": 4,
    "total": 1, "finish": 1, "place": 2,
}


class Plan:
    def __init__(self, slots, rows, multi):
        self.slots, self.rows, self.multi = slots, rows, multi

    def section(self, info):
        return info[2 * self.slots]

    def image(self, info, slot):
        return info[slot]

    def limit(self, info, slot):
        height = info[self.slots + info[slot]]
        return height - info[2 * self.slots + 1] * self.rows

    def odd(self, info):
        return info[2 * self.slots + 1] % 2

    def shard(self, info):
        return info[2 * self.slots + 2]


class Packed:
    def __init__(self, ref):
        self.ref = ref

    def bias(self, at):
        return self.ref[49 + at : 50 + at]

    def gain(self):
        return self.ref[52:53]

    def scale(self):
        return self.ref[53:54]


def group_of(rows):
    return next(g for g in (8, 6, 4, 3, 2, 1) if rows % g == 0)


def masked_rows(value, first, limit):
    row = lax.broadcasted_iota(jnp.int32, value.shape, 0) + first
    return jnp.where(row < limit, value, 0.0)


def moved_cols(value, steps):
    if steps == 0:
        return value
    cols = value.shape[1]
    col = lax.broadcasted_iota(jnp.int32, value.shape, 1)
    inside = col < cols - steps if steps > 0 else col >= -steps
    return jnp.where(inside, pltpu.roll(value, (-steps) % cols, 1), 0.0)


def fill_field(field, middle, near, far, odd, limit):
    rows = middle.shape[0]
    field[3 : 3 + rows] = masked_rows(middle.astype(F32), 0, limit)
    near = near.astype(F32)
    far = jnp.zeros(near.shape, F32) if far is None else far.astype(F32)

    @pl.when(odd == 1)
    def _():
        field[0:3] = masked_rows(near, -3, limit)
        field[rows + 3 :] = masked_rows(far, rows, limit)

    @pl.when(odd == 0)
    def _():
        field[0:3] = masked_rows(far, -3, limit)
        field[rows + 3 :] = masked_rows(near, rows, limit)


def depthwise(field, kern, out, bias, flip):
    rows, cols, channels = out.shape
    group = group_of(rows)
    groups = rows // group

    def step(n, _):
        g = n % groups
        lanes = pl.ds(pl.multiple_of(n // groups * LANES, LANES), LANES)
        part = field[pl.ds(g * group, group + 6), :, lanes]
        total = jnp.zeros((group, cols, LANES), F32)
        for j in range(7):
            acc = jnp.zeros((group, cols, LANES), F32)
            for i in range(7):
                tap = 48 - (i * 7 + j) if flip else i * 7 + j
                acc = acc + kern[tap : tap + 1, lanes][None] * part[i : i + group]
            total = total + moved_cols(acc, j - 3)
        if bias is not None:
            total = total + kern[bias : bias + 1, lanes][None]
        out[pl.ds(g * group, group), :, lanes] = total
        return 0

    lax.fori_loop(0, groups * (channels // LANES), step, 0)


def pick_edge(odd, value, near, far):
    rows = value.shape[0]

    @pl.when(odd == 1)
    def _():
        near[...] = value[0:3]
        if far is not None:
            far[...] = value[rows - 3 :]

    @pl.when(odd == 0)
    def _():
        near[...] = value[rows - 3 :]
        if far is not None:
            far[...] = value[0:3]


def forward_kernel(plan, section, slot, sends, cold, info, *refs):
    refs = list(refs)
    if section == 0:
        source = [refs.pop(0), refs.pop(0), refs.pop(0) if plan.multi else None]
    else:
        package = refs.pop(0)
    packed = Packed(refs.pop(0))
    up_bias, up, down = refs.pop(0), refs.pop(0), refs.pop(0)
    far_up, far_down, far_bias = up, down, up_bias
    outgoing = refs.pop(0) if sends else None
    near = refs.pop(0) if sends else None
    far = refs.pop(0) if sends and plan.multi else None
    o_pad, o_z, o_rs, o_n, o_h, o_slope, o_branch, field = refs[:8]
    fetches = []
    if section == 0:
        image, flag = refs[8], refs[-1]
        one = pltpu.make_async_copy(source[0].at[plan.image(info, slot)], image, flag.at[0])
    if cold:
        up, down, up_bias = refs[9:12]
        fetches = [
            pltpu.make_async_copy(far_up, up, flag.at[1]),
            pltpu.make_async_copy(far_down, down, flag.at[2]),
            pltpu.make_async_copy(far_bias, up_bias, flag.at[3]),
        ]
    rows, cols, channels = o_z.shape
    count = rows * cols
    hidden = up.shape[2]
    limit = plan.limit(info, slot)
    odd = plan.odd(info)

    @pl.when(plan.section(info) == section)
    def _():
        if section == 0:
            one.start()
        for fetch in fetches:
            fetch.start()
        if section == 0:
            at = plan.image(info, slot)
            one.wait()
            parts = [image[...]] + [None if v is None else v[at] for v in source[1:]]
        else:
            far_rows = package[rows + 3 :] if plan.multi else None
            parts = [package[0:rows], package[rows : rows + 3], far_rows]
        fill_field(field, *parts, odd, limit)
        o_pad[...] = field[...].astype(BF)
        depthwise(field, packed.ref, o_z, 49, False)
        conv = o_z[...].reshape(count, channels)
        centred = conv - jnp.mean(conv, axis=-1, keepdims=True)
        inv_std = lax.rsqrt(jnp.mean(centred * centred, axis=-1, keepdims=True) + EPS)
        normed = centred * inv_std
        o_z[...] = normed.reshape(rows, cols, channels)
        o_rs[...] = jnp.broadcast_to(inv_std, (count, LANES))
        features = (normed * packed.gain() + packed.bias(1)).astype(BF)
        o_n[...] = features
        o_branch[...] = jnp.broadcast_to(packed.bias(2), (count, channels))
        for fetch in fetches:
            fetch.wait()

        def units(n, _):
            span = pl.ds(pl.multiple_of(n * CHUNK, CHUNK), CHUNK)
            pre = jnp.dot(o_n[...], up[0, :, span], preferred_element_type=F32) + up_bias[:, span]
            bell = 1.0 + lax.erf(pre * ROOT_HALF)
            act = (0.5 * pre * bell).astype(BF)
            o_h[:, span] = act
            o_slope[:, span] = (
                0.5 * bell + pre * jnp.exp(-0.5 * pre * pre) * INV_ROOT_TAU
            ).astype(BF)
            o_branch[...] += jnp.dot(act, down[0, span, :], preferred_element_type=F32)
            return 0

        lax.fori_loop(0, hidden // CHUNK, units, 0, unroll=True)
        branch = o_branch[...]
        if sends:
            value = field[3 : 3 + rows] + (packed.scale() * branch).reshape(rows, cols, channels)
            outgoing[0:rows] = masked_rows(value, 0, limit).astype(BF)
            pick_edge(odd, outgoing.at[0:rows], near, far)


def chain_kernel(plan, section, slot, top, edges, info, *refs):
    refs = list(refs)
    grad_out, z, rs, slope, branch = (refs.pop(0) for _ in range(5))
    packed = Packed(refs.pop(0))
    up, down = refs.pop(0), refs.pop(0)
    o_res = refs.pop(0) if edges else None
    o_low = refs.pop(0) if edges else None
    near = refs.pop(0) if edges else None
    far = refs.pop(0) if edges and plan.multi else None
    o_conv, o_go, o_gl, o_sums, o_up_bias, feat_ref = refs
    rows, cols, channels = o_conv.shape
    count = rows * cols
    hidden = up.shape[2]

    @pl.when(plan.section(info) == section)
    def _():
        grad = grad_out[slot] if top else grad_out[...]
        grad_res = masked_rows(grad.astype(F32), 0, plan.limit(info, slot))
        if edges:
            o_res[...] = grad_res.astype(BF)
        flat = grad_res.reshape(count, channels)
        scaled = packed.scale() * flat
        sum_scale = jnp.sum(branch[...] * flat, axis=0, keepdims=True)
        sum_out = jnp.sum(scaled, axis=0, keepdims=True)
        go = scaled.astype(BF)
        o_go[...] = go
        feat_ref[...] = jnp.zeros((count, channels), F32)
        last_dims = (((1,), (1,)), ((), ()))

        def units(n, _):
            span = pl.ds(pl.multiple_of(n * CHUNK, CHUNK), CHUNK)
            grad_hidden = lax.dot_general(
                o_go[...], down[0, span, :], last_dims, preferred_element_type=F32
            )
            grad_pre = grad_hidden * slope[:, span].astype(F32)
            o_up_bias[:, span] = jnp.sum(grad_pre, axis=0, keepdims=True)
            low = grad_pre.astype(BF)
            o_gl[:, span] = low
            feat_ref[...] += lax.dot_general(
                low, up[0, :, span], last_dims, preferred_element_type=F32
            )
            return 0

        lax.fori_loop(0, hidden // CHUNK, units, 0, unroll=True)
        feat = feat_ref[...]
        normed = z[...].reshape(count, channels)
        sum_gain = jnp.sum(feat * normed, axis=0, keepdims=True)
        sum_norm = jnp.sum(feat, axis=0, keepdims=True)
        grad_normed = feat * packed.gain()
        inner = (
            grad_normed
            - jnp.mean(grad_normed, axis=-1, keepdims=True)
            - normed * jnp.mean(grad_normed * normed, axis=-1, keepdims=True)
        )
        for at in range(0, channels, LANES):
            lanes = slice(at, at + LANES)
            o_conv[:, :, lanes] = (rs[...] * inner[:, lanes]).reshape(rows, cols, LANES)
        grad_conv = o_conv[...]
        sum_conv = jnp.sum(grad_conv.reshape(count, channels), axis=0, keepdims=True)
        if edges:
            o_low[...] = grad_conv.astype(BF)
            pick_edge(plan.odd(info), o_low, near, far)
        blank = jnp.zeros((3, channels), F32)
        o_sums[...] = jnp.concatenate(
            [sum_conv, sum_norm, sum_out, sum_gain, sum_scale, blank], axis=0
        )


def spread_kernel(plan, section, slot, info, *refs):
    refs = list(refs)
    low, near = refs.pop(0), refs.pop(0)
    far = refs.pop(0) if plan.multi else None
    res, packed, out, field, total = refs
    rows = low.shape[0]

    @pl.when(plan.section(info) == section)
    def _():
        fill_field(
            field,
            low[...],
            near[...],
            None if far is None else far[...],
            plan.odd(info),
            rows + 3,
        )
        depthwise(field, packed, total, None, True)
        value = total[...] + res[...].astype(F32)
        out[...] = masked_rows(value, 0, plan.limit(info, slot)).astype(BF)


def taps_kernel(info, pad, conv, sums, units, out, field):
    rows, cols, channels = conv.shape
    group = group_of(rows)
    wide = units.shape[1] // channels
    out[49:54] = sums[0:5]
    for k in range(wide):
        out[54 + k : 55 + k] = units[:, k * channels : (k + 1) * channels]
    out[54 + wide :] = jnp.zeros((out.shape[0] - 54 - wide, channels), F32)
    field[...] = pad[...].astype(F32)

    def across(n, _):
        lanes = pl.ds(pl.multiple_of(n * LANES, LANES), LANES)
        for j in range(7):

            def step(g, accs, j=j):
                part = field[pl.ds(g * group, group + 6), :, lanes]
                grad = moved_cols(conv[pl.ds(g * group, group), :, lanes], 3 - j)
                return tuple(
                    acc
                    + jnp.sum(
                        (part[i : i + group] * grad).reshape(group * cols // 8, 8, LANES),
                        axis=0,
                    )
                    for i, acc in enumerate(accs)
                )

            zero = jnp.zeros((8, LANES), F32)
            accs = lax.fori_loop(0, rows // group, step, (zero,) * 7, unroll=True)
            for i in range(7):
                tap = i * 7 + j
                out[tap : tap + 1, lanes] = jnp.sum(accs[i], axis=0, keepdims=True)
        return 0

    lax.fori_loop(0, channels // LANES, across, 0)


def product_kernel(plan, wide_left, more, last, info, left, right, *refs):
    width = (left if wide_left else right).shape[-1] // 4
    size = width if wide_left else left.shape[-1]
    first_dims = (((0,), (0,)), ((), ()))
    odd = plan.odd(info)
    smalls, (theirs, mine) = refs[more:-2], refs[-2:]
    for block in range(4):
        at = pl.multiple_of((block + 2 * (1 - odd)) % 4 * width, LANES)
        span = pl.ds(at, width)
        total = lax.dot_general(
            left[:, span] if wide_left else left[...],
            right[...] if wide_left else right[:, span],
            first_dims,
            preferred_element_type=F32,
        )
        rows = slice(block % 2 * size, (block % 2 + 1) * size)
        out, at = (theirs, 0) if block < 2 else (mine, more - 1)
        if more and (more == 2 or block >= 2):
            total = total + refs[at][rows]
        out[rows] = total.astype(out.dtype)
    if last and smalls:
        rows = smalls[0].shape[0] // 2
        blank = jnp.zeros((mine.shape[0] - 2 * size - rows, mine.shape[1]), F32)

        def half(at):
            start = pl.multiple_of(at * rows, 8)
            return jnp.concatenate([tree([v[pl.ds(start, rows)] for v in smalls]), blank], axis=0)

        mine[2 * size :] = half(odd).astype(mine.dtype)
        theirs[2 * size :] = half(1 - odd).astype(mine.dtype)


def add_kernel(info, mine, theirs, out):
    out[...] = mine[...] + theirs[...].astype(F32)


def merge_kernel(plan, info, mine, theirs, *refs):
    outs, total = refs[:-1], refs[-1]
    share = outs[0].shape[0]
    total[...] = mine[...].astype(F32) + theirs[...].astype(F32)
    for k, out in enumerate(outs):
        at = pl.multiple_of((plan.shard(info) ^ k) * share, 16)
        out[...] = total[pl.ds(at, share)].astype(BF)


def tree(values):
    while len(values) > 1:
        pairs = [a + b for a, b in zip(values[::2], values[1::2])]
        values = pairs + values[len(pairs) * 2 :]
    return values[0]


def place_kernel(plan, shards, info, *refs):
    each = 2 * shards
    outs = refs[2 * each :]
    place_down_kernel(plan, shards, info, *refs[:each], outs[0])
    place_up_kernel(plan, shards, info, *refs[each : 2 * each], *outs[1:])


def pack_kernel(plan, section, info, *refs):
    edges, out = refs[:-1], refs[-1]
    rows = out.shape[0] - 3 * len(edges)

    @pl.when(plan.section(info) == section)
    def _():
        for k, edge in enumerate(edges):
            out[rows + 3 * k : rows + 3 * (k + 1)] = edge[...]


def finish_kernel(factor, info, *refs):
    refs[-1][...] = (tree([r[...].astype(F32) for r in refs[:-1]]) * factor).astype(BF)


def place_down_kernel(plan, shards, info, *refs):
    pieces, out = refs[:-1], refs[-1]
    share = pieces[0].shape[0]
    for side in range(2):
        base = (plan.odd(info) ^ side) * shards
        for k in range(shards):
            at = pl.multiple_of((base + (plan.shard(info) ^ k)) * share, 16)
            out[pl.ds(at, share)] = pieces[side * shards + k][...]


def place_up_kernel(plan, shards, info, *refs):
    pieces = refs[: 2 * shards]
    up, kern, bias, gain, scale, units, full = refs[2 * shards :]
    share = pieces[0].shape[0]
    channels = up.shape[0]
    for side in range(2):
        half = plan.odd(info) ^ side
        for k in range(shards):
            at = pl.multiple_of((plan.shard(info) ^ k) * share, 16)
            full[half, pl.ds(at, share)] = pieces[side * shards + k][...]
    for half in range(2):
        for block in range(2):
            lane = (2 * half + block) * channels
            up[:, lane : lane + channels] = full[half, block * channels : (block + 1) * channels]
    small = jnp.concatenate(
        [full[half, 2 * channels : 2 * channels + 32] for half in range(2)], axis=0
    ).astype(F32)
    kern[...] = small[0:49].astype(BF)
    bias[...] = small[49:52].astype(BF)
    gain[...] = small[52:53].astype(BF)
    scale[...] = small[53:54].astype(BF)
    for k in range(units.shape[1] // channels):
        units[:, k * channels : (k + 1) * channels] = small[54 + k : 55 + k].astype(BF)


def body(
    images, cotangent, order, heights, kernel, biases, gain, scale, up_weight, up_bias, down_weight
):
    sections = lax.axis_size("section")
    shards = lax.axis_size("dp")
    strips = lax.axis_size("rows")
    section_at = lax.axis_index("section")
    row_at = lax.axis_index("rows")
    shard_at = lax.axis_index("dp")
    multi = strips > 2
    slots, rows, cols, channels = images.shape
    hidden = up_weight.shape[2]
    count = rows * cols
    odd = row_at % 2
    plan = Plan(slots, rows, multi)
    here = jnp.stack([section_at, row_at, shard_at]).astype(jnp.int32)
    info = jnp.concatenate([order[0], heights, here])
    packed = jnp.concatenate([kernel[0], biases[0], gain, scale])

    row_pairs = [(i, i ^ 1) for i in range(strips)]
    straight = [(i, i) for i in range(strips)]
    beyond = [(i, i + 1) for i in range(1, strips - 1, 2)]
    beyond += [(b, a) for a, b in beyond]

    def carry(value, pairs, source, target):
        return lax.ppermute(
            value,
            ("section", "rows"),
            [(source * strips + a, target * strips + b) for a, b in pairs],
        )

    def halos_of(near, far, section):
        return [lax.ppermute(near, "rows", row_pairs)] + (
            [carry(far, beyond, section, section)] if multi else []
        )

    last_rows, first_rows = images[:, rows - 3 :], images[:, :3]
    image_near = jnp.where(odd == 1, first_rows, last_rows)
    image_far = jnp.where(odd == 1, last_rows, first_rows) if multi else None
    image_halos = halos_of(image_near, image_far, 0)

    strip_shape = (rows, cols, channels)
    field_shape = (rows + 6, cols, channels)
    strip_out = (strip_shape, BF)
    package_out = ((rows + (6 if multi else 3), cols, channels), BF)
    edge_outs = [((3, cols, channels), BF)] * (2 if multi else 1)

    kept_outs = [
        (field_shape, BF),
        (strip_shape, F32),
        ((count, LANES), F32),
        ((count, channels), BF),
        ((count, hidden), BF),
        ((count, hidden), BF),
        ((count, channels), F32),
    ]
    chain_outs = [
        (strip_shape, F32),
        ((count, channels), BF),
        ((count, hidden), BF),
        ((8, channels), F32),
        ((1, hidden), F32),
    ]
    kept = [[] for _ in range(slots)]
    chained = [[] for _ in range(slots)]
    moved = [[images] + image_halos] * slots
    incoming = [cotangent] * slots
    partial = [[], []]
    token = jnp.zeros(*TOKEN)

    def forward(section, slot):
        nonlocal token
        sends = section < sections - 1
        cold = section == 0 and slot == 0
        operands = moved[slot] + [packed, up_bias, up_weight, down_weight]
        places = [0] * (section == 0) + [len(operands) - k for k in (1, 2, 3)] * cold
        for k in places:
            operands[k] = pltpu.with_memory_space_constraint(operands[k], pltpu.HBM)
        fetched = [(strip_shape, BF)] * (section == 0)
        fetched += [(v.shape, v.dtype) for v in (up_weight, down_weight, up_bias)] * cold
        token, results = call(
            functools.partial(forward_kernel, plan, section, slot, sends, cold),
            "forward",
            info,
            operands,
            ([package_out] + edge_outs) * sends + kept_outs,
            token,
            keeps=kept[slot],
            scratch=[(field_shape, F32)] + fetched,
            apart=places,
            flags=[pltpu.SemaphoreType.DMA((4,))] * (section == 0),
        )
        kept[slot] = results[len(results) - len(kept_outs) :]
        if sends:
            halos = halos_of(results[1], results[2] if multi else None, section)
            token, package = call(
                functools.partial(pack_kernel, plan, section),
                "pack",
                info,
                halos,
                [package_out],
                token,
                keeps=[results[0]],
            )
            moved[slot] = [carry(package[0], straight, section, section + 1)]

    def backward(section, slot):
        nonlocal token
        edges = section > 0
        _, z, rs, _, _, slope, branch = kept[slot]
        token, results = call(
            functools.partial(chain_kernel, plan, section, slot, section == sections - 1, edges),
            "chain",
            info,
            [incoming[slot], z, rs, slope, branch, packed, up_weight, down_weight],
            ([strip_out] * 2 + edge_outs) * edges + chain_outs,
            token,
            keeps=chained[slot],
            scratch=[((count, channels), F32)],
        )
        chained[slot] = results[len(results) - len(chain_outs) :]
        if edges:
            halos = halos_of(results[2], results[3] if multi else None, section)
            token, (spread,) = call(
                functools.partial(spread_kernel, plan, section, slot),
                "spread",
                info,
                [results[1]] + halos + [results[0], packed],
                [strip_out],
                token,
                scratch=[(field_shape, F32), (strip_shape, F32)],
            )
            incoming[slot] = carry(spread, straight, section, section - 1)

    for section in range(sections - 1):
        for slot in range(slots):
            forward(section, slot)
    for slot in range(slots):
        forward(sections - 1, slot)
        backward(sections - 1, slot)
    for section in range(sections - 2, 0, -1):
        for slot in range(slots):
            backward(section, slot)
    factor = 1.0 / math.sqrt(shards * slots * strips * rows * cols)
    heights_of = [hidden // 2 + pad for pad in (0, 64)]
    partial = [[], []]
    earlier = [[], []]
    smalls = []

    def swap(value):
        return lax.ppermute(value, "rows", row_pairs)

    def product(at, slot):
        nonlocal token
        last = slot == slots - 1
        left, right = [
            (kept[slot][4], chained[slot][1]),
            (kept[slot][3], chained[slot][2]),
        ][at]
        extra = smalls if last and at == 1 else []
        older = partial[at] if at == 1 else partial[at][1:]
        outputs = [((hidden // 2, channels), F32 if at == 1 else BF), ((hidden // 2, channels), F32)]
        if last:
            outputs = [((heights_of[at], channels), BF)] * 2
        token, (theirs, mine) = call(
            functools.partial(product_kernel, plan, at == 0, len(older), last),
            "product",
            info,
            [left, right] + older + extra,
            outputs,
            token,
        )
        partial[at] = [theirs, mine]

    def collect(at):
        nonlocal token
        theirs, mine = partial[at]
        earlier[at].append(theirs)
        if not multi:
            token, (mine,) = call(
                add_kernel,
                "total",
                info,
                [mine, swap(theirs)],
                [((hidden // 2, channels), F32)],
                token,
            )
        partial[at] = [theirs, mine]

    def small_terms(slot):
        nonlocal token
        conv, _, _, sums, units = chained[slot]
        token, (small,) = call(
            taps_kernel,
            "taps",
            info,
            [kept[slot][0], conv, sums, units],
            [((64, channels), F32)],
            token,
            scratch=[(field_shape, F32)],
        )
        smalls.append(small)

    for slot in range(slots):
        backward(0, slot)
        product(0, slot)
        if slot < slots - 1:
            product(1, slot)
        small_terms(slot)
        if slot < slots - 1:
            collect(0)

    def peers(values):
        return [
            lax.ppermute(v, "dp", [(i, i ^ k) for i in range(shards)])
            for k, v in enumerate(values)
            if k
        ]

    def merged(at):
        nonlocal token
        theirs, mine = partial[at]
        share = heights_of[at] // shards
        token, pieces = call(
            functools.partial(merge_kernel, plan),
            "merge",
            info,
            [mine, swap(theirs)],
            [((share, channels), BF)] * shards,
            token,
            scratch=[((heights_of[at], channels), F32)],
        )
        return [pieces[0]] + peers(pieces)

    def finished(pieces):
        nonlocal token
        token, (own,) = call(
            functools.partial(finish_kernel, factor),
            "finish",
            info,
            pieces,
            [(pieces[0].shape, BF)],
            token,
        )
        half = [own] + peers([own] * shards)
        return half + [swap(v) for v in half]

    small_outs = [((49, channels), BF), ((3, channels), BF), ((1, channels), BF)]
    small_outs += [((1, channels), BF), ((1, hidden), BF)]
    if multi:
        product(1, slots - 1)
        sides = []
        for at, (theirs, mine) in enumerate(partial):
            for term in earlier[at]:
                theirs = theirs.at[: hidden // 2].add(term)
            pair = jnp.where(odd == 1, jnp.stack([theirs, mine]), jnp.stack([mine, theirs]))
            sides.append(lax.psum(pair.astype(F32), ("rows", "dp")) * factor)
        down_grad = sides[0].reshape(hidden, channels).astype(BF)
        up_grad = sides[1][:, : 2 * channels].reshape(4, channels, channels)
        up_grad = up_grad.transpose(1, 0, 2).reshape(channels, hidden).astype(BF)
        small = sides[1][:, 2 * channels : 2 * channels + 32].reshape(64, channels).astype(BF)
        kern_grad, bias_grad, gain_grad, scale_grad = (
            small[:49], small[49:52], small[52:53], small[53:54]
        )
        unit_grad = small[54 : 54 + hidden // channels].reshape(1, hidden)
    else:
        first = merged(0)
        product(1, slots - 1)
        second = merged(1)
        down_half = finished(first)
        up_half = finished(second)
        token, results = call(
            functools.partial(place_kernel, plan, shards),
            "place",
            info,
            down_half + up_half,
            [((hidden, channels), BF), ((channels, hidden), BF)] + small_outs,
            token,
            scratch=[((2, heights_of[1], channels), BF)],
        )
        down_grad, up_grad, kern_grad, bias_grad, gain_grad, scale_grad, unit_grad = results
    return (
        kern_grad[None],
        bias_grad[None],
        gain_grad,
        scale_grad,
        up_grad[None],
        unit_grad,
        down_grad[None],
    )


def solution(mesh):
    in_specs = (
        P("dp", "rows", None, None),
        P("dp", "rows", None, None),
        P("dp", None),
        P("dp"),
        P("section", None, None),
        P("section", None, None),
        P("section", None),
        P("section", None),
        P("section", None, None),
        P("section", None),
        P("section", None, None),
    )
    out_specs = (
        P("section", None, None),
        P("section", None, None),
        P("section", None),
        P("section", None),
        P("section", None, None),
        P("section", None),
        P("section", None, None),
    )
    return jax.shard_map(body, mesh=mesh, in_specs=in_specs, out_specs=out_specs, check_vma=False)
```
